128 devices in a mesh: req: 16 (over y_lo, z, core), tp: 8 (over y_hi, x).
Axes of the slice: x: 4, y: 4 (y_hi: 2, y_lo: 2; y = y_hi * 2 + y_lo), z: 4, core: 2. Of those that a mesh axis runs over, the one named last changes fastest.
Arguments:
- tokens: bfloat16 [2048, 2048], P('req')
- attn_gain: float32 [2048], replicated, may hold values from 0.25 to 1.75
- query_gain: float32 [128], replicated, may hold values from 0.8 to 2
- key_gain: float32 [128], replicated, may hold values from 0.8 to 2
- moe_gain: float32 [2048], replicated, may hold values from 0.25 to 1.75
- query_weight: float32 [2048, 2048], P('req', 'tp'), may hold values from -0.125 to 0.125
- key_weight: float32 [2048, 2048], P('req', 'tp'), may hold values from -0.125 to 0.125
- value_weight: float32 [2048, 2048], P('req', 'tp'), may hold values from -0.125 to 0.125
- out_weight: float32 [2048, 2048], P('tp', 'req'), may hold values from -0.125 to 0.125
- gate_weight: float32 [64, 2048, 1024], P(None, ('req', 'tp')), may hold values from -0.125 to 0.125
- up_weight: float32 [64, 2048, 1024], P(None, ('req', 'tp')), may hold values from -0.125 to 0.125
- down_weight: bfloat16 [128, 512, 2048], P(('req', 'tp')), may hold values from -0.1875 to 0.1875
- router_weight: bfloat16 [2048, 64], replicated, may hold values from -0.125 to 0.125
- page_store: bfloat16 [128, 128, 2, 2048], P('req', None, None, 'tp'), may hold values from -3 to 3
- prompt_lengths: int32 [32], replicated, may hold values from 32 to 96, as said below
- continues: int32 [32], replicated, may hold values from 0 to 1, as said below
- page_owner: int32 [16, 16], replicated, may hold values from 0 to 15, as said below
- page_slot: int32 [16, 16], replicated, may hold values from 0 to 7
- routes: int32 [2048, 8], P(('req', 'tp')), may hold values from 0 to 63, as said below
Outputs:
- server_qkv: bfloat16 [2048, 6144], P(None, 'tp')
- server_out: bfloat16 [2048, 2048], P('tp')
- server_gate_up: bfloat16 [128, 2048, 1024], P(('req', 'tp'))
- hidden: bfloat16 [2048, 2048], P(('req', 'tp'))
- new_cache: bfloat16 [2048, 2, 2048], P('req', None, 'tp')
The draws below stay inside these ranges and needn't reach their ends.
Inputs may be any that keep to these rules, and one draw needn't show every extreme that they name: `prompt_lengths`: entries 2g and 2g + 1 are the two prompt lengths of group g and sum to 128. Exactly one of the two prompts of each group continues an earlier request. `page_owner`: no page of group g lies on g itself; at most 2 of a group's 16 pages lie on one owner, and every group has exactly 2 pages on some owner. `routes`: each row names 8 different experts. In each aligned block of 16 rows (the rows of one device) no expert is named by more than 3 rows, and one expert, the same in every block, is named by exactly 3 rows in each block.
All inputs are finite; a program needn't handle non-finite values.
Results may differ from the reference program's by a relative error of at most 0.0057.
Values may be sent and summed in bfloat16 or wider, within the bound.
A program may use at most 128 MiB of HBM per device.

```python
import math
import jax
import jax.numpy as jnp
from jax import lax

D = 2048
H = 16
HD = 128
FF = 1024
TOPK = 8
TOK_GROUP = 128
PAGE = 128
CTXP = 16
PAGES_DEV = 8
EXPERTS = 64
SHARD = 16
MOST = 3
CAP = 2
CTX = 2048
MINLEN = 32
REQUESTS = 32
TOKENS = 2048
N_REQ = 16
N_TP = 8


def draw_tokens(key, part):
    key_rows, key_cols, key_base = jax.random.split(key, 3)
    row_scale = jnp.exp(jax.random.uniform(key_rows, (TOKENS, 1), jnp.float32, math.log(0.5), math.log(2.0)))
    col_scale = jnp.exp(jax.random.uniform(key_cols, (1, D), jnp.float32, math.log(0.35), math.log(3.5)))
    base = jnp.clip(jax.random.normal(key_base, (TOKENS, D), jnp.float32), -4.0, 4.0)
    return (base * row_scale * col_scale).astype(jnp.bfloat16)


def draw_prompt_lengths(key, part):
    groups = REQUESTS // 2
    key_first, key_forced = jax.random.split(jax.random.fold_in(key, 3))
    first_len = jax.random.randint(key_first, (groups,), MINLEN, TOK_GROUP - MINLEN + 1)
    forced = jax.random.randint(key_forced, (), 0, groups)
    first_len = jnp.where(jnp.arange(groups) == forced, TOK_GROUP - MINLEN, first_len)
    return jnp.stack([first_len, TOK_GROUP - first_len], axis=1).reshape(REQUESTS).astype(jnp.int32)


def draw_continues(key, part):
    groups = REQUESTS // 2
    chosen = jax.random.randint(jax.random.fold_in(key, 5), (groups,), 0, 2)
    return jnp.stack([1 - chosen, chosen], axis=1).reshape(REQUESTS).astype(jnp.int32)


def draw_page_owner(key, part):
    groups = REQUESTS // 2
    others = groups - 1
    group_keys = jax.random.split(jax.random.fold_in(key, 9), groups)

    def one_group(group_key, group_id):
        key_order, key_rest, key_shuffle = jax.random.split(group_key, 3)
        order = jax.random.permutation(key_order, others)
        pooled = jnp.repeat(order, CAP)
        remaining = CAP + jax.random.permutation(key_rest, others * CAP - CAP)
        chosen = jnp.concatenate([jnp.arange(CAP), remaining[:CTXP - CAP]])
        picked = pooled[chosen]
        picked = picked[jax.random.permutation(key_shuffle, CTXP)]
        return (group_id + 1 + picked) % groups
    return jax.vmap(one_group)(group_keys, jnp.arange(groups)).astype(jnp.int32)


def draw_routes(key, part):
    blocks = TOKENS // SHARD
    total = EXPERTS * MOST
    dropped = total - SHARD * TOPK
    starred = jax.random.randint(jax.random.fold_in(key, 7), (), 0, EXPERTS)
    copies = jnp.repeat(jnp.arange(EXPERTS, dtype=jnp.int32), MOST)

    def one_block(block_key):
        key_order, key_rows = jax.random.split(block_key)
        order = jax.random.permutation(key_order, total).astype(jnp.int32)
        scores = jnp.where(copies == starred, total + jnp.arange(total, dtype=jnp.int32), order)
        ranked = jnp.argsort(jnp.argsort(scores))
        keeping = ranked >= dropped
        places = jnp.where(keeping, jnp.cumsum(keeping.astype(jnp.int32)) - 1, SHARD * TOPK)
        listing = jnp.zeros((SHARD * TOPK,), jnp.int32).at[places].set(copies, mode='drop')
        row_order = jax.random.permutation(key_rows, SHARD)
        entries = jnp.arange(SHARD * TOPK)
        return jnp.zeros((SHARD, TOPK), jnp.int32).at[row_order[entries % SHARD], entries // SHARD].set(listing)
    block_keys = jax.random.split(jax.random.fold_in(key, 11), blocks)
    return jax.vmap(one_block)(block_keys).reshape(TOKENS, TOPK).astype(jnp.int32)


def with_ends(values, key, least, high):
    longest = values.shape.index(max(values.shape))
    spots = []
    for shift in (0, 1):
        where = [jax.random.randint(jax.random.fold_in(key, axis), (), 0, length) for axis, length in enumerate(values.shape)]
        where[longest] = (where[longest] + shift) % values.shape[longest]
        spots.append(tuple(where))
    return values.at[spots[0]].set(least).at[spots[1]].set(high)


def level_of(own_key, dims, cuts, low, largest):
    level, own = 1.0, jax.random.fold_in(own_key, 6)
    for axis_at, shards_of in cuts:
        heights = jnp.exp(jax.random.uniform(jax.random.fold_in(own, axis_at), (shards_of,), jnp.float32, low / len(cuts), largest / len(cuts)))
        level = level * jnp.repeat(heights, dims[axis_at] // shards_of).reshape([-1 if axis == axis_at else 1 for axis in range(len(dims))])
    return level


def normal_values(key, dims, scale, bound, pieces=(), kind=jnp.bfloat16):
    drawn = scale * jax.random.normal(key, dims, jnp.float32)
    if pieces:
        drawn = drawn * level_of(key, dims, pieces, -0.22, 0.18)
    return jnp.clip(drawn, -bound, bound).astype(kind)


def setup_inputs(seed: int = 0) -> dict:
    seeds = jax.random.split(jax.random.key(seed), 20)
    return {
        "tokens": draw_tokens(jax.random.fold_in(seeds[19], 71), 0),
        "attn_gain": jnp.clip(1.0 + 0.15 * jax.random.normal(seeds[1], (D,), jnp.float32), 0.25, 1.75),
        "query_gain": jnp.clip(jnp.exp(jax.random.uniform(seeds[2], (HD,), jnp.float32, math.log(0.8), math.log(2.0))), 0.8, 2.0),
        "key_gain": jnp.clip(jnp.exp(jax.random.uniform(seeds[3], (HD,), jnp.float32, math.log(0.8), math.log(2.0))), 0.8, 2.0),
        "moe_gain": jnp.clip(1.0 + 0.15 * jax.random.normal(seeds[4], (D,), jnp.float32), 0.25, 1.75),
        "query_weight": normal_values(seeds[5], (D, H * HD), D ** -0.5, 0.125, ((0, 16), (1, 8)), jnp.float32),
        "key_weight": normal_values(seeds[6], (D, H * HD), D ** -0.5, 0.125, ((0, 16), (1, 8)), jnp.float32),
        "value_weight": normal_values(seeds[7], (D, H * HD), D ** -0.5, 0.125, ((0, 16), (1, 8)), jnp.float32),
        "out_weight": normal_values(seeds[8], (H * HD, D), (H * HD) ** -0.5, 0.125, ((0, 8), (1, 16)), jnp.float32),
        "gate_weight": normal_values(seeds[9], (EXPERTS, D, FF), D ** -0.5, 0.125, ((1, 128),), jnp.float32),
        "up_weight": normal_values(seeds[10], (EXPERTS, D, FF), D ** -0.5, 0.125, ((1, 128),), jnp.float32),
        "down_weight": normal_values(seeds[11], (2 * EXPERTS, FF // 2, D), FF ** -0.5, 0.1875, ((0, 128),)),
        "router_weight": normal_values(seeds[12], (D, EXPERTS), D ** -0.5, 0.125),
        "page_store": normal_values(seeds[13], (N_REQ * PAGES_DEV, PAGE, 2, H * HD), 1.0, 3.0, ((0, 16), (3, 8))),
        "prompt_lengths": draw_prompt_lengths(jax.random.fold_in(seeds[19], 71), 0),
        "continues": draw_continues(jax.random.fold_in(seeds[19], 71), 0),
        "page_owner": draw_page_owner(jax.random.fold_in(seeds[19], 71), 0),
        "page_slot": with_ends(jax.random.randint(seeds[17], (N_REQ, CTXP), 0, PAGES_DEV), jax.random.fold_in(seeds[17], 1), 0, PAGES_DEV - 1).astype(jnp.int32),
        "routes": draw_routes(jax.random.fold_in(seeds[19], 71), 0),
    }


norm_eps = 1e-06
rope_base = 50000.0

def rms_scale(values, gain_vec):
    return values * lax.rsqrt(lax.optimization_barrier(jnp.mean(values * values, axis=-1, keepdims=True)) + norm_eps) * gain_vec

def rotate_half(values, cosine, sine_part):
    half_width = values.shape[-1] // 2
    first_half = values[..., :half_width]
    second_half = values[..., half_width:]
    return jnp.concatenate([first_half * cosine - second_half * sine_part, second_half * cosine + first_half * sine_part], axis=-1)

def reference(tokens, attn_gain, query_gain, key_gain, moe_gain, query_weight, key_weight, value_weight, out_weight, gate_weight, up_weight, down_weight, router_weight, page_store, prompt_lengths, continues, page_owner, page_slot, routes):
    lane_width = H * HD // N_TP

    def lane_blocks(weights):
        return weights.astype(jnp.bfloat16).reshape(D, N_TP, 1, lane_width)
    server_qkv = jnp.concatenate([lane_blocks(query_weight), lane_blocks(key_weight), lane_blocks(value_weight)], axis=2).reshape(D, 3 * H * HD)
    server_out = out_weight.astype(jnp.bfloat16)

    def split_halves(weights):
        return weights.astype(jnp.bfloat16).reshape(EXPERTS, D, 2, FF // 2).transpose(0, 2, 1, 3)
    server_gate_up = jnp.concatenate([split_halves(gate_weight), split_halves(up_weight)], axis=3).reshape(2 * EXPERTS, D, FF)
    query_bf = query_weight.astype(jnp.bfloat16)
    key_bf = key_weight.astype(jnp.bfloat16)
    value_bf = value_weight.astype(jnp.bfloat16)
    grouped = tokens.reshape(N_REQ, TOK_GROUP, D)
    inverse = jnp.power(jnp.float32(rope_base), -(jnp.arange(HD // 2, dtype=jnp.float32) * 2.0 / HD))
    score_scale = 1.0 / math.sqrt(HD)

    def attend(group_id):
        rows_f32 = lax.dynamic_index_in_dim(grouped, group_id, 0, keepdims=False).astype(jnp.float32)
        normed = rms_scale(rows_f32, attn_gain).astype(jnp.bfloat16)
        query_raw = jnp.dot(normed, query_bf, preferred_element_type=jnp.float32).reshape(TOK_GROUP, H, HD)
        key_raw = jnp.dot(normed, key_bf, preferred_element_type=jnp.float32).reshape(TOK_GROUP, H, HD)
        value_raw = jnp.dot(normed, value_bf, preferred_element_type=jnp.float32)
        first_length = lax.dynamic_index_in_dim(prompt_lengths, 2 * group_id, 0, keepdims=False)
        carry_flags = lax.dynamic_slice_in_dim(continues, 2 * group_id, 2)
        row_ids = jnp.arange(TOK_GROUP, dtype=jnp.int32)
        second = (row_ids >= first_length).astype(jnp.int32)
        within = row_ids - second * first_length
        carried = jnp.where(second == 1, carry_flags[1], carry_flags[0])
        position = (within + CTX * carried).astype(jnp.float32)
        angles = position[:, None, None] * inverse[None, None, :]
        cosine = jnp.cos(angles)
        sine_part = jnp.sin(angles)
        query_rows = rotate_half(rms_scale(query_raw, query_gain), cosine, sine_part).astype(jnp.bfloat16)
        keys_new = rotate_half(rms_scale(key_raw, key_gain), cosine, sine_part).astype(jnp.bfloat16)
        values_new = value_raw.astype(jnp.bfloat16)
        page_index = lax.dynamic_index_in_dim(page_owner, group_id, 0, keepdims=False) * PAGES_DEV + lax.dynamic_index_in_dim(page_slot, group_id, 0, keepdims=False)
        context = jnp.take(page_store, page_index, axis=0).reshape(CTX, 2, H, HD)
        near_scores = jnp.einsum('ihc,jhc->hij', query_rows.astype(jnp.float32), keys_new.astype(jnp.float32)) * score_scale
        far_scores = jnp.einsum('ihc,jhc->hij', query_rows.astype(jnp.float32), context[:, 0].astype(jnp.float32)) * score_scale
        same_request = second[:, None] == second[None, :]
        near_weights = jnp.where(same_request[None], jnp.exp(near_scores), jnp.float32(0.0))
        far_weights = jnp.where((carried == 1)[None, :, None], jnp.exp(far_scores), jnp.float32(0.0))
        totals = lax.optimization_barrier(jnp.sum(near_weights, axis=2, keepdims=True)) + lax.optimization_barrier(jnp.sum(far_weights, axis=2, keepdims=True))
        near_probs = (near_weights / totals).astype(jnp.bfloat16)
        far_probs = (far_weights / totals).astype(jnp.bfloat16)
        attended = jnp.einsum('hij,jhc->ihc', near_probs.astype(jnp.float32), values_new.reshape(TOK_GROUP, H, HD).astype(jnp.float32))
        attended = attended + jnp.einsum('hij,jhc->ihc', far_probs.astype(jnp.float32), context[:, 1].astype(jnp.float32))
        attended = attended.astype(jnp.bfloat16).reshape(TOK_GROUP, H * HD)
        residual = rows_f32 + jnp.dot(attended, server_out, preferred_element_type=jnp.float32)
        cache_rows = jnp.stack([keys_new.reshape(TOK_GROUP, H * HD), values_new], axis=1)
        return (residual, cache_rows)
    residual, cache_rows = lax.map(attend, jnp.arange(N_REQ, dtype=jnp.int32))
    residual = residual.reshape(TOKENS, D)
    new_cache = cache_rows.reshape(TOKENS, 2, H * HD)
    moe_in = rms_scale(residual, moe_gain).astype(jnp.bfloat16)
    logits = jnp.dot(moe_in, router_weight, preferred_element_type=jnp.float32)
    exps = jnp.exp(logits)
    routed_total = lax.optimization_barrier(jnp.sum(jnp.take_along_axis(exps, routes, axis=1), axis=1, keepdims=True))
    gates = exps / routed_total
    blocks = TOKENS // SHARD
    flat_routes = routes.reshape(blocks, SHARD * TOPK)
    onehot = (flat_routes[:, :, None] == jnp.arange(EXPERTS, dtype=jnp.int32)[None, None, :]).astype(jnp.int32)
    entry_rank = lax.optimization_barrier(jnp.sum((jnp.cumsum(onehot, axis=1) - onehot) * onehot, axis=2))
    entry_slot = flat_routes * MOST + entry_rank
    token_ids = jnp.arange(blocks, dtype=jnp.int32)[:, None] * SHARD + jnp.arange(SHARD * TOPK, dtype=jnp.int32)[None, :] // TOPK
    block_ids = jnp.broadcast_to(jnp.arange(blocks, dtype=jnp.int32)[:, None], entry_slot.shape)
    token_of = jnp.full((blocks, EXPERTS * MOST), -1, dtype=jnp.int32).at[block_ids, entry_slot].set(token_ids)

    def expert_step(total, expert_id):
        picked = lax.dynamic_slice_in_dim(token_of, expert_id * MOST, MOST, axis=1).reshape(-1)
        live = picked >= 0
        safe_ids = jnp.where(live, picked, 0)
        rows_in = jnp.where(live[:, None], jnp.take(moe_in, safe_ids, axis=0), jnp.zeros((), jnp.bfloat16))
        joined = jnp.zeros((rows_in.shape[0], D), jnp.float32)
        for half_id in range(2):
            block = lax.dynamic_index_in_dim(server_gate_up, 2 * expert_id + half_id, 0, keepdims=False)
            both = jnp.dot(rows_in, block, preferred_element_type=jnp.float32)
            act = (jax.nn.silu(both[:, :FF // 2]) * both[:, FF // 2:]).astype(jnp.bfloat16)
            down_block = lax.dynamic_index_in_dim(down_weight, 2 * expert_id + half_id, 0, keepdims=False)
            part = jnp.dot(act, down_block, preferred_element_type=jnp.float32).astype(jnp.bfloat16)
            joined = joined + part.astype(jnp.float32)
        entry_gates = lax.dynamic_index_in_dim(jnp.take(gates, safe_ids, axis=0), expert_id, 1, keepdims=False)
        total = total.at[safe_ids].add(jnp.where(live[:, None], joined * entry_gates[:, None], jnp.float32(0.0)))
        return (total, None)
    moe_out, unused = lax.scan(expert_step, jnp.zeros((TOKENS, D), jnp.float32), jnp.arange(EXPERTS, dtype=jnp.int32))
    hidden = (residual + moe_out).astype(jnp.bfloat16)
    return (server_qkv, server_out, server_gate_up, hidden, new_cache)
```

```python
import math

import jax
import jax.numpy as jnp
from jax import lax
from jax.sharding import PartitionSpec as P

norm_eps = 1e-06
rope_base = 50000.0


def rms_scale(values, gain_vec):
    return (
        values * lax.rsqrt(jnp.mean(values * values, axis=-1, keepdims=True) + norm_eps) * gain_vec
    )


def rotate_half(values, cosine, sine_part):
    half_width = values.shape[-1] // 2
    first_half = values[..., :half_width]
    second_half = values[..., half_width:]
    return jnp.concatenate(
        [
            first_half * cosine - second_half * sine_part,
            second_half * cosine + first_half * sine_part,
        ],
        axis=-1,
    )


def split_halves(weights):
    expert_count, rows_here, hidden_units = weights.shape
    return weights.reshape(expert_count, rows_here, 2, hidden_units // 2).transpose(0, 2, 1, 3)


def body(
    tokens,
    attn_gain,
    query_gain,
    key_gain,
    moe_gain,
    query_weight,
    key_weight,
    value_weight,
    out_weight,
    gate_weight,
    up_weight,
    down_weight,
    router_weight,
    page_store,
    prompt_lengths,
    continues,
    page_owner,
    page_slot,
    routes,
):
    req_count = lax.axis_size("req")
    req_index = lax.axis_index("req")
    lane_index = lax.axis_index("tp")
    joined_local = jnp.concatenate(
        [
            query_weight.astype(jnp.bfloat16),
            key_weight.astype(jnp.bfloat16),
            value_weight.astype(jnp.bfloat16),
        ],
        axis=1,
    )
    server_qkv, server_out = (
        lax.all_gather(joined_local, "req", axis=0, tiled=True),
        lax.all_gather(out_weight.astype(jnp.bfloat16), "req", axis=1, tiled=True),
    )
    expert_count, rows_here, hidden_units = gate_weight.shape
    half_units = hidden_units // 2
    packed = jnp.concatenate(
        [
            split_halves(gate_weight.astype(jnp.bfloat16)),
            split_halves(up_weight.astype(jnp.bfloat16)),
        ],
        axis=3,
    ).reshape(2 * expert_count, rows_here, hidden_units)
    server_gate_up = lax.all_to_all(packed, ("req", "tp"), split_axis=0, concat_axis=1, tiled=True)
    group_rows, model_width = tokens.shape
    tokens_f32 = tokens.astype(jnp.float32)
    normed = rms_scale(tokens_f32, attn_gain).astype(jnp.bfloat16)
    projected = jnp.dot(normed, server_qkv, preferred_element_type=jnp.float32)
    head_dim = query_gain.shape[0]
    lane_width = server_qkv.shape[1] // 3
    lane_heads = lane_width // head_dim
    query_raw = projected[:, :lane_width].reshape(group_rows, lane_heads, head_dim)
    key_raw = projected[:, lane_width : 2 * lane_width].reshape(group_rows, lane_heads, head_dim)
    value_raw = projected[:, 2 * lane_width :]
    first_length = lax.dynamic_index_in_dim(prompt_lengths, 2 * req_index, 0, keepdims=False)
    carry_flags = lax.dynamic_slice_in_dim(continues, 2 * req_index, 2)
    row_ids = jnp.arange(group_rows, dtype=jnp.int32)
    second = (row_ids >= first_length).astype(jnp.int32)
    within = row_ids - second * first_length
    carried = jnp.where(second == 1, carry_flags[1], carry_flags[0])
    pages_per = page_owner.shape[1]
    page_rows = page_store.shape[1]
    context_len = pages_per * page_rows
    position = (within + context_len * carried).astype(jnp.float32)
    inverse = jnp.power(
        jnp.float32(rope_base), -(jnp.arange(head_dim // 2, dtype=jnp.float32) * 2.0 / head_dim)
    )
    angles = position[:, None, None] * inverse[None, None, :]
    cosine = jnp.cos(angles)
    sine_part = jnp.sin(angles)
    query_rows = rotate_half(rms_scale(query_raw, query_gain), cosine, sine_part).astype(
        jnp.bfloat16
    )
    keys_new = rotate_half(rms_scale(key_raw, key_gain), cosine, sine_part).astype(jnp.bfloat16)
    values_new = value_raw.astype(jnp.bfloat16)
    new_cache = jnp.stack([keys_new.reshape(group_rows, lane_width), values_new], axis=1)
    capacity = max(2, (pages_per + req_count - 2) // (req_count - 1))
    page_ids = jnp.arange(pages_per, dtype=jnp.int32)
    earlier = page_ids[None, :] < page_ids[:, None]
    same_owner = page_owner[:, :, None] == page_owner[:, None, :]
    page_rank = jnp.sum((same_owner & earlier[None]).astype(jnp.int32), axis=2)
    owned_here = page_owner == req_index
    chosen = owned_here[:, None, :] & (
        page_rank[:, None, :] == jnp.arange(capacity, dtype=jnp.int32)[None, :, None]
    )
    send_slot = jnp.sum(jnp.where(chosen, page_slot[:, None, :], 0), axis=2)
    send_live = jnp.any(chosen, axis=2)
    page_shape = page_store.shape[1:]
    outgoing_pages = jnp.take(page_store, send_slot.reshape(-1), axis=0).reshape(
        (req_count, capacity) + page_shape
    )
    outgoing_pages = jnp.where(
        send_live[:, :, None, None, None], outgoing_pages, jnp.zeros_like(outgoing_pages)
    )
    arrived_pages = lax.all_to_all(outgoing_pages, "req", split_axis=0, concat_axis=0, tiled=True)
    own_owner = jnp.take(page_owner, req_index, axis=0)
    own_rank = jnp.take(page_rank, req_index, axis=0)
    context = jnp.take(
        arrived_pages.reshape((req_count * capacity,) + page_shape),
        own_owner * capacity + own_rank,
        axis=0,
    )
    context = context.reshape(context_len, 2, lane_heads, head_dim)
    score_scale = 1.0 / math.sqrt(head_dim)
    near_scores = (
        jnp.einsum("ihc,jhc->hij", query_rows, keys_new, preferred_element_type=jnp.float32)
        * score_scale
    )
    far_scores = (
        jnp.einsum("ihc,jhc->hij", query_rows, context[:, 0], preferred_element_type=jnp.float32)
        * score_scale
    )
    same_request = second[:, None] == second[None, :]
    near_weights = jnp.where(same_request[None], jnp.exp(near_scores), jnp.float32(0.0))
    far_weights = jnp.where((carried == 1)[None, :, None], jnp.exp(far_scores), jnp.float32(0.0))
    totals = jnp.sum(near_weights, axis=2, keepdims=True) + jnp.sum(
        far_weights, axis=2, keepdims=True
    )
    near_probs = (near_weights / totals).astype(jnp.bfloat16)
    far_probs = (far_weights / totals).astype(jnp.bfloat16)
    attended = jnp.einsum(
        "hij,jhc->ihc",
        near_probs,
        values_new.reshape(group_rows, lane_heads, head_dim),
        preferred_element_type=jnp.float32,
    )
    attended = attended + jnp.einsum(
        "hij,jhc->ihc", far_probs, context[:, 1], preferred_element_type=jnp.float32
    )
    attended = attended.astype(jnp.bfloat16).reshape(group_rows, lane_width)
    shard_rows = routes.shape[0]
    row_start = lane_index * shard_rows
    head_terms = jnp.dot(attended, server_out, preferred_element_type=jnp.float32)
    server_gate_up, head_terms = lax.optimization_barrier((server_gate_up, head_terms))
    mixed_own = lax.psum_scatter(head_terms, "tp", scatter_dimension=0, tiled=True)
    residual_own = lax.dynamic_slice_in_dim(tokens_f32, row_start, shard_rows, 0) + mixed_own
    moe_own = rms_scale(residual_own, moe_gain).astype(jnp.bfloat16)
    logits = jnp.dot(moe_own, router_weight, preferred_element_type=jnp.float32)
    exps = jnp.exp(logits)
    routed_exps = jnp.take_along_axis(exps, routes, axis=1)
    entry_gates = routed_exps / jnp.sum(routed_exps, axis=1, keepdims=True)
    top_count = routes.shape[1]
    slot_depth = 3 * shard_rows * top_count // (2 * expert_count)
    flat_routes = routes.reshape(-1)
    onehot = (flat_routes[:, None] == jnp.arange(expert_count, dtype=jnp.int32)[None, :]).astype(
        jnp.int32
    )
    entry_rank = jnp.sum((jnp.cumsum(onehot, axis=0) - onehot) * onehot, axis=1)
    entry_slot = (flat_routes * slot_depth + entry_rank).reshape(shard_rows, top_count)
    select_table = jnp.any(
        entry_slot[None, :, :]
        == jnp.arange(expert_count * slot_depth, dtype=jnp.int32)[:, None, None],
        axis=2,
    ).astype(jnp.bfloat16)
    outgoing_rows = jnp.dot(select_table, moe_own, preferred_element_type=jnp.float32).astype(
        jnp.bfloat16
    )
    send_rows = jnp.broadcast_to(
        outgoing_rows.reshape(expert_count, 1, slot_depth, model_width),
        (expert_count, 2, slot_depth, model_width),
    ).reshape(2 * expert_count, slot_depth, model_width)
    arrived_rows = lax.all_to_all(send_rows, ("req", "tp"), split_axis=0, concat_axis=0, tiled=True)
    flat_rows = arrived_rows.reshape(-1, model_width)
    both = jnp.dot(flat_rows, server_gate_up[0], preferred_element_type=jnp.float32)
    act = (jax.nn.silu(both[:, :half_units]) * both[:, half_units:]).astype(jnp.bfloat16)
    expert_rows = (
        jnp.dot(act, down_weight[0], preferred_element_type=jnp.float32)
        .astype(jnp.bfloat16)
        .reshape(arrived_rows.shape)
    )
    returned = lax.all_to_all(expert_rows, ("req", "tp"), split_axis=0, concat_axis=0, tiled=True)
    returned = returned.reshape(expert_count, 2, slot_depth, model_width)
    joined_out = (returned[:, 0].astype(jnp.float32) + returned[:, 1].astype(jnp.float32)).reshape(
        expert_count * slot_depth, model_width
    )
    picked_rows = jnp.take(joined_out, entry_slot.reshape(-1), axis=0).reshape(
        shard_rows, top_count, model_width
    )
    moe_out = jnp.sum(picked_rows * entry_gates[:, :, None], axis=1)
    hidden_rows = (residual_own + moe_out).astype(jnp.bfloat16)
    return (server_qkv, server_out, server_gate_up, hidden_rows, new_cache)


def solution(mesh):
    in_specs = (
        P("req", None),
        P(),
        P(),
        P(),
        P(),
        P("req", "tp"),
        P("req", "tp"),
        P("req", "tp"),
        P("tp", "req"),
        P(None, ("req", "tp"), None),
        P(None, ("req", "tp"), None),
        P(("req", "tp"), None, None),
        P(),
        P("req", None, None, "tp"),
        P(),
        P(),
        P(),
        P(),
        P(("req", "tp"), None),
    )
    out_specs = (
        P(None, "tp"),
        P("tp", None),
        P(("req", "tp"), None, None),
        P(("req", "tp"), None),
        P("req", None, "tp"),
    )
    return jax.shard_map(body, mesh=mesh, in_specs=in_specs, out_specs=out_specs, check_vma=False)
```

```python
import functools
import math

import jax
import jax.numpy as jnp
from jax import lax
from jax.experimental import pallas as pl
from jax.experimental.pallas import tpu as pltpu
from jax.sharding import PartitionSpec as P

MESH = pl.DeviceIdType.MESH

norm_eps = 1e-06
rope_base = 50000.0


def rms_scale(values, gain_vec):
    return (
        values * lax.rsqrt(jnp.mean(values * values, axis=-1, keepdims=True) + norm_eps) * gain_vec
    )


def rotate_half(values, cosine, sine_part):
    half_width = values.shape[-1] // 2
    first_half = values[..., :half_width]
    second_half = values[..., half_width:]
    return jnp.concatenate(
        [
            first_half * cosine - second_half * sine_part,
            second_half * cosine + first_half * sine_part,
        ],
        axis=-1,
    )


def split_halves(weights):
    expert_count, rows_here, hidden_units = weights.shape
    return weights.reshape(expert_count, rows_here, 2, hidden_units // 2).transpose(0, 2, 1, 3)


def scatter_sum_kernel(parts, x_ref, out_ref, held, send_sem, recv_sem):
    me = lax.axis_index("tp")
    group = lax.axis_index("req")
    rows = out_ref.shape[0]
    barrier = pltpu.get_barrier_semaphore()
    for step in range(1, parts):
        peer = lax.rem(me + step, parts)
        pl.semaphore_signal(barrier, inc=1, device_id=(group, peer), device_id_type=MESH)
    pl.semaphore_wait(barrier, parts - 1)

    def outgoing(peer):
        return pltpu.make_async_remote_copy(
            src_ref=x_ref.at[pl.ds(pl.multiple_of(peer * rows, rows), rows)],
            dst_ref=held.at[me],
            send_sem=send_sem.at[peer],
            recv_sem=recv_sem.at[me],
            device_id=(group, peer),
            device_id_type=MESH,
        )

    def incoming(peer):
        return pltpu.make_async_remote_copy(
            src_ref=x_ref.at[pl.ds(pl.multiple_of(me * rows, rows), rows)],
            dst_ref=held.at[peer],
            send_sem=send_sem.at[peer],
            recv_sem=recv_sem.at[peer],
            device_id=(group, peer),
            device_id_type=MESH,
        )

    for step in range(1, parts):
        outgoing(lax.rem(me + step, parts)).start()
    total = x_ref[pl.ds(pl.multiple_of(me * rows, rows), rows), :]
    for step in range(1, parts):
        peer = lax.rem(me + parts - step, parts)
        incoming(peer).wait_recv()
        total = total + held[peer]
    for step in range(1, parts):
        outgoing(lax.rem(me + step, parts)).wait_send()
    out_ref[...] = total


def scatter_sum(x, parts):
    rows = x.shape[0] // parts
    return pl.pallas_call(
        functools.partial(scatter_sum_kernel, parts),
        out_shape=jax.ShapeDtypeStruct((rows, x.shape[1]), x.dtype),
        in_specs=[pl.BlockSpec(memory_space=pltpu.VMEM)],
        out_specs=pl.BlockSpec(memory_space=pltpu.VMEM),
        scratch_shapes=[
            pltpu.VMEM((parts, rows, x.shape[1]), x.dtype),
            pltpu.SemaphoreType.DMA((parts,)),
            pltpu.SemaphoreType.DMA((parts,)),
        ],
        compiler_params=pltpu.CompilerParams(collective_id=0, has_side_effects=True),
    )(x)


def body(
    tokens,
    attn_gain,
    query_gain,
    key_gain,
    moe_gain,
    query_weight,
    key_weight,
    value_weight,
    out_weight,
    gate_weight,
    up_weight,
    down_weight,
    router_weight,
    page_store,
    prompt_lengths,
    continues,
    page_owner,
    page_slot,
    routes,
):
    req_count = lax.axis_size("req")
    req_index = lax.axis_index("req")
    lane_index = lax.axis_index("tp")
    joined_local = jnp.concatenate(
        [
            query_weight.astype(jnp.bfloat16),
            key_weight.astype(jnp.bfloat16),
            value_weight.astype(jnp.bfloat16),
        ],
        axis=1,
    )
    server_qkv, server_out = (
        lax.all_gather(joined_local, "req", axis=0, tiled=True),
        lax.all_gather(out_weight.astype(jnp.bfloat16), "req", axis=1, tiled=True),
    )
    expert_count, rows_here, hidden_units = gate_weight.shape
    half_units = hidden_units // 2
    packed = jnp.concatenate(
        [
            split_halves(gate_weight.astype(jnp.bfloat16)),
            split_halves(up_weight.astype(jnp.bfloat16)),
        ],
        axis=3,
    ).reshape(2 * expert_count, rows_here, hidden_units)
    server_gate_up = lax.all_to_all(packed, ("req", "tp"), split_axis=0, concat_axis=1, tiled=True)
    group_rows, model_width = tokens.shape
    tokens_f32 = tokens.astype(jnp.float32)
    normed = rms_scale(tokens_f32, attn_gain).astype(jnp.bfloat16)
    projected = jnp.dot(normed, server_qkv, preferred_element_type=jnp.float32)
    head_dim = query_gain.shape[0]
    lane_width = server_qkv.shape[1] // 3
    lane_heads = lane_width // head_dim
    query_raw = projected[:, :lane_width].reshape(group_rows, lane_heads, head_dim)
    key_raw = projected[:, lane_width : 2 * lane_width].reshape(group_rows, lane_heads, head_dim)
    value_raw = projected[:, 2 * lane_width :]
    first_length = lax.dynamic_index_in_dim(prompt_lengths, 2 * req_index, 0, keepdims=False)
    carry_flags = lax.dynamic_slice_in_dim(continues, 2 * req_index, 2)
    row_ids = jnp.arange(group_rows, dtype=jnp.int32)
    second = (row_ids >= first_length).astype(jnp.int32)
    within = row_ids - second * first_length
    carried = jnp.where(second == 1, carry_flags[1], carry_flags[0])
    pages_per = page_owner.shape[1]
    page_rows = page_store.shape[1]
    context_len = pages_per * page_rows
    position = (within + context_len * carried).astype(jnp.float32)
    inverse = jnp.power(
        jnp.float32(rope_base), -(jnp.arange(head_dim // 2, dtype=jnp.float32) * 2.0 / head_dim)
    )
    angles = position[:, None, None] * inverse[None, None, :]
    cosine = jnp.cos(angles)
    sine_part = jnp.sin(angles)
    query_rows = rotate_half(rms_scale(query_raw, query_gain), cosine, sine_part).astype(
        jnp.bfloat16
    )
    keys_new = rotate_half(rms_scale(key_raw, key_gain), cosine, sine_part).astype(jnp.bfloat16)
    values_new = value_raw.astype(jnp.bfloat16)
    new_cache = jnp.stack([keys_new.reshape(group_rows, lane_width), values_new], axis=1)
    capacity = max(2, (pages_per + req_count - 2) // (req_count - 1))
    page_ids = jnp.arange(pages_per, dtype=jnp.int32)
    earlier = page_ids[None, :] < page_ids[:, None]
    same_owner = page_owner[:, :, None] == page_owner[:, None, :]
    page_rank = jnp.sum((same_owner & earlier[None]).astype(jnp.int32), axis=2)
    owned_here = page_owner == req_index
    chosen = owned_here[:, None, :] & (
        page_rank[:, None, :] == jnp.arange(capacity, dtype=jnp.int32)[None, :, None]
    )
    send_slot = jnp.sum(jnp.where(chosen, page_slot[:, None, :], 0), axis=2)
    send_live = jnp.any(chosen, axis=2)
    page_shape = page_store.shape[1:]
    outgoing_pages = jnp.take(page_store, send_slot.reshape(-1), axis=0).reshape(
        (req_count, capacity) + page_shape
    )
    outgoing_pages = jnp.where(
        send_live[:, :, None, None, None], outgoing_pages, jnp.zeros_like(outgoing_pages)
    )
    arrived_pages = lax.all_to_all(outgoing_pages, "req", split_axis=0, concat_axis=0, tiled=True)
    own_owner = jnp.take(page_owner, req_index, axis=0)
    own_rank = jnp.take(page_rank, req_index, axis=0)
    context = jnp.take(
        arrived_pages.reshape((req_count * capacity,) + page_shape),
        own_owner * capacity + own_rank,
        axis=0,
    )
    context = context.reshape(context_len, 2, lane_heads, head_dim)
    score_scale = 1.0 / math.sqrt(head_dim)
    near_scores = (
        jnp.einsum("ihc,jhc->hij", query_rows, keys_new, preferred_element_type=jnp.float32)
        * score_scale
    )
    far_scores = (
        jnp.einsum("ihc,jhc->hij", query_rows, context[:, 0], preferred_element_type=jnp.float32)
        * score_scale
    )
    same_request = second[:, None] == second[None, :]
    near_weights = jnp.where(same_request[None], jnp.exp(near_scores), jnp.float32(0.0))
    far_weights = jnp.where((carried == 1)[None, :, None], jnp.exp(far_scores), jnp.float32(0.0))
    totals = jnp.sum(near_weights, axis=2, keepdims=True) + jnp.sum(
        far_weights, axis=2, keepdims=True
    )
    near_probs = (near_weights / totals).astype(jnp.bfloat16)
    far_probs = (far_weights / totals).astype(jnp.bfloat16)
    attended = jnp.einsum(
        "hij,jhc->ihc",
        near_probs,
        values_new.reshape(group_rows, lane_heads, head_dim),
        preferred_element_type=jnp.float32,
    )
    attended = attended + jnp.einsum(
        "hij,jhc->ihc", far_probs, context[:, 1], preferred_element_type=jnp.float32
    )
    attended = attended.astype(jnp.bfloat16).reshape(group_rows, lane_width)
    shard_rows = routes.shape[0]
    row_start = lane_index * shard_rows
    head_terms = jnp.dot(attended, server_out, preferred_element_type=jnp.float32)
    server_gate_up, head_terms = lax.optimization_barrier((server_gate_up, head_terms))
    mixed_own = scatter_sum(head_terms, lax.axis_size("tp"))
    residual_own = lax.dynamic_slice_in_dim(tokens_f32, row_start, shard_rows, 0) + mixed_own
    moe_own = rms_scale(residual_own, moe_gain).astype(jnp.bfloat16)
    logits = jnp.dot(moe_own, router_weight, preferred_element_type=jnp.float32)
    exps = jnp.exp(logits)
    routed_exps = jnp.take_along_axis(exps, routes, axis=1)
    entry_gates = routed_exps / jnp.sum(routed_exps, axis=1, keepdims=True)
    top_count = routes.shape[1]
    slot_depth = 3 * shard_rows * top_count // (2 * expert_count)
    flat_routes = routes.reshape(-1)
    onehot = (flat_routes[:, None] == jnp.arange(expert_count, dtype=jnp.int32)[None, :]).astype(
        jnp.int32
    )
    entry_rank = jnp.sum((jnp.cumsum(onehot, axis=0) - onehot) * onehot, axis=1)
    entry_slot = (flat_routes * slot_depth + entry_rank).reshape(shard_rows, top_count)
    select_table = jnp.any(
        entry_slot[None, :, :]
        == jnp.arange(expert_count * slot_depth, dtype=jnp.int32)[:, None, None],
        axis=2,
    ).astype(jnp.bfloat16)
    outgoing_rows = jnp.dot(select_table, moe_own, preferred_element_type=jnp.float32).astype(
        jnp.bfloat16
    )
    send_rows = jnp.broadcast_to(
        outgoing_rows.reshape(expert_count, 1, slot_depth, model_width),
        (expert_count, 2, slot_depth, model_width),
    ).reshape(2 * expert_count, slot_depth, model_width)
    arrived_rows = lax.all_to_all(send_rows, ("req", "tp"), split_axis=0, concat_axis=0, tiled=True)
    flat_rows = arrived_rows.reshape(-1, model_width)
    both = jnp.dot(flat_rows, server_gate_up[0], preferred_element_type=jnp.float32)
    act = (jax.nn.silu(both[:, :half_units]) * both[:, half_units:]).astype(jnp.bfloat16)
    expert_rows = (
        jnp.dot(act, down_weight[0], preferred_element_type=jnp.float32)
        .astype(jnp.bfloat16)
        .reshape(arrived_rows.shape)
    )
    returned = lax.all_to_all(expert_rows, ("req", "tp"), split_axis=0, concat_axis=0, tiled=True)
    returned = returned.reshape(expert_count, 2, slot_depth, model_width)
    joined_out = (returned[:, 0].astype(jnp.float32) + returned[:, 1].astype(jnp.float32)).reshape(
        expert_count * slot_depth, model_width
    )
    picked_rows = jnp.take(joined_out, entry_slot.reshape(-1), axis=0).reshape(
        shard_rows, top_count, model_width
    )
    moe_out = jnp.sum(picked_rows * entry_gates[:, :, None], axis=1)
    hidden_rows = (residual_own + moe_out).astype(jnp.bfloat16)
    return (server_qkv, server_out, server_gate_up, hidden_rows, new_cache)


def solution(mesh):
    in_specs = (
        P("req", None),
        P(),
        P(),
        P(),
        P(),
        P("req", "tp"),
        P("req", "tp"),
        P("req", "tp"),
        P("tp", "req"),
        P(None, ("req", "tp"), None),
        P(None, ("req", "tp"), None),
        P(("req", "tp"), None, None),
        P(),
        P("req", None, None, "tp"),
        P(),
        P(),
        P(),
        P(),
        P(("req", "tp"), None),
    )
    out_specs = (
        P(None, "tp"),
        P("tp", None),
        P(("req", "tp"), None, None),
        P(("req", "tp"), None),
        P("req", None, "tp"),
    )
    return jax.shard_map(body, mesh=mesh, in_specs=in_specs, out_specs=out_specs, check_vma=False)
```

```python
import functools
import math

import jax
import jax.numpy as jnp
from jax import lax
from jax.experimental import pallas as pl
from jax.experimental.pallas import tpu as pltpu
from jax.sharding import PartitionSpec as P

MESH = pl.DeviceIdType.MESH

norm_eps = 1e-06
rope_base = 50000.0


def rms_scale(values, gain_vec):
    return (
        values * lax.rsqrt(jnp.mean(values * values, axis=-1, keepdims=True) + norm_eps) * gain_vec
    )


def rotate_half(values, cosine, sine_part):
    half_width = values.shape[-1] // 2
    first_half = values[..., :half_width]
    second_half = values[..., half_width:]
    return jnp.concatenate(
        [
            first_half * cosine - second_half * sine_part,
            second_half * cosine + first_half * sine_part,
        ],
        axis=-1,
    )


def split_halves(weights):
    expert_count, rows_here, hidden_units = weights.shape
    return weights.reshape(expert_count, rows_here, 2, hidden_units // 2).transpose(0, 2, 1, 3)


def scatter_sum_kernel(parts, x_ref, out_ref, held, send_sem, recv_sem):
    me = lax.axis_index("tp")
    group = lax.axis_index("req")
    rows = out_ref.shape[0]
    barrier = pltpu.get_barrier_semaphore()
    for step in range(1, parts):
        peer = lax.rem(me + step, parts)
        pl.semaphore_signal(barrier, inc=1, device_id=(group, peer), device_id_type=MESH)
    pl.semaphore_wait(barrier, parts - 1)

    def outgoing(peer):
        return pltpu.make_async_remote_copy(
            src_ref=x_ref.at[pl.ds(pl.multiple_of(peer * rows, rows), rows)],
            dst_ref=held.at[me],
            send_sem=send_sem.at[peer],
            recv_sem=recv_sem.at[me],
            device_id=(group, peer),
            device_id_type=MESH,
        )

    def incoming(peer):
        return pltpu.make_async_remote_copy(
            src_ref=x_ref.at[pl.ds(pl.multiple_of(me * rows, rows), rows)],
            dst_ref=held.at[peer],
            send_sem=send_sem.at[peer],
            recv_sem=recv_sem.at[peer],
            device_id=(group, peer),
            device_id_type=MESH,
        )

    for step in range(1, parts):
        outgoing(lax.rem(me + step, parts)).start()
    total = x_ref[pl.ds(pl.multiple_of(me * rows, rows), rows), :]
    for step in range(1, parts):
        peer = lax.rem(me + parts - step, parts)
        incoming(peer).wait_recv()
        total = total + held[peer]
    for step in range(1, parts):
        outgoing(lax.rem(me + step, parts)).wait_send()
    out_ref[...] = total


def scatter_sum(x, parts):
    rows = x.shape[0] // parts
    return pl.pallas_call(
        functools.partial(scatter_sum_kernel, parts),
        out_shape=jax.ShapeDtypeStruct((rows, x.shape[1]), x.dtype),
        in_specs=[pl.BlockSpec(memory_space=pltpu.VMEM)],
        out_specs=pl.BlockSpec(memory_space=pltpu.VMEM),
        scratch_shapes=[
            pltpu.VMEM((parts, rows, x.shape[1]), x.dtype),
            pltpu.SemaphoreType.DMA((parts,)),
            pltpu.SemaphoreType.DMA((parts,)),
        ],
        compiler_params=pltpu.CompilerParams(collective_id=0, has_side_effects=True),
    )(x)


def exchange_kernel(count, width, x_ref, out_ref, held, send_sem, recv_sem):
    me = lax.axis_index("req") * width + lax.axis_index("tp")
    barrier = pltpu.get_barrier_semaphore()

    def greet(step, carry):
        peer = lax.rem(me + step, count)
        pl.semaphore_signal(
            barrier, inc=1, device_id=(peer // width, lax.rem(peer, width)), device_id_type=MESH
        )
        return carry

    lax.fori_loop(1, count, greet, 0)
    pl.semaphore_wait(barrier, count - 1)

    def send(step, carry):
        peer = lax.rem(me + step, count)
        pltpu.make_async_remote_copy(
            src_ref=x_ref.at[peer],
            dst_ref=held.at[me],
            send_sem=send_sem,
            recv_sem=recv_sem,
            device_id=(peer // width, lax.rem(peer, width)),
            device_id_type=MESH,
        ).start()
        return carry

    lax.fori_loop(1, count, send, 0)
    held[me] = x_ref[me]
    everything = pltpu.make_async_remote_copy(
        src_ref=x_ref.at[pl.ds(0, count - 1)],
        dst_ref=held.at[pl.ds(0, count - 1)],
        send_sem=send_sem,
        recv_sem=recv_sem,
        device_id=(0, 0),
        device_id_type=MESH,
    )
    everything.wait_recv()
    everything.wait_send()
    out_ref[...] = held[...]


def exchange(x, collective):
    count = x.shape[0]
    width = lax.axis_size("tp")
    return pl.pallas_call(
        functools.partial(exchange_kernel, count, width),
        out_shape=jax.ShapeDtypeStruct(x.shape, x.dtype),
        in_specs=[pl.BlockSpec(memory_space=pltpu.VMEM)],
        out_specs=pl.BlockSpec(memory_space=pltpu.VMEM),
        scratch_shapes=[
            pltpu.VMEM(x.shape, x.dtype),
            pltpu.SemaphoreType.DMA(()),
            pltpu.SemaphoreType.DMA(()),
        ],
        compiler_params=pltpu.CompilerParams(collective_id=collective, has_side_effects=True),
    )(x)


def body(
    tokens,
    attn_gain,
    query_gain,
    key_gain,
    moe_gain,
    query_weight,
    key_weight,
    value_weight,
    out_weight,
    gate_weight,
    up_weight,
    down_weight,
    router_weight,
    page_store,
    prompt_lengths,
    continues,
    page_owner,
    page_slot,
    routes,
):
    req_count = lax.axis_size("req")
    req_index = lax.axis_index("req")
    lane_index = lax.axis_index("tp")
    joined_local = jnp.concatenate(
        [
            query_weight.astype(jnp.bfloat16),
            key_weight.astype(jnp.bfloat16),
            value_weight.astype(jnp.bfloat16),
        ],
        axis=1,
    )
    server_qkv, server_out = (
        lax.all_gather(joined_local, "req", axis=0, tiled=True),
        lax.all_gather(out_weight.astype(jnp.bfloat16), "req", axis=1, tiled=True),
    )
    expert_count, rows_here, hidden_units = gate_weight.shape
    half_units = hidden_units // 2
    packed = jnp.concatenate(
        [
            split_halves(gate_weight.astype(jnp.bfloat16)),
            split_halves(up_weight.astype(jnp.bfloat16)),
        ],
        axis=3,
    ).reshape(2 * expert_count, rows_here, hidden_units)
    server_gate_up = lax.all_to_all(packed, ("req", "tp"), split_axis=0, concat_axis=1, tiled=True)
    group_rows, model_width = tokens.shape
    tokens_f32 = tokens.astype(jnp.float32)
    normed = rms_scale(tokens_f32, attn_gain).astype(jnp.bfloat16)
    projected = jnp.dot(normed, server_qkv, preferred_element_type=jnp.float32)
    head_dim = query_gain.shape[0]
    lane_width = server_qkv.shape[1] // 3
    lane_heads = lane_width // head_dim
    query_raw = projected[:, :lane_width].reshape(group_rows, lane_heads, head_dim)
    key_raw = projected[:, lane_width : 2 * lane_width].reshape(group_rows, lane_heads, head_dim)
    value_raw = projected[:, 2 * lane_width :]
    first_length = lax.dynamic_index_in_dim(prompt_lengths, 2 * req_index, 0, keepdims=False)
    carry_flags = lax.dynamic_slice_in_dim(continues, 2 * req_index, 2)
    row_ids = jnp.arange(group_rows, dtype=jnp.int32)
    second = (row_ids >= first_length).astype(jnp.int32)
    within = row_ids - second * first_length
    carried = jnp.where(second == 1, carry_flags[1], carry_flags[0])
    pages_per = page_owner.shape[1]
    page_rows = page_store.shape[1]
    context_len = pages_per * page_rows
    position = (within + context_len * carried).astype(jnp.float32)
    inverse = jnp.power(
        jnp.float32(rope_base), -(jnp.arange(head_dim // 2, dtype=jnp.float32) * 2.0 / head_dim)
    )
    angles = position[:, None, None] * inverse[None, None, :]
    cosine = jnp.cos(angles)
    sine_part = jnp.sin(angles)
    query_rows = rotate_half(rms_scale(query_raw, query_gain), cosine, sine_part).astype(
        jnp.bfloat16
    )
    keys_new = rotate_half(rms_scale(key_raw, key_gain), cosine, sine_part).astype(jnp.bfloat16)
    values_new = value_raw.astype(jnp.bfloat16)
    new_cache = jnp.stack([keys_new.reshape(group_rows, lane_width), values_new], axis=1)
    capacity = max(2, (pages_per + req_count - 2) // (req_count - 1))
    page_ids = jnp.arange(pages_per, dtype=jnp.int32)
    earlier = page_ids[None, :] < page_ids[:, None]
    same_owner = page_owner[:, :, None] == page_owner[:, None, :]
    page_rank = jnp.sum((same_owner & earlier[None]).astype(jnp.int32), axis=2)
    owned_here = page_owner == req_index
    chosen = owned_here[:, None, :] & (
        page_rank[:, None, :] == jnp.arange(capacity, dtype=jnp.int32)[None, :, None]
    )
    send_slot = jnp.sum(jnp.where(chosen, page_slot[:, None, :], 0), axis=2)
    send_live = jnp.any(chosen, axis=2)
    page_shape = page_store.shape[1:]
    outgoing_pages = jnp.take(page_store, send_slot.reshape(-1), axis=0).reshape(
        (req_count, capacity) + page_shape
    )
    outgoing_pages = jnp.where(
        send_live[:, :, None, None, None], outgoing_pages, jnp.zeros_like(outgoing_pages)
    )
    arrived_pages = lax.all_to_all(outgoing_pages, "req", split_axis=0, concat_axis=0, tiled=True)
    own_owner = jnp.take(page_owner, req_index, axis=0)
    own_rank = jnp.take(page_rank, req_index, axis=0)
    context = jnp.take(
        arrived_pages.reshape((req_count * capacity,) + page_shape),
        own_owner * capacity + own_rank,
        axis=0,
    )
    context = context.reshape(context_len, 2, lane_heads, head_dim)
    score_scale = 1.0 / math.sqrt(head_dim)
    near_scores = (
        jnp.einsum("ihc,jhc->hij", query_rows, keys_new, preferred_element_type=jnp.float32)
        * score_scale
    )
    far_scores = (
        jnp.einsum("ihc,jhc->hij", query_rows, context[:, 0], preferred_element_type=jnp.float32)
        * score_scale
    )
    same_request = second[:, None] == second[None, :]
    near_weights = jnp.where(same_request[None], jnp.exp(near_scores), jnp.float32(0.0))
    far_weights = jnp.where((carried == 1)[None, :, None], jnp.exp(far_scores), jnp.float32(0.0))
    totals = jnp.sum(near_weights, axis=2, keepdims=True) + jnp.sum(
        far_weights, axis=2, keepdims=True
    )
    near_probs = (near_weights / totals).astype(jnp.bfloat16)
    far_probs = (far_weights / totals).astype(jnp.bfloat16)
    attended = jnp.einsum(
        "hij,jhc->ihc",
        near_probs,
        values_new.reshape(group_rows, lane_heads, head_dim),
        preferred_element_type=jnp.float32,
    )
    attended = attended + jnp.einsum(
        "hij,jhc->ihc", far_probs, context[:, 1], preferred_element_type=jnp.float32
    )
    attended = attended.astype(jnp.bfloat16).reshape(group_rows, lane_width)
    shard_rows = routes.shape[0]
    row_start = lane_index * shard_rows
    head_terms = jnp.dot(attended, server_out, preferred_element_type=jnp.float32)
    server_gate_up, head_terms = lax.optimization_barrier((server_gate_up, head_terms))
    mixed_own = scatter_sum(head_terms, lax.axis_size("tp"))
    residual_own = lax.dynamic_slice_in_dim(tokens_f32, row_start, shard_rows, 0) + mixed_own
    moe_own = rms_scale(residual_own, moe_gain).astype(jnp.bfloat16)
    logits = jnp.dot(moe_own, router_weight, preferred_element_type=jnp.float32)
    exps = jnp.exp(logits)
    routed_exps = jnp.take_along_axis(exps, routes, axis=1)
    entry_gates = routed_exps / jnp.sum(routed_exps, axis=1, keepdims=True)
    top_count = routes.shape[1]
    slot_depth = 3 * shard_rows * top_count // (2 * expert_count)
    flat_routes = routes.reshape(-1)
    onehot = (flat_routes[:, None] == jnp.arange(expert_count, dtype=jnp.int32)[None, :]).astype(
        jnp.int32
    )
    entry_rank = jnp.sum((jnp.cumsum(onehot, axis=0) - onehot) * onehot, axis=1)
    entry_slot = (flat_routes * slot_depth + entry_rank).reshape(shard_rows, top_count)
    select_table = jnp.any(
        entry_slot[None, :, :]
        == jnp.arange(expert_count * slot_depth, dtype=jnp.int32)[:, None, None],
        axis=2,
    ).astype(jnp.bfloat16)
    outgoing_rows = jnp.dot(select_table, moe_own, preferred_element_type=jnp.float32).astype(
        jnp.bfloat16
    )
    send_rows = jnp.broadcast_to(
        outgoing_rows.reshape(expert_count, 1, slot_depth, model_width),
        (expert_count, 2, slot_depth, model_width),
    ).reshape(2 * expert_count, slot_depth, model_width)
    arrived_rows = exchange(send_rows, 1)
    flat_rows = arrived_rows.reshape(-1, model_width)
    both = jnp.dot(flat_rows, server_gate_up[0], preferred_element_type=jnp.float32)
    act = (jax.nn.silu(both[:, :half_units]) * both[:, half_units:]).astype(jnp.bfloat16)
    expert_rows = (
        jnp.dot(act, down_weight[0], preferred_element_type=jnp.float32)
        .astype(jnp.bfloat16)
        .reshape(arrived_rows.shape)
    )
    returned = exchange(expert_rows, 2)
    returned = returned.reshape(expert_count, 2, slot_depth, model_width)
    joined_out = (returned[:, 0].astype(jnp.float32) + returned[:, 1].astype(jnp.float32)).reshape(
        expert_count * slot_depth, model_width
    )
    picked_rows = jnp.take(joined_out, entry_slot.reshape(-1), axis=0).reshape(
        shard_rows, top_count, model_width
    )
    moe_out = jnp.sum(picked_rows * entry_gates[:, :, None], axis=1)
    hidden_rows = (residual_own + moe_out).astype(jnp.bfloat16)
    return (server_qkv, server_out, server_gate_up, hidden_rows, new_cache)


def solution(mesh):
    in_specs = (
        P("req", None),
        P(),
        P(),
        P(),
        P(),
        P("req", "tp"),
        P("req", "tp"),
        P("req", "tp"),
        P("tp", "req"),
        P(None, ("req", "tp"), None),
        P(None, ("req", "tp"), None),
        P(("req", "tp"), None, None),
        P(),
        P("req", None, None, "tp"),
        P(),
        P(),
        P(),
        P(),
        P(("req", "tp"), None),
    )
    out_specs = (
        P(None, "tp"),
        P("tp", None),
        P(("req", "tp"), None, None),
        P(("req", "tp"), None),
        P("req", None, "tp"),
    )
    return jax.shard_map(body, mesh=mesh, in_specs=in_specs, out_specs=out_specs, check_vma=False)
```

```python
import functools
import math

import jax
import jax.numpy as jnp
from jax import lax
from jax.experimental import pallas as pl
from jax.experimental.pallas import tpu as pltpu
from jax.sharding import PartitionSpec as P

MESH = pl.DeviceIdType.MESH

norm_eps = 1e-06
rope_base = 50000.0


def rms_scale(values, gain_vec):
    return (
        values * lax.rsqrt(jnp.mean(values * values, axis=-1, keepdims=True) + norm_eps) * gain_vec
    )


def rotate_half(values, cosine, sine_part):
    half_width = values.shape[-1] // 2
    first_half = values[..., :half_width]
    second_half = values[..., half_width:]
    return jnp.concatenate(
        [
            first_half * cosine - second_half * sine_part,
            second_half * cosine + first_half * sine_part,
        ],
        axis=-1,
    )


def split_halves(weights):
    expert_count, rows_here, hidden_units = weights.shape
    return weights.reshape(expert_count, rows_here, 2, hidden_units // 2).transpose(0, 2, 1, 3)


def scatter_sum_kernel(parts, x_ref, out_ref, held, send_sem, recv_sem):
    me = lax.axis_index("tp")
    group = lax.axis_index("req")
    rows = out_ref.shape[0]
    barrier = pltpu.get_barrier_semaphore()
    for step in range(1, parts):
        peer = lax.rem(me + step, parts)
        pl.semaphore_signal(barrier, inc=1, device_id=(group, peer), device_id_type=MESH)
    pl.semaphore_wait(barrier, parts - 1)

    def outgoing(peer):
        return pltpu.make_async_remote_copy(
            src_ref=x_ref.at[pl.ds(pl.multiple_of(peer * rows, rows), rows)],
            dst_ref=held.at[me],
            send_sem=send_sem.at[peer],
            recv_sem=recv_sem.at[me],
            device_id=(group, peer),
            device_id_type=MESH,
        )

    def incoming(peer):
        return pltpu.make_async_remote_copy(
            src_ref=x_ref.at[pl.ds(pl.multiple_of(me * rows, rows), rows)],
            dst_ref=held.at[peer],
            send_sem=send_sem.at[peer],
            recv_sem=recv_sem.at[peer],
            device_id=(group, peer),
            device_id_type=MESH,
        )

    for step in range(1, parts):
        outgoing(lax.rem(me + step, parts)).start()
    total = x_ref[pl.ds(pl.multiple_of(me * rows, rows), rows), :]
    for step in range(1, parts):
        peer = lax.rem(me + parts - step, parts)
        incoming(peer).wait_recv()
        total = total + held[peer]
    for step in range(1, parts):
        outgoing(lax.rem(me + step, parts)).wait_send()
    out_ref[...] = total


def scatter_sum(x, parts):
    rows = x.shape[0] // parts
    return pl.pallas_call(
        functools.partial(scatter_sum_kernel, parts),
        out_shape=jax.ShapeDtypeStruct((rows, x.shape[1]), x.dtype),
        in_specs=[pl.BlockSpec(memory_space=pltpu.VMEM)],
        out_specs=pl.BlockSpec(memory_space=pltpu.VMEM),
        scratch_shapes=[
            pltpu.VMEM((parts, rows, x.shape[1]), x.dtype),
            pltpu.SemaphoreType.DMA((parts,)),
            pltpu.SemaphoreType.DMA((parts,)),
        ],
        compiler_params=pltpu.CompilerParams(collective_id=0, has_side_effects=True),
    )(x)


def body(
    tokens,
    attn_gain,
    query_gain,
    key_gain,
    moe_gain,
    query_weight,
    key_weight,
    value_weight,
    out_weight,
    gate_weight,
    up_weight,
    down_weight,
    router_weight,
    page_store,
    prompt_lengths,
    continues,
    page_owner,
    page_slot,
    routes,
):
    req_count = lax.axis_size("req")
    req_index = lax.axis_index("req")
    lane_index = lax.axis_index("tp")
    joined_local = jnp.concatenate(
        [
            query_weight.astype(jnp.bfloat16),
            key_weight.astype(jnp.bfloat16),
            value_weight.astype(jnp.bfloat16),
        ],
        axis=1,
    )
    server_qkv = lax.all_gather(joined_local, "req", axis=0, tiled=True)
    out_block = out_weight.astype(jnp.bfloat16)
    expert_count, rows_here, hidden_units = gate_weight.shape
    half_units = hidden_units // 2
    packed = jnp.concatenate(
        [
            split_halves(gate_weight.astype(jnp.bfloat16)),
            split_halves(up_weight.astype(jnp.bfloat16)),
        ],
        axis=3,
    ).reshape(2 * expert_count, rows_here, hidden_units)
    server_gate_up = lax.all_to_all(packed, ("req", "tp"), split_axis=0, concat_axis=1, tiled=True)
    group_rows, model_width = tokens.shape
    tokens_f32 = tokens.astype(jnp.float32)
    normed = rms_scale(tokens_f32, attn_gain).astype(jnp.bfloat16)
    projected = jnp.dot(normed, server_qkv, preferred_element_type=jnp.float32)
    head_dim = query_gain.shape[0]
    lane_width = server_qkv.shape[1] // 3
    lane_heads = lane_width // head_dim
    query_raw = projected[:, :lane_width].reshape(group_rows, lane_heads, head_dim)
    key_raw = projected[:, lane_width : 2 * lane_width].reshape(group_rows, lane_heads, head_dim)
    value_raw = projected[:, 2 * lane_width :]
    first_length = lax.dynamic_index_in_dim(prompt_lengths, 2 * req_index, 0, keepdims=False)
    carry_flags = lax.dynamic_slice_in_dim(continues, 2 * req_index, 2)
    row_ids = jnp.arange(group_rows, dtype=jnp.int32)
    second = (row_ids >= first_length).astype(jnp.int32)
    within = row_ids - second * first_length
    carried = jnp.where(second == 1, carry_flags[1], carry_flags[0])
    pages_per = page_owner.shape[1]
    page_rows = page_store.shape[1]
    context_len = pages_per * page_rows
    position = (within + context_len * carried).astype(jnp.float32)
    inverse = jnp.power(
        jnp.float32(rope_base), -(jnp.arange(head_dim // 2, dtype=jnp.float32) * 2.0 / head_dim)
    )
    angles = position[:, None, None] * inverse[None, None, :]
    cosine = jnp.cos(angles)
    sine_part = jnp.sin(angles)
    query_rows = rotate_half(rms_scale(query_raw, query_gain), cosine, sine_part).astype(
        jnp.bfloat16
    )
    keys_new = rotate_half(rms_scale(key_raw, key_gain), cosine, sine_part).astype(jnp.bfloat16)
    values_new = value_raw.astype(jnp.bfloat16)
    new_cache = jnp.stack([keys_new.reshape(group_rows, lane_width), values_new], axis=1)
    capacity = max(2, (pages_per + req_count - 2) // (req_count - 1))
    page_ids = jnp.arange(pages_per, dtype=jnp.int32)
    earlier = page_ids[None, :] < page_ids[:, None]
    same_owner = page_owner[:, :, None] == page_owner[:, None, :]
    page_rank = jnp.sum((same_owner & earlier[None]).astype(jnp.int32), axis=2)
    owned_here = page_owner == req_index
    chosen = owned_here[:, None, :] & (
        page_rank[:, None, :] == jnp.arange(capacity, dtype=jnp.int32)[None, :, None]
    )
    slot_count = page_store.shape[0]
    send_pick = jnp.sum(
        (
            chosen[:, :, :, None]
            & (page_slot[:, None, :, None] == jnp.arange(slot_count, dtype=jnp.int32)[None, None, None, :])
        ).astype(jnp.int32),
        axis=2,
    ).astype(jnp.bfloat16)
    page_shape = page_store.shape[1:]
    page_size = math.prod(page_shape)
    outgoing_pages = jnp.dot(
        send_pick.reshape(req_count * capacity, slot_count),
        page_store.reshape(slot_count, page_size),
        preferred_element_type=jnp.bfloat16,
    ).reshape(req_count, capacity * page_size)
    out_flat = jnp.broadcast_to(out_block.reshape(1, -1), (req_count, out_block.size))
    arrived = lax.all_to_all(
        jnp.concatenate([outgoing_pages, out_flat], axis=1), "req", split_axis=0, concat_axis=0, tiled=True
    )
    server_out = (
        arrived[:, capacity * page_size :]
        .reshape((req_count,) + out_block.shape)
        .transpose(1, 0, 2)
        .reshape(out_block.shape[0], req_count * out_block.shape[1])
    )
    arrived_pages = arrived[:, : capacity * page_size].reshape(
        (req_count * capacity * page_rows,) + page_shape[1:]
    )
    own_count = jnp.sum(
        (page_owner[req_index][None, :] == jnp.arange(req_count, dtype=jnp.int32)[:, None]).astype(jnp.int32),
        axis=1,
    )
    slot_live = (jnp.arange(capacity, dtype=jnp.int32)[None, :] < own_count[:, None]).reshape(-1)
    key_live = jnp.repeat(slot_live, page_rows)
    context = arrived_pages.reshape(req_count * capacity * page_rows, 2, lane_heads, head_dim)
    score_scale = 1.0 / math.sqrt(head_dim)
    near_scores = (
        jnp.einsum("ihc,jhc->hij", query_rows, keys_new, preferred_element_type=jnp.float32)
        * score_scale
    )
    far_scores = (
        jnp.einsum("ihc,jhc->hij", query_rows, context[:, 0], preferred_element_type=jnp.float32)
        * score_scale
    )
    same_request = second[:, None] == second[None, :]
    near_weights = jnp.where(same_request[None], jnp.exp(near_scores), jnp.float32(0.0))
    far_weights = jnp.where(
        ((carried == 1)[:, None] & key_live[None, :])[None], jnp.exp(far_scores), jnp.float32(0.0)
    )
    totals = jnp.sum(near_weights, axis=2, keepdims=True) + jnp.sum(
        far_weights, axis=2, keepdims=True
    )
    near_probs = (near_weights / totals).astype(jnp.bfloat16)
    far_probs = (far_weights / totals).astype(jnp.bfloat16)
    attended = jnp.einsum(
        "hij,jhc->ihc",
        near_probs,
        values_new.reshape(group_rows, lane_heads, head_dim),
        preferred_element_type=jnp.float32,
    )
    attended = attended + jnp.einsum(
        "hij,jhc->ihc", far_probs, context[:, 1], preferred_element_type=jnp.float32
    )
    attended = attended.astype(jnp.bfloat16).reshape(group_rows, lane_width)
    shard_rows = routes.shape[0]
    row_start = lane_index * shard_rows
    head_terms = jnp.dot(attended, server_out, preferred_element_type=jnp.float32)
    server_gate_up, head_terms = lax.optimization_barrier((server_gate_up, head_terms))
    mixed_own = scatter_sum(head_terms, lax.axis_size("tp"))
    residual_own = lax.dynamic_slice_in_dim(tokens_f32, row_start, shard_rows, 0) + mixed_own
    moe_own = rms_scale(residual_own, moe_gain).astype(jnp.bfloat16)
    logits = jnp.dot(moe_own, router_weight, preferred_element_type=jnp.float32)
    exps = jnp.exp(logits)
    routed_exps = jnp.take_along_axis(exps, routes, axis=1)
    entry_gates = routed_exps / jnp.sum(routed_exps, axis=1, keepdims=True)
    top_count = routes.shape[1]
    slot_depth = 3 * shard_rows * top_count // (2 * expert_count)
    flat_routes = routes.reshape(-1)
    onehot = (flat_routes[:, None] == jnp.arange(expert_count, dtype=jnp.int32)[None, :]).astype(
        jnp.int32
    )
    entry_rank = jnp.sum((jnp.cumsum(onehot, axis=0) - onehot) * onehot, axis=1)
    entry_slot = (flat_routes * slot_depth + entry_rank).reshape(shard_rows, top_count)
    select_table = jnp.any(
        entry_slot[None, :, :]
        == jnp.arange(expert_count * slot_depth, dtype=jnp.int32)[:, None, None],
        axis=2,
    ).astype(jnp.bfloat16)
    outgoing_rows = jnp.dot(select_table, moe_own, preferred_element_type=jnp.float32).astype(
        jnp.bfloat16
    )
    send_rows = jnp.broadcast_to(
        outgoing_rows.reshape(expert_count, 1, slot_depth, model_width),
        (expert_count, 2, slot_depth, model_width),
    ).reshape(2 * expert_count, slot_depth, model_width)
    arrived_rows = lax.all_to_all(send_rows, ("req", "tp"), split_axis=0, concat_axis=0, tiled=True)
    flat_rows = arrived_rows.reshape(-1, model_width)
    both = jnp.dot(flat_rows, server_gate_up[0], preferred_element_type=jnp.float32)
    act = (jax.nn.silu(both[:, :half_units]) * both[:, half_units:]).astype(jnp.bfloat16)
    expert_rows = (
        jnp.dot(act, down_weight[0], preferred_element_type=jnp.float32)
        .astype(jnp.bfloat16)
        .reshape(arrived_rows.shape)
    )
    returned = lax.all_to_all(expert_rows, ("req", "tp"), split_axis=0, concat_axis=0, tiled=True)
    returned = returned.reshape(expert_count, 2, slot_depth, model_width)
    joined_out = (returned[:, 0].astype(jnp.float32) + returned[:, 1].astype(jnp.float32)).reshape(
        expert_count * slot_depth, model_width
    )
    picked_rows = jnp.take(joined_out, entry_slot.reshape(-1), axis=0).reshape(
        shard_rows, top_count, model_width
    )
    moe_out = jnp.sum(picked_rows * entry_gates[:, :, None], axis=1)
    hidden_rows = (residual_own + moe_out).astype(jnp.bfloat16)
    return (server_qkv, server_out, server_gate_up, hidden_rows, new_cache)


def solution(mesh):
    in_specs = (
        P("req", None),
        P(),
        P(),
        P(),
        P(),
        P("req", "tp"),
        P("req", "tp"),
        P("req", "tp"),
        P("tp", "req"),
        P(None, ("req", "tp"), None),
        P(None, ("req", "tp"), None),
        P(("req", "tp"), None, None),
        P(),
        P("req", None, None, "tp"),
        P(),
        P(),
        P(),
        P(),
        P(("req", "tp"), None),
    )
    out_specs = (
        P(None, "tp"),
        P("tp", None),
        P(("req", "tp"), None, None),
        P(("req", "tp"), None),
        P("req", None, "tp"),
    )
    return jax.shard_map(body, mesh=mesh, in_specs=in_specs, out_specs=out_specs, check_vma=False)
```

```python
import functools
import math

import jax
import jax.numpy as jnp
from jax import lax
from jax.experimental import pallas as pl
from jax.experimental.pallas import tpu as pltpu
from jax.sharding import PartitionSpec as P

MESH = pl.DeviceIdType.MESH

norm_eps = 1e-06
rope_base = 50000.0


def rms_scale(values, gain_vec):
    return (
        values * lax.rsqrt(jnp.mean(values * values, axis=-1, keepdims=True) + norm_eps) * gain_vec
    )


def rotate_half(values, cosine, sine_part):
    half_width = values.shape[-1] // 2
    first_half = values[..., :half_width]
    second_half = values[..., half_width:]
    return jnp.concatenate(
        [
            first_half * cosine - second_half * sine_part,
            second_half * cosine + first_half * sine_part,
        ],
        axis=-1,
    )


def split_halves(weights):
    expert_count, rows_here, hidden_units = weights.shape
    return weights.reshape(expert_count, rows_here, 2, hidden_units // 2).transpose(0, 2, 1, 3)


def scatter_sum_kernel(parts, x_ref, out_ref, held, send_sem, recv_sem):
    me = lax.axis_index("tp")
    group = lax.axis_index("req")
    rows = out_ref.shape[0]
    barrier = pltpu.get_barrier_semaphore()
    for step in range(1, parts):
        peer = lax.rem(me + step, parts)
        pl.semaphore_signal(barrier, inc=1, device_id=(group, peer), device_id_type=MESH)
    pl.semaphore_wait(barrier, parts - 1)

    def outgoing(peer):
        return pltpu.make_async_remote_copy(
            src_ref=x_ref.at[pl.ds(pl.multiple_of(peer * rows, rows), rows)],
            dst_ref=held.at[me],
            send_sem=send_sem.at[peer],
            recv_sem=recv_sem.at[me],
            device_id=(group, peer),
            device_id_type=MESH,
        )

    def incoming(peer):
        return pltpu.make_async_remote_copy(
            src_ref=x_ref.at[pl.ds(pl.multiple_of(me * rows, rows), rows)],
            dst_ref=held.at[peer],
            send_sem=send_sem.at[peer],
            recv_sem=recv_sem.at[peer],
            device_id=(group, peer),
            device_id_type=MESH,
        )

    for step in range(1, parts):
        outgoing(lax.rem(me + step, parts)).start()
    total = x_ref[pl.ds(pl.multiple_of(me * rows, rows), rows), :]
    for step in range(1, parts):
        peer = lax.rem(me + parts - step, parts)
        incoming(peer).wait_recv()
        total = total + held[peer]
    for step in range(1, parts):
        outgoing(lax.rem(me + step, parts)).wait_send()
    out_ref[...] = total


def scatter_sum(x, parts):
    rows = x.shape[0] // parts
    return pl.pallas_call(
        functools.partial(scatter_sum_kernel, parts),
        out_shape=jax.ShapeDtypeStruct((rows, x.shape[1]), x.dtype),
        in_specs=[pl.BlockSpec(memory_space=pltpu.VMEM)],
        out_specs=pl.BlockSpec(memory_space=pltpu.VMEM),
        scratch_shapes=[
            pltpu.VMEM((parts, rows, x.shape[1]), x.dtype),
            pltpu.SemaphoreType.DMA((parts,)),
            pltpu.SemaphoreType.DMA((parts,)),
        ],
        compiler_params=pltpu.CompilerParams(collective_id=0, has_side_effects=True),
    )(x)


def body(
    tokens,
    attn_gain,
    query_gain,
    key_gain,
    moe_gain,
    query_weight,
    key_weight,
    value_weight,
    out_weight,
    gate_weight,
    up_weight,
    down_weight,
    router_weight,
    page_store,
    prompt_lengths,
    continues,
    page_owner,
    page_slot,
    routes,
):
    req_count = lax.axis_size("req")
    req_index = lax.axis_index("req")
    lane_index = lax.axis_index("tp")
    joined_local = jnp.concatenate(
        [
            query_weight.astype(jnp.bfloat16),
            key_weight.astype(jnp.bfloat16),
            value_weight.astype(jnp.bfloat16),
        ],
        axis=1,
    )
    server_qkv = lax.all_gather(joined_local, "req", axis=0, tiled=True)
    out_block = out_weight.astype(jnp.bfloat16)
    expert_count, rows_here, hidden_units = gate_weight.shape
    half_units = hidden_units // 2
    packed = jnp.concatenate(
        [
            split_halves(gate_weight.astype(jnp.bfloat16)),
            split_halves(up_weight.astype(jnp.bfloat16)),
        ],
        axis=3,
    ).reshape(2 * expert_count, rows_here, hidden_units)
    server_gate_up = lax.all_to_all(packed, ("req", "tp"), split_axis=0, concat_axis=1, tiled=True)
    group_rows, model_width = tokens.shape
    tokens_f32 = tokens.astype(jnp.float32)
    normed = rms_scale(tokens_f32, attn_gain).astype(jnp.bfloat16)
    projected = jnp.dot(normed, server_qkv, preferred_element_type=jnp.float32)
    head_dim = query_gain.shape[0]
    lane_width = server_qkv.shape[1] // 3
    lane_heads = lane_width // head_dim
    query_raw = projected[:, :lane_width].reshape(group_rows, lane_heads, head_dim)
    key_raw = projected[:, lane_width : 2 * lane_width].reshape(group_rows, lane_heads, head_dim)
    value_raw = projected[:, 2 * lane_width :]
    first_length = lax.dynamic_index_in_dim(prompt_lengths, 2 * req_index, 0, keepdims=False)
    carry_flags = lax.dynamic_slice_in_dim(continues, 2 * req_index, 2)
    row_ids = jnp.arange(group_rows, dtype=jnp.int32)
    second = (row_ids >= first_length).astype(jnp.int32)
    within = row_ids - second * first_length
    carried = jnp.where(second == 1, carry_flags[1], carry_flags[0])
    pages_per = page_owner.shape[1]
    page_rows = page_store.shape[1]
    context_len = pages_per * page_rows
    position = (within + context_len * carried).astype(jnp.float32)
    inverse = jnp.power(
        jnp.float32(rope_base), -(jnp.arange(head_dim // 2, dtype=jnp.float32) * 2.0 / head_dim)
    )
    angles = position[:, None, None] * inverse[None, None, :]
    cosine = jnp.cos(angles)
    sine_part = jnp.sin(angles)
    query_rows = rotate_half(rms_scale(query_raw, query_gain), cosine, sine_part).astype(
        jnp.bfloat16
    )
    keys_new = rotate_half(rms_scale(key_raw, key_gain), cosine, sine_part).astype(jnp.bfloat16)
    values_new = value_raw.astype(jnp.bfloat16)
    new_cache = jnp.stack([keys_new.reshape(group_rows, lane_width), values_new], axis=1)
    capacity = max(2, (pages_per + req_count - 2) // (req_count - 1))
    page_ids = jnp.arange(pages_per, dtype=jnp.int32)
    earlier = page_ids[None, :] < page_ids[:, None]
    same_owner = page_owner[:, :, None] == page_owner[:, None, :]
    page_rank = jnp.sum((same_owner & earlier[None]).astype(jnp.int32), axis=2)
    owned_here = page_owner == req_index
    chosen = owned_here[:, None, :] & (
        page_rank[:, None, :] == jnp.arange(capacity, dtype=jnp.int32)[None, :, None]
    )
    send_slot = jnp.sum(jnp.where(chosen, page_slot[:, None, :], 0), axis=2)
    send_live = jnp.any(chosen, axis=2)
    page_shape = page_store.shape[1:]
    outgoing_pages = jnp.take(page_store, send_slot.reshape(-1), axis=0).reshape(
        (req_count, capacity) + page_shape
    )
    outgoing_pages = jnp.where(
        send_live[:, :, None, None, None], outgoing_pages, jnp.zeros_like(outgoing_pages)
    )
    out_pair = out_block.reshape(page_shape[0], page_shape[2])
    out_slot = jnp.stack([out_pair, jnp.zeros_like(out_pair)], axis=1)
    outgoing_all = jnp.concatenate(
        [outgoing_pages, jnp.broadcast_to(out_slot[None, None], (req_count, 1) + page_shape)], axis=1
    )
    arrived_all = lax.all_to_all(outgoing_all, "req", split_axis=0, concat_axis=0, tiled=True)
    arrived_pages = arrived_all[:, :capacity]
    server_out = (
        arrived_all[:, capacity, :, 0, :]
        .reshape((req_count,) + out_block.shape)
        .transpose(1, 0, 2)
        .reshape(out_block.shape[0], req_count * out_block.shape[1])
    )
    own_owner = jnp.take(page_owner, req_index, axis=0)
    own_rank = jnp.take(page_rank, req_index, axis=0)
    context = jnp.take(
        arrived_pages.reshape((req_count * capacity,) + page_shape),
        own_owner * capacity + own_rank,
        axis=0,
    )
    context = context.reshape(context_len, 2, lane_heads, head_dim)
    score_scale = 1.0 / math.sqrt(head_dim)
    near_scores = (
        jnp.einsum("ihc,jhc->hij", query_rows, keys_new, preferred_element_type=jnp.float32)
        * score_scale
    )
    far_scores = (
        jnp.einsum("ihc,jhc->hij", query_rows, context[:, 0], preferred_element_type=jnp.float32)
        * score_scale
    )
    same_request = second[:, None] == second[None, :]
    near_weights = jnp.where(same_request[None], jnp.exp(near_scores), jnp.float32(0.0))
    far_weights = jnp.where((carried == 1)[None, :, None], jnp.exp(far_scores), jnp.float32(0.0))
    totals = jnp.sum(near_weights, axis=2, keepdims=True) + jnp.sum(
        far_weights, axis=2, keepdims=True
    )
    near_probs = (near_weights / totals).astype(jnp.bfloat16)
    far_probs = (far_weights / totals).astype(jnp.bfloat16)
    attended = jnp.einsum(
        "hij,jhc->ihc",
        near_probs,
        values_new.reshape(group_rows, lane_heads, head_dim),
        preferred_element_type=jnp.float32,
    )
    attended = attended + jnp.einsum(
        "hij,jhc->ihc", far_probs, context[:, 1], preferred_element_type=jnp.float32
    )
    attended = attended.astype(jnp.bfloat16).reshape(group_rows, lane_width)
    shard_rows = routes.shape[0]
    row_start = lane_index * shard_rows
    head_terms = jnp.dot(attended, server_out, preferred_element_type=jnp.float32)
    server_gate_up, head_terms = lax.optimization_barrier((server_gate_up, head_terms))
    mixed_own = scatter_sum(head_terms, lax.axis_size("tp"))
    residual_own = lax.dynamic_slice_in_dim(tokens_f32, row_start, shard_rows, 0) + mixed_own
    moe_own = rms_scale(residual_own, moe_gain).astype(jnp.bfloat16)
    logits = jnp.dot(moe_own, router_weight, preferred_element_type=jnp.float32)
    exps = jnp.exp(logits)
    routed_exps = jnp.take_along_axis(exps, routes, axis=1)
    entry_gates = routed_exps / jnp.sum(routed_exps, axis=1, keepdims=True)
    top_count = routes.shape[1]
    slot_depth = 3 * shard_rows * top_count // (2 * expert_count)
    flat_routes = routes.reshape(-1)
    onehot = (flat_routes[:, None] == jnp.arange(expert_count, dtype=jnp.int32)[None, :]).astype(
        jnp.int32
    )
    entry_rank = jnp.sum((jnp.cumsum(onehot, axis=0) - onehot) * onehot, axis=1)
    entry_slot = (flat_routes * slot_depth + entry_rank).reshape(shard_rows, top_count)
    select_table = jnp.any(
        entry_slot[None, :, :]
        == jnp.arange(expert_count * slot_depth, dtype=jnp.int32)[:, None, None],
        axis=2,
    ).astype(jnp.bfloat16)
    outgoing_rows = jnp.dot(select_table, moe_own, preferred_element_type=jnp.float32).astype(
        jnp.bfloat16
    )
    send_rows = jnp.broadcast_to(
        outgoing_rows.reshape(expert_count, 1, slot_depth, model_width),
        (expert_count, 2, slot_depth, model_width),
    ).reshape(2 * expert_count, slot_depth, model_width)
    arrived_rows = lax.all_to_all(send_rows, ("req", "tp"), split_axis=0, concat_axis=0, tiled=True)
    flat_rows = arrived_rows.reshape(-1, model_width)
    both = jnp.dot(flat_rows, server_gate_up[0], preferred_element_type=jnp.float32)
    act = (jax.nn.silu(both[:, :half_units]) * both[:, half_units:]).astype(jnp.bfloat16)
    expert_rows = (
        jnp.dot(act, down_weight[0], preferred_element_type=jnp.float32)
        .astype(jnp.bfloat16)
        .reshape(arrived_rows.shape)
    )
    returned = lax.all_to_all(expert_rows, ("req", "tp"), split_axis=0, concat_axis=0, tiled=True)
    returned = returned.reshape(expert_count, 2, slot_depth, model_width)
    joined_out = (returned[:, 0].astype(jnp.float32) + returned[:, 1].astype(jnp.float32)).reshape(
        expert_count * slot_depth, model_width
    )
    picked_rows = jnp.take(joined_out, entry_slot.reshape(-1), axis=0).reshape(
        shard_rows, top_count, model_width
    )
    moe_out = jnp.sum(picked_rows * entry_gates[:, :, None], axis=1)
    hidden_rows = (residual_own + moe_out).astype(jnp.bfloat16)
    return (server_qkv, server_out, server_gate_up, hidden_rows, new_cache)


def solution(mesh):
    in_specs = (
        P("req", None),
        P(),
        P(),
        P(),
        P(),
        P("req", "tp"),
        P("req", "tp"),
        P("req", "tp"),
        P("tp", "req"),
        P(None, ("req", "tp"), None),
        P(None, ("req", "tp"), None),
        P(("req", "tp"), None, None),
        P(),
        P("req", None, None, "tp"),
        P(),
        P(),
        P(),
        P(),
        P(("req", "tp"), None),
    )
    out_specs = (
        P(None, "tp"),
        P("tp", None),
        P(("req", "tp"), None, None),
        P(("req", "tp"), None),
        P("req", None, "tp"),
    )
    return jax.shard_map(body, mesh=mesh, in_specs=in_specs, out_specs=out_specs, check_vma=False)
```

```python
import functools
import math

import jax
import jax.numpy as jnp
from jax import lax
from jax.experimental import pallas as pl
from jax.experimental.pallas import tpu as pltpu
from jax.sharding import PartitionSpec as P

MESH = pl.DeviceIdType.MESH

norm_eps = 1e-06
rope_base = 50000.0


def rms_scale(values, gain_vec):
    return (
        values * lax.rsqrt(jnp.mean(values * values, axis=-1, keepdims=True) + norm_eps) * gain_vec
    )


def rotate_half(values, cosine, sine_part):
    half_width = values.shape[-1] // 2
    first_half = values[..., :half_width]
    second_half = values[..., half_width:]
    return jnp.concatenate(
        [
            first_half * cosine - second_half * sine_part,
            second_half * cosine + first_half * sine_part,
        ],
        axis=-1,
    )


def split_halves(weights):
    expert_count, rows_here, hidden_units = weights.shape
    return weights.reshape(expert_count, rows_here, 2, hidden_units // 2).transpose(0, 2, 1, 3)


def scatter_sum_kernel(parts, x_ref, out_ref, held, send_sem, recv_sem):
    me = lax.axis_index("tp")
    group = lax.axis_index("req")
    rows = out_ref.shape[0]
    barrier = pltpu.get_barrier_semaphore()
    for step in range(1, parts):
        peer = lax.rem(me + step, parts)
        pl.semaphore_signal(barrier, inc=1, device_id=(group, peer), device_id_type=MESH)
    pl.semaphore_wait(barrier, parts - 1)

    def outgoing(peer):
        return pltpu.make_async_remote_copy(
            src_ref=x_ref.at[pl.ds(pl.multiple_of(peer * rows, rows), rows)],
            dst_ref=held.at[me],
            send_sem=send_sem.at[peer],
            recv_sem=recv_sem.at[me],
            device_id=(group, peer),
            device_id_type=MESH,
        )

    def incoming(peer):
        return pltpu.make_async_remote_copy(
            src_ref=x_ref.at[pl.ds(pl.multiple_of(me * rows, rows), rows)],
            dst_ref=held.at[peer],
            send_sem=send_sem.at[peer],
            recv_sem=recv_sem.at[peer],
            device_id=(group, peer),
            device_id_type=MESH,
        )

    for step in range(1, parts):
        outgoing(lax.rem(me + step, parts)).start()
    total = x_ref[pl.ds(pl.multiple_of(me * rows, rows), rows), :]
    for step in range(1, parts):
        peer = lax.rem(me + parts - step, parts)
        incoming(peer).wait_recv()
        total = total + held[peer]
    for step in range(1, parts):
        outgoing(lax.rem(me + step, parts)).wait_send()
    out_ref[...] = total


def scatter_sum(x, parts):
    rows = x.shape[0] // parts
    return pl.pallas_call(
        functools.partial(scatter_sum_kernel, parts),
        out_shape=jax.ShapeDtypeStruct((rows, x.shape[1]), x.dtype),
        in_specs=[pl.BlockSpec(memory_space=pltpu.VMEM)],
        out_specs=pl.BlockSpec(memory_space=pltpu.VMEM),
        scratch_shapes=[
            pltpu.VMEM((parts, rows, x.shape[1]), x.dtype),
            pltpu.SemaphoreType.DMA((parts,)),
            pltpu.SemaphoreType.DMA((parts,)),
        ],
        compiler_params=pltpu.CompilerParams(collective_id=0, has_side_effects=True),
    )(x)


def body(
    tokens,
    attn_gain,
    query_gain,
    key_gain,
    moe_gain,
    query_weight,
    key_weight,
    value_weight,
    out_weight,
    gate_weight,
    up_weight,
    down_weight,
    router_weight,
    page_store,
    prompt_lengths,
    continues,
    page_owner,
    page_slot,
    routes,
):
    req_count = lax.axis_size("req")
    req_index = lax.axis_index("req")
    lane_index = lax.axis_index("tp")
    joined_local = jnp.concatenate(
        [
            query_weight.astype(jnp.bfloat16),
            key_weight.astype(jnp.bfloat16),
            value_weight.astype(jnp.bfloat16),
        ],
        axis=1,
    )
    server_qkv, server_out = (
        lax.all_gather(joined_local, "req", axis=0, tiled=True),
        lax.all_gather(out_weight.astype(jnp.bfloat16), "req", axis=1, tiled=True),
    )
    expert_count, rows_here, hidden_units = gate_weight.shape
    half_units = hidden_units // 2
    packed = jnp.concatenate(
        [
            split_halves(gate_weight.astype(jnp.bfloat16)),
            split_halves(up_weight.astype(jnp.bfloat16)),
        ],
        axis=3,
    ).reshape(2 * expert_count, rows_here, hidden_units)
    server_gate_up = lax.all_to_all(packed, ("req", "tp"), split_axis=0, concat_axis=1, tiled=True)
    group_rows, model_width = tokens.shape
    tokens_f32 = tokens.astype(jnp.float32)
    normed = rms_scale(tokens_f32, attn_gain).astype(jnp.bfloat16)
    projected = jnp.dot(normed, server_qkv, preferred_element_type=jnp.float32)
    head_dim = query_gain.shape[0]
    lane_width = server_qkv.shape[1] // 3
    lane_heads = lane_width // head_dim
    query_raw = projected[:, :lane_width].reshape(group_rows, lane_heads, head_dim)
    key_raw = projected[:, lane_width : 2 * lane_width].reshape(group_rows, lane_heads, head_dim)
    value_raw = projected[:, 2 * lane_width :]
    first_length = lax.dynamic_index_in_dim(prompt_lengths, 2 * req_index, 0, keepdims=False)
    carry_flags = lax.dynamic_slice_in_dim(continues, 2 * req_index, 2)
    row_ids = jnp.arange(group_rows, dtype=jnp.int32)
    second = (row_ids >= first_length).astype(jnp.int32)
    within = row_ids - second * first_length
    carried = jnp.where(second == 1, carry_flags[1], carry_flags[0])
    pages_per = page_owner.shape[1]
    page_rows = page_store.shape[1]
    context_len = pages_per * page_rows
    position = (within + context_len * carried).astype(jnp.float32)
    inverse = jnp.power(
        jnp.float32(rope_base), -(jnp.arange(head_dim // 2, dtype=jnp.float32) * 2.0 / head_dim)
    )
    angles = position[:, None, None] * inverse[None, None, :]
    cosine = jnp.cos(angles)
    sine_part = jnp.sin(angles)
    query_rows = rotate_half(rms_scale(query_raw, query_gain), cosine, sine_part).astype(
        jnp.bfloat16
    )
    keys_new = rotate_half(rms_scale(key_raw, key_gain), cosine, sine_part).astype(jnp.bfloat16)
    values_new = value_raw.astype(jnp.bfloat16)
    new_cache = jnp.stack([keys_new.reshape(group_rows, lane_width), values_new], axis=1)
    capacity = max(2, (pages_per + req_count - 2) // (req_count - 1))
    page_ids = jnp.arange(pages_per, dtype=jnp.int32)
    earlier = page_ids[None, :] < page_ids[:, None]
    same_owner = page_owner[:, :, None] == page_owner[:, None, :]
    page_rank = jnp.sum((same_owner & earlier[None]).astype(jnp.int32), axis=2)
    owned_here = page_owner == req_index
    chosen = owned_here[:, None, :] & (
        page_rank[:, None, :] == jnp.arange(capacity, dtype=jnp.int32)[None, :, None]
    )
    send_slot = jnp.sum(jnp.where(chosen, page_slot[:, None, :], 0), axis=2)
    page_shape = page_store.shape[1:]
    outgoing_pages = jnp.take(page_store, send_slot.reshape(-1), axis=0).reshape(
        (req_count, capacity) + page_shape
    )
    arrived_pages = lax.all_to_all(outgoing_pages, "req", split_axis=0, concat_axis=0, tiled=True)
    own_owner = jnp.take(page_owner, req_index, axis=0)
    own_rank = jnp.take(page_rank, req_index, axis=0)
    context = jnp.take(
        arrived_pages.reshape((req_count * capacity,) + page_shape),
        own_owner * capacity + own_rank,
        axis=0,
    )
    context = context.reshape(context_len, 2, lane_heads, head_dim)
    score_scale = 1.0 / math.sqrt(head_dim)
    near_scores = (
        jnp.einsum("ihc,jhc->hij", query_rows, keys_new, preferred_element_type=jnp.float32)
        * score_scale
    )
    far_scores = (
        jnp.einsum("ihc,jhc->hij", query_rows, context[:, 0], preferred_element_type=jnp.float32)
        * score_scale
    )
    same_request = second[:, None] == second[None, :]
    near_weights = jnp.where(same_request[None], jnp.exp(near_scores), jnp.float32(0.0))
    far_weights = jnp.where((carried == 1)[None, :, None], jnp.exp(far_scores), jnp.float32(0.0))
    totals = jnp.sum(near_weights, axis=2, keepdims=True) + jnp.sum(
        far_weights, axis=2, keepdims=True
    )
    near_probs = (near_weights / totals).astype(jnp.bfloat16)
    far_probs = (far_weights / totals).astype(jnp.bfloat16)
    attended = jnp.einsum(
        "hij,jhc->ihc",
        near_probs,
        values_new.reshape(group_rows, lane_heads, head_dim),
        preferred_element_type=jnp.float32,
    )
    attended = attended + jnp.einsum(
        "hij,jhc->ihc", far_probs, context[:, 1], preferred_element_type=jnp.float32
    )
    attended = attended.astype(jnp.bfloat16).reshape(group_rows, lane_width)
    shard_rows = routes.shape[0]
    row_start = lane_index * shard_rows
    head_terms = jnp.dot(attended, server_out, preferred_element_type=jnp.float32)
    server_gate_up, head_terms = lax.optimization_barrier((server_gate_up, head_terms))
    mixed_own = scatter_sum(head_terms, lax.axis_size("tp"))
    residual_own = lax.dynamic_slice_in_dim(tokens_f32, row_start, shard_rows, 0) + mixed_own
    moe_own = rms_scale(residual_own, moe_gain).astype(jnp.bfloat16)
    logits = jnp.dot(moe_own, router_weight, preferred_element_type=jnp.float32)
    exps = jnp.exp(logits)
    routed_exps = jnp.take_along_axis(exps, routes, axis=1)
    entry_gates = routed_exps / jnp.sum(routed_exps, axis=1, keepdims=True)
    top_count = routes.shape[1]
    slot_depth = 3 * shard_rows * top_count // (2 * expert_count)
    flat_routes = routes.reshape(-1)
    onehot = (flat_routes[:, None] == jnp.arange(expert_count, dtype=jnp.int32)[None, :]).astype(
        jnp.int32
    )
    entry_rank = jnp.sum((jnp.cumsum(onehot, axis=0) - onehot) * onehot, axis=1)
    entry_slot = (flat_routes * slot_depth + entry_rank).reshape(shard_rows, top_count)
    select_table = jnp.any(
        entry_slot[None, :, :]
        == jnp.arange(expert_count * slot_depth, dtype=jnp.int32)[:, None, None],
        axis=2,
    ).astype(jnp.bfloat16)
    outgoing_rows = jnp.dot(select_table, moe_own, preferred_element_type=jnp.float32).astype(
        jnp.bfloat16
    )
    send_rows = jnp.broadcast_to(
        outgoing_rows.reshape(expert_count, 1, slot_depth, model_width),
        (expert_count, 2, slot_depth, model_width),
    ).reshape(2 * expert_count, slot_depth, model_width)
    arrived_rows = lax.all_to_all(send_rows, ("req", "tp"), split_axis=0, concat_axis=0, tiled=True)
    flat_rows = arrived_rows.reshape(-1, model_width)
    both = jnp.dot(flat_rows, server_gate_up[0], preferred_element_type=jnp.float32)
    act = (jax.nn.silu(both[:, :half_units]) * both[:, half_units:]).astype(jnp.bfloat16)
    expert_rows = (
        jnp.dot(act, down_weight[0], preferred_element_type=jnp.float32)
        .astype(jnp.bfloat16)
        .reshape(arrived_rows.shape)
    )
    returned = lax.all_to_all(expert_rows, ("req", "tp"), split_axis=0, concat_axis=0, tiled=True)
    returned = returned.reshape(expert_count, 2, slot_depth, model_width)
    joined_out = (returned[:, 0].astype(jnp.float32) + returned[:, 1].astype(jnp.float32)).reshape(
        expert_count * slot_depth, model_width
    )
    picked_rows = jnp.take(joined_out, entry_slot.reshape(-1), axis=0).reshape(
        shard_rows, top_count, model_width
    )
    moe_out = jnp.sum(picked_rows * entry_gates[:, :, None], axis=1)
    hidden_rows = (residual_own + moe_out).astype(jnp.bfloat16)
    return (server_qkv, server_out, server_gate_up, hidden_rows, new_cache)


def solution(mesh):
    in_specs = (
        P("req", None),
        P(),
        P(),
        P(),
        P(),
        P("req", "tp"),
        P("req", "tp"),
        P("req", "tp"),
        P("tp", "req"),
        P(None, ("req", "tp"), None),
        P(None, ("req", "tp"), None),
        P(("req", "tp"), None, None),
        P(),
        P("req", None, None, "tp"),
        P(),
        P(),
        P(),
        P(),
        P(("req", "tp"), None),
    )
    out_specs = (
        P(None, "tp"),
        P("tp", None),
        P(("req", "tp"), None, None),
        P(("req", "tp"), None),
        P("req", None, "tp"),
    )
    return jax.shard_map(body, mesh=mesh, in_specs=in_specs, out_specs=out_specs, check_vma=False)
```

```python
import functools
import math

import jax
import jax.numpy as jnp
from jax import lax
from jax.experimental import pallas as pl
from jax.experimental.pallas import tpu as pltpu
from jax.sharding import PartitionSpec as P

MESH = pl.DeviceIdType.MESH

norm_eps = 1e-06
rope_base = 50000.0


def rms_scale(values, gain_vec):
    return (
        values * lax.rsqrt(jnp.mean(values * values, axis=-1, keepdims=True) + norm_eps) * gain_vec
    )


def rotate_half(values, cosine, sine_part):
    half_width = values.shape[-1] // 2
    first_half = values[..., :half_width]
    second_half = values[..., half_width:]
    return jnp.concatenate(
        [
            first_half * cosine - second_half * sine_part,
            second_half * cosine + first_half * sine_part,
        ],
        axis=-1,
    )


def split_halves(weights):
    expert_count, rows_here, hidden_units = weights.shape
    return weights.reshape(expert_count, rows_here, 2, hidden_units // 2).transpose(0, 2, 1, 3)


def scatter_sum_kernel(parts, x_ref, out_ref, held, send_sem, recv_sem):
    me = lax.axis_index("tp")
    group = lax.axis_index("req")
    rows = out_ref.shape[0]
    barrier = pltpu.get_barrier_semaphore()
    for step in range(1, parts):
        peer = lax.rem(me + step, parts)
        pl.semaphore_signal(barrier, inc=1, device_id=(group, peer), device_id_type=MESH)
    pl.semaphore_wait(barrier, parts - 1)

    def outgoing(peer):
        return pltpu.make_async_remote_copy(
            src_ref=x_ref.at[pl.ds(pl.multiple_of(peer * rows, rows), rows)],
            dst_ref=held.at[me],
            send_sem=send_sem.at[peer],
            recv_sem=recv_sem.at[me],
            device_id=(group, peer),
            device_id_type=MESH,
        )

    def incoming(peer):
        return pltpu.make_async_remote_copy(
            src_ref=x_ref.at[pl.ds(pl.multiple_of(me * rows, rows), rows)],
            dst_ref=held.at[peer],
            send_sem=send_sem.at[peer],
            recv_sem=recv_sem.at[peer],
            device_id=(group, peer),
            device_id_type=MESH,
        )

    for step in range(1, parts):
        outgoing(lax.rem(me + step, parts)).start()
    total = x_ref[pl.ds(pl.multiple_of(me * rows, rows), rows), :]
    for step in range(1, parts):
        peer = lax.rem(me + parts - step, parts)
        incoming(peer).wait_recv()
        total = total + held[peer]
    for step in range(1, parts):
        outgoing(lax.rem(me + step, parts)).wait_send()
    out_ref[...] = total


def scatter_sum(x, parts):
    rows = x.shape[0] // parts
    return pl.pallas_call(
        functools.partial(scatter_sum_kernel, parts),
        out_shape=jax.ShapeDtypeStruct((rows, x.shape[1]), x.dtype),
        in_specs=[pl.BlockSpec(memory_space=pltpu.VMEM)],
        out_specs=pl.BlockSpec(memory_space=pltpu.VMEM),
        scratch_shapes=[
            pltpu.VMEM((parts, rows, x.shape[1]), x.dtype),
            pltpu.SemaphoreType.DMA((parts,)),
            pltpu.SemaphoreType.DMA((parts,)),
        ],
        compiler_params=pltpu.CompilerParams(collective_id=0, has_side_effects=True),
    )(x)


def gather_kernel(count, x_ref, out_ref, held, send_sem, recv_sem):
    me = lax.axis_index("req")
    lane = lax.axis_index("tp")
    width = x_ref.shape[1]
    barrier = pltpu.get_barrier_semaphore()
    for step in range(1, count):
        peer = lax.rem(me + step, count)
        pl.semaphore_signal(barrier, inc=1, device_id=(peer, lane), device_id_type=MESH)
    pl.semaphore_wait(barrier, count - 1)

    def transfer(peer, slot):
        return pltpu.make_async_remote_copy(
            src_ref=x_ref,
            dst_ref=held.at[slot],
            send_sem=send_sem.at[peer],
            recv_sem=recv_sem.at[slot],
            device_id=(peer, lane),
            device_id_type=MESH,
        )

    for step in range(1, count):
        peer = lax.rem(me + step, count)
        transfer(peer, me).start()
    held[me] = x_ref[...]
    for step in range(1, count):
        peer = lax.rem(me + count - step, count)
        transfer(peer, peer).wait_recv()
    for step in range(1, count):
        peer = lax.rem(me + step, count)
        transfer(peer, me).wait_send()
    for slot in range(count):
        out_ref[:, slot * width : (slot + 1) * width] = held[slot]


def gather_columns(x, count):
    return pl.pallas_call(
        functools.partial(gather_kernel, count),
        out_shape=jax.ShapeDtypeStruct((x.shape[0], count * x.shape[1]), x.dtype),
        in_specs=[pl.BlockSpec(memory_space=pltpu.VMEM)],
        out_specs=pl.BlockSpec(memory_space=pltpu.VMEM),
        scratch_shapes=[
            pltpu.VMEM((count,) + x.shape, x.dtype),
            pltpu.SemaphoreType.DMA((count,)),
            pltpu.SemaphoreType.DMA((count,)),
        ],
        compiler_params=pltpu.CompilerParams(collective_id=3, has_side_effects=True),
    )(x)


def body(
    tokens,
    attn_gain,
    query_gain,
    key_gain,
    moe_gain,
    query_weight,
    key_weight,
    value_weight,
    out_weight,
    gate_weight,
    up_weight,
    down_weight,
    router_weight,
    page_store,
    prompt_lengths,
    continues,
    page_owner,
    page_slot,
    routes,
):
    req_count = lax.axis_size("req")
    req_index = lax.axis_index("req")
    lane_index = lax.axis_index("tp")
    joined_local = jnp.concatenate(
        [
            query_weight.astype(jnp.bfloat16),
            key_weight.astype(jnp.bfloat16),
            value_weight.astype(jnp.bfloat16),
        ],
        axis=1,
    )
    server_qkv = lax.all_gather(joined_local, "req", axis=0, tiled=True)
    server_out = gather_columns(out_weight.astype(jnp.bfloat16), req_count)
    expert_count, rows_here, hidden_units = gate_weight.shape
    half_units = hidden_units // 2
    packed = jnp.concatenate(
        [
            split_halves(gate_weight.astype(jnp.bfloat16)),
            split_halves(up_weight.astype(jnp.bfloat16)),
        ],
        axis=3,
    ).reshape(2 * expert_count, rows_here, hidden_units)
    packed, server_out = lax.optimization_barrier((packed, server_out))
    server_gate_up = lax.all_to_all(packed, ("req", "tp"), split_axis=0, concat_axis=1, tiled=True)
    group_rows, model_width = tokens.shape
    tokens_f32 = tokens.astype(jnp.float32)
    normed = rms_scale(tokens_f32, attn_gain).astype(jnp.bfloat16)
    projected = jnp.dot(normed, server_qkv, preferred_element_type=jnp.float32)
    head_dim = query_gain.shape[0]
    lane_width = server_qkv.shape[1] // 3
    lane_heads = lane_width // head_dim
    query_raw = projected[:, :lane_width].reshape(group_rows, lane_heads, head_dim)
    key_raw = projected[:, lane_width : 2 * lane_width].reshape(group_rows, lane_heads, head_dim)
    value_raw = projected[:, 2 * lane_width :]
    first_length = lax.dynamic_index_in_dim(prompt_lengths, 2 * req_index, 0, keepdims=False)
    carry_flags = lax.dynamic_slice_in_dim(continues, 2 * req_index, 2)
    row_ids = jnp.arange(group_rows, dtype=jnp.int32)
    second = (row_ids >= first_length).astype(jnp.int32)
    within = row_ids - second * first_length
    carried = jnp.where(second == 1, carry_flags[1], carry_flags[0])
    pages_per = page_owner.shape[1]
    page_rows = page_store.shape[1]
    context_len = pages_per * page_rows
    position = (within + context_len * carried).astype(jnp.float32)
    inverse = jnp.power(
        jnp.float32(rope_base), -(jnp.arange(head_dim // 2, dtype=jnp.float32) * 2.0 / head_dim)
    )
    angles = position[:, None, None] * inverse[None, None, :]
    cosine = jnp.cos(angles)
    sine_part = jnp.sin(angles)
    query_rows = rotate_half(rms_scale(query_raw, query_gain), cosine, sine_part).astype(
        jnp.bfloat16
    )
    keys_new = rotate_half(rms_scale(key_raw, key_gain), cosine, sine_part).astype(jnp.bfloat16)
    values_new = value_raw.astype(jnp.bfloat16)
    new_cache = jnp.stack([keys_new.reshape(group_rows, lane_width), values_new], axis=1)
    capacity = max(2, (pages_per + req_count - 2) // (req_count - 1))
    page_ids = jnp.arange(pages_per, dtype=jnp.int32)
    earlier = page_ids[None, :] < page_ids[:, None]
    same_owner = page_owner[:, :, None] == page_owner[:, None, :]
    page_rank = jnp.sum((same_owner & earlier[None]).astype(jnp.int32), axis=2)
    owned_here = page_owner == req_index
    chosen = owned_here[:, None, :] & (
        page_rank[:, None, :] == jnp.arange(capacity, dtype=jnp.int32)[None, :, None]
    )
    send_slot = jnp.sum(jnp.where(chosen, page_slot[:, None, :], 0), axis=2)
    page_shape = page_store.shape[1:]
    outgoing_pages = jnp.take(page_store, send_slot.reshape(-1), axis=0).reshape(
        (req_count, capacity) + page_shape
    )
    arrived_pages = lax.all_to_all(outgoing_pages, "req", split_axis=0, concat_axis=0, tiled=True)
    own_owner = jnp.take(page_owner, req_index, axis=0)
    own_rank = jnp.take(page_rank, req_index, axis=0)
    context = jnp.take(
        arrived_pages.reshape((req_count * capacity,) + page_shape),
        own_owner * capacity + own_rank,
        axis=0,
    )
    context = context.reshape(context_len, 2, lane_heads, head_dim)
    score_scale = 1.0 / math.sqrt(head_dim)
    near_scores = (
        jnp.einsum("ihc,jhc->hij", query_rows, keys_new, preferred_element_type=jnp.float32)
        * score_scale
    )
    far_scores = (
        jnp.einsum("ihc,jhc->hij", query_rows, context[:, 0], preferred_element_type=jnp.float32)
        * score_scale
    )
    same_request = second[:, None] == second[None, :]
    near_weights = jnp.where(same_request[None], jnp.exp(near_scores), jnp.float32(0.0))
    far_weights = jnp.where((carried == 1)[None, :, None], jnp.exp(far_scores), jnp.float32(0.0))
    totals = jnp.sum(near_weights, axis=2, keepdims=True) + jnp.sum(
        far_weights, axis=2, keepdims=True
    )
    near_probs = (near_weights / totals).astype(jnp.bfloat16)
    far_probs = (far_weights / totals).astype(jnp.bfloat16)
    attended = jnp.einsum(
        "hij,jhc->ihc",
        near_probs,
        values_new.reshape(group_rows, lane_heads, head_dim),
        preferred_element_type=jnp.float32,
    )
    attended = attended + jnp.einsum(
        "hij,jhc->ihc", far_probs, context[:, 1], preferred_element_type=jnp.float32
    )
    attended = attended.astype(jnp.bfloat16).reshape(group_rows, lane_width)
    shard_rows = routes.shape[0]
    row_start = lane_index * shard_rows
    head_terms = jnp.dot(attended, server_out, preferred_element_type=jnp.float32)
    server_gate_up, head_terms = lax.optimization_barrier((server_gate_up, head_terms))
    mixed_own = scatter_sum(head_terms, lax.axis_size("tp"))
    residual_own = lax.dynamic_slice_in_dim(tokens_f32, row_start, shard_rows, 0) + mixed_own
    moe_own = rms_scale(residual_own, moe_gain).astype(jnp.bfloat16)
    logits = jnp.dot(moe_own, router_weight, preferred_element_type=jnp.float32)
    exps = jnp.exp(logits)
    routed_exps = jnp.take_along_axis(exps, routes, axis=1)
    entry_gates = routed_exps / jnp.sum(routed_exps, axis=1, keepdims=True)
    top_count = routes.shape[1]
    slot_depth = 3 * shard_rows * top_count // (2 * expert_count)
    flat_routes = routes.reshape(-1)
    onehot = (flat_routes[:, None] == jnp.arange(expert_count, dtype=jnp.int32)[None, :]).astype(
        jnp.int32
    )
    entry_rank = jnp.sum((jnp.cumsum(onehot, axis=0) - onehot) * onehot, axis=1)
    entry_slot = (flat_routes * slot_depth + entry_rank).reshape(shard_rows, top_count)
    select_table = jnp.any(
        entry_slot[None, :, :]
        == jnp.arange(expert_count * slot_depth, dtype=jnp.int32)[:, None, None],
        axis=2,
    ).astype(jnp.bfloat16)
    outgoing_rows = jnp.dot(select_table, moe_own, preferred_element_type=jnp.float32).astype(
        jnp.bfloat16
    )
    send_rows = jnp.broadcast_to(
        outgoing_rows.reshape(expert_count, 1, slot_depth, model_width),
        (expert_count, 2, slot_depth, model_width),
    ).reshape(2 * expert_count, slot_depth, model_width)
    arrived_rows = lax.all_to_all(send_rows, ("req", "tp"), split_axis=0, concat_axis=0, tiled=True)
    flat_rows = arrived_rows.reshape(-1, model_width)
    both = jnp.dot(flat_rows, server_gate_up[0], preferred_element_type=jnp.float32)
    act = (jax.nn.silu(both[:, :half_units]) * both[:, half_units:]).astype(jnp.bfloat16)
    expert_rows = (
        jnp.dot(act, down_weight[0], preferred_element_type=jnp.float32)
        .astype(jnp.bfloat16)
        .reshape(arrived_rows.shape)
    )
    returned = lax.all_to_all(expert_rows, ("req", "tp"), split_axis=0, concat_axis=0, tiled=True)
    returned = returned.reshape(expert_count, 2, slot_depth, model_width)
    joined_out = (returned[:, 0].astype(jnp.float32) + returned[:, 1].astype(jnp.float32)).reshape(
        expert_count * slot_depth, model_width
    )
    picked_rows = jnp.take(joined_out, entry_slot.reshape(-1), axis=0).reshape(
        shard_rows, top_count, model_width
    )
    moe_out = jnp.sum(picked_rows * entry_gates[:, :, None], axis=1)
    hidden_rows = (residual_own + moe_out).astype(jnp.bfloat16)
    return (server_qkv, server_out, server_gate_up, hidden_rows, new_cache)


def solution(mesh):
    in_specs = (
        P("req", None),
        P(),
        P(),
        P(),
        P(),
        P("req", "tp"),
        P("req", "tp"),
        P("req", "tp"),
        P("tp", "req"),
        P(None, ("req", "tp"), None),
        P(None, ("req", "tp"), None),
        P(("req", "tp"), None, None),
        P(),
        P("req", None, None, "tp"),
        P(),
        P(),
        P(),
        P(),
        P(("req", "tp"), None),
    )
    out_specs = (
        P(None, "tp"),
        P("tp", None),
        P(("req", "tp"), None, None),
        P(("req", "tp"), None),
        P("req", None, "tp"),
    )
    return jax.shard_map(body, mesh=mesh, in_specs=in_specs, out_specs=out_specs, check_vma=False)
```

```python
import functools
import math

import jax
import jax.numpy as jnp
from jax import lax
from jax.experimental import pallas as pl
from jax.experimental.pallas import tpu as pltpu
from jax.sharding import PartitionSpec as P

MESH = pl.DeviceIdType.MESH

norm_eps = 1e-06
rope_base = 50000.0


def rms_scale(values, gain_vec):
    return (
        values * lax.rsqrt(jnp.mean(values * values, axis=-1, keepdims=True) + norm_eps) * gain_vec
    )


def rotate_half(values, cosine, sine_part):
    half_width = values.shape[-1] // 2
    first_half = values[..., :half_width]
    second_half = values[..., half_width:]
    return jnp.concatenate(
        [
            first_half * cosine - second_half * sine_part,
            second_half * cosine + first_half * sine_part,
        ],
        axis=-1,
    )


def split_halves(weights):
    expert_count, rows_here, hidden_units = weights.shape
    return weights.reshape(expert_count, rows_here, 2, hidden_units // 2).transpose(0, 2, 1, 3)


def scatter_sum_kernel(parts, x_ref, out_ref, held, send_sem, recv_sem):
    me = lax.axis_index("tp")
    group = lax.axis_index("req")
    rows = out_ref.shape[0]
    barrier = pltpu.get_barrier_semaphore()
    for step in range(1, parts):
        peer = lax.rem(me + step, parts)
        pl.semaphore_signal(barrier, inc=1, device_id=(group, peer), device_id_type=MESH)
    pl.semaphore_wait(barrier, parts - 1)

    def outgoing(peer):
        return pltpu.make_async_remote_copy(
            src_ref=x_ref.at[pl.ds(pl.multiple_of(peer * rows, rows), rows)],
            dst_ref=held.at[me],
            send_sem=send_sem.at[peer],
            recv_sem=recv_sem.at[me],
            device_id=(group, peer),
            device_id_type=MESH,
        )

    def incoming(peer):
        return pltpu.make_async_remote_copy(
            src_ref=x_ref.at[pl.ds(pl.multiple_of(me * rows, rows), rows)],
            dst_ref=held.at[peer],
            send_sem=send_sem.at[peer],
            recv_sem=recv_sem.at[peer],
            device_id=(group, peer),
            device_id_type=MESH,
        )

    for step in range(1, parts):
        outgoing(lax.rem(me + step, parts)).start()
    total = x_ref[pl.ds(pl.multiple_of(me * rows, rows), rows), :]
    for step in range(1, parts):
        peer = lax.rem(me + parts - step, parts)
        incoming(peer).wait_recv()
        total = total + held[peer]
    for step in range(1, parts):
        outgoing(lax.rem(me + step, parts)).wait_send()
    out_ref[...] = total


def scatter_sum(x, parts):
    rows = x.shape[0] // parts
    return pl.pallas_call(
        functools.partial(scatter_sum_kernel, parts),
        out_shape=jax.ShapeDtypeStruct((rows, x.shape[1]), x.dtype),
        in_specs=[pl.BlockSpec(memory_space=pltpu.VMEM)],
        out_specs=pl.BlockSpec(memory_space=pltpu.VMEM),
        scratch_shapes=[
            pltpu.VMEM((parts, rows, x.shape[1]), x.dtype),
            pltpu.SemaphoreType.DMA((parts,)),
            pltpu.SemaphoreType.DMA((parts,)),
        ],
        compiler_params=pltpu.CompilerParams(collective_id=0, has_side_effects=True),
    )(x)


def gather_kernel(count, x_ref, out_ref, held, send_sem, recv_sem):
    me = lax.axis_index("req")
    lane = lax.axis_index("tp")
    width = x_ref.shape[1]
    barrier = pltpu.get_barrier_semaphore()
    for step in range(1, count):
        peer = lax.rem(me + step, count)
        pl.semaphore_signal(barrier, inc=1, device_id=(peer, lane), device_id_type=MESH)
    pl.semaphore_wait(barrier, count - 1)

    def transfer(peer, slot):
        return pltpu.make_async_remote_copy(
            src_ref=x_ref,
            dst_ref=held.at[slot],
            send_sem=send_sem.at[peer],
            recv_sem=recv_sem.at[slot],
            device_id=(peer, lane),
            device_id_type=MESH,
        )

    for step in range(1, count):
        peer = lax.rem(me + step, count)
        transfer(peer, me).start()
    held[me] = x_ref[...]
    for step in range(1, count):
        peer = lax.rem(me + count - step, count)
        transfer(peer, peer).wait_recv()
    for step in range(1, count):
        peer = lax.rem(me + step, count)
        transfer(peer, me).wait_send()
    for slot in range(count):
        out_ref[:, slot * width : (slot + 1) * width] = held[slot]


def gather_columns(x, count):
    return pl.pallas_call(
        functools.partial(gather_kernel, count),
        out_shape=jax.ShapeDtypeStruct((x.shape[0], count * x.shape[1]), x.dtype),
        in_specs=[pl.BlockSpec(memory_space=pltpu.VMEM)],
        out_specs=pl.BlockSpec(memory_space=pltpu.VMEM),
        scratch_shapes=[
            pltpu.VMEM((count,) + x.shape, x.dtype),
            pltpu.SemaphoreType.DMA((count,)),
            pltpu.SemaphoreType.DMA((count,)),
        ],
        compiler_params=pltpu.CompilerParams(collective_id=3, has_side_effects=True),
    )(x)


def pack_kernel(gate_ref, up_ref, out_ref):
    half = gate_ref.shape[2] // 2
    for expert in range(gate_ref.shape[0]):
        for half_id in range(2):
            columns = slice(half_id * half, (half_id + 1) * half)
            out_ref[2 * expert + half_id, :, :half] = gate_ref[expert, :, columns].astype(out_ref.dtype)
            out_ref[2 * expert + half_id, :, half:] = up_ref[expert, :, columns].astype(out_ref.dtype)


def pack_halves(gate, up, step_experts=8):
    expert_count, rows_here, hidden_units = gate.shape
    block = (step_experts, rows_here, hidden_units)
    return pl.pallas_call(
        pack_kernel,
        out_shape=jax.ShapeDtypeStruct((2 * expert_count, rows_here, hidden_units), jnp.bfloat16),
        grid=(expert_count // step_experts,),
        in_specs=[pl.BlockSpec(block, lambda i: (i, 0, 0))] * 2,
        out_specs=pl.BlockSpec((2 * step_experts, rows_here, hidden_units), lambda i: (i, 0, 0)),
    )(gate, up)


def body(
    tokens,
    attn_gain,
    query_gain,
    key_gain,
    moe_gain,
    query_weight,
    key_weight,
    value_weight,
    out_weight,
    gate_weight,
    up_weight,
    down_weight,
    router_weight,
    page_store,
    prompt_lengths,
    continues,
    page_owner,
    page_slot,
    routes,
):
    req_count = lax.axis_size("req")
    req_index = lax.axis_index("req")
    lane_index = lax.axis_index("tp")
    joined_local = jnp.concatenate(
        [
            query_weight.astype(jnp.bfloat16),
            key_weight.astype(jnp.bfloat16),
            value_weight.astype(jnp.bfloat16),
        ],
        axis=1,
    )
    server_qkv = lax.all_gather(joined_local, "req", axis=0, tiled=True)
    server_out = gather_columns(out_weight.astype(jnp.bfloat16), req_count)
    expert_count, rows_here, hidden_units = gate_weight.shape
    half_units = hidden_units // 2
    packed = pack_halves(gate_weight, up_weight)
    packed, server_out = lax.optimization_barrier((packed, server_out))
    server_gate_up = lax.all_to_all(packed, ("req", "tp"), split_axis=0, concat_axis=1, tiled=True)
    group_rows, model_width = tokens.shape
    tokens_f32 = tokens.astype(jnp.float32)
    normed = rms_scale(tokens_f32, attn_gain).astype(jnp.bfloat16)
    projected = jnp.dot(normed, server_qkv, preferred_element_type=jnp.float32)
    head_dim = query_gain.shape[0]
    lane_width = server_qkv.shape[1] // 3
    lane_heads = lane_width // head_dim
    query_raw = projected[:, :lane_width].reshape(group_rows, lane_heads, head_dim)
    key_raw = projected[:, lane_width : 2 * lane_width].reshape(group_rows, lane_heads, head_dim)
    value_raw = projected[:, 2 * lane_width :]
    first_length = lax.dynamic_index_in_dim(prompt_lengths, 2 * req_index, 0, keepdims=False)
    carry_flags = lax.dynamic_slice_in_dim(continues, 2 * req_index, 2)
    row_ids = jnp.arange(group_rows, dtype=jnp.int32)
    second = (row_ids >= first_length).astype(jnp.int32)
    within = row_ids - second * first_length
    carried = jnp.where(second == 1, carry_flags[1], carry_flags[0])
    pages_per = page_owner.shape[1]
    page_rows = page_store.shape[1]
    context_len = pages_per * page_rows
    position = (within + context_len * carried).astype(jnp.float32)
    inverse = jnp.power(
        jnp.float32(rope_base), -(jnp.arange(head_dim // 2, dtype=jnp.float32) * 2.0 / head_dim)
    )
    angles = position[:, None, None] * inverse[None, None, :]
    cosine = jnp.cos(angles)
    sine_part = jnp.sin(angles)
    query_rows = rotate_half(rms_scale(query_raw, query_gain), cosine, sine_part).astype(
        jnp.bfloat16
    )
    keys_new = rotate_half(rms_scale(key_raw, key_gain), cosine, sine_part).astype(jnp.bfloat16)
    values_new = value_raw.astype(jnp.bfloat16)
    new_cache = jnp.stack([keys_new.reshape(group_rows, lane_width), values_new], axis=1)
    capacity = max(2, (pages_per + req_count - 2) // (req_count - 1))
    page_ids = jnp.arange(pages_per, dtype=jnp.int32)
    earlier = page_ids[None, :] < page_ids[:, None]
    same_owner = page_owner[:, :, None] == page_owner[:, None, :]
    page_rank = jnp.sum((same_owner & earlier[None]).astype(jnp.int32), axis=2)
    owned_here = page_owner == req_index
    chosen = owned_here[:, None, :] & (
        page_rank[:, None, :] == jnp.arange(capacity, dtype=jnp.int32)[None, :, None]
    )
    send_slot = jnp.sum(jnp.where(chosen, page_slot[:, None, :], 0), axis=2)
    page_shape = page_store.shape[1:]
    outgoing_pages = jnp.take(page_store, send_slot.reshape(-1), axis=0).reshape(
        (req_count, capacity) + page_shape
    )
    arrived_pages = lax.all_to_all(outgoing_pages, "req", split_axis=0, concat_axis=0, tiled=True)
    own_owner = jnp.take(page_owner, req_index, axis=0)
    own_rank = jnp.take(page_rank, req_index, axis=0)
    context = jnp.take(
        arrived_pages.reshape((req_count * capacity,) + page_shape),
        own_owner * capacity + own_rank,
        axis=0,
    )
    context = context.reshape(context_len, 2, lane_heads, head_dim)
    score_scale = 1.0 / math.sqrt(head_dim)
    near_scores = (
        jnp.einsum("ihc,jhc->hij", query_rows, keys_new, preferred_element_type=jnp.float32)
        * score_scale
    )
    far_scores = (
        jnp.einsum("ihc,jhc->hij", query_rows, context[:, 0], preferred_element_type=jnp.float32)
        * score_scale
    )
    same_request = second[:, None] == second[None, :]
    near_weights = jnp.where(same_request[None], jnp.exp(near_scores), jnp.float32(0.0))
    far_weights = jnp.where((carried == 1)[None, :, None], jnp.exp(far_scores), jnp.float32(0.0))
    totals = jnp.sum(near_weights, axis=2, keepdims=True) + jnp.sum(
        far_weights, axis=2, keepdims=True
    )
    near_probs = (near_weights / totals).astype(jnp.bfloat16)
    far_probs = (far_weights / totals).astype(jnp.bfloat16)
    attended = jnp.einsum(
        "hij,jhc->ihc",
        near_probs,
        values_new.reshape(group_rows, lane_heads, head_dim),
        preferred_element_type=jnp.float32,
    )
    attended = attended + jnp.einsum(
        "hij,jhc->ihc", far_probs, context[:, 1], preferred_element_type=jnp.float32
    )
    attended = attended.astype(jnp.bfloat16).reshape(group_rows, lane_width)
    shard_rows = routes.shape[0]
    row_start = lane_index * shard_rows
    head_terms = jnp.dot(attended, server_out, preferred_element_type=jnp.float32)
    mixed_own = scatter_sum(head_terms, lax.axis_size("tp"))
    residual_own = lax.dynamic_slice_in_dim(tokens_f32, row_start, shard_rows, 0) + mixed_own
    moe_own = rms_scale(residual_own, moe_gain).astype(jnp.bfloat16)
    logits = jnp.dot(moe_own, router_weight, preferred_element_type=jnp.float32)
    exps = jnp.exp(logits)
    routed_exps = jnp.take_along_axis(exps, routes, axis=1)
    entry_gates = routed_exps / jnp.sum(routed_exps, axis=1, keepdims=True)
    top_count = routes.shape[1]
    slot_depth = 3 * shard_rows * top_count // (2 * expert_count)
    flat_routes = routes.reshape(-1)
    onehot = (flat_routes[:, None] == jnp.arange(expert_count, dtype=jnp.int32)[None, :]).astype(
        jnp.int32
    )
    entry_rank = jnp.sum((jnp.cumsum(onehot, axis=0) - onehot) * onehot, axis=1)
    entry_slot = (flat_routes * slot_depth + entry_rank).reshape(shard_rows, top_count)
    select_table = jnp.any(
        entry_slot[None, :, :]
        == jnp.arange(expert_count * slot_depth, dtype=jnp.int32)[:, None, None],
        axis=2,
    ).astype(jnp.bfloat16)
    outgoing_rows = jnp.dot(select_table, moe_own, preferred_element_type=jnp.float32).astype(
        jnp.bfloat16
    )
    send_rows = jnp.broadcast_to(
        outgoing_rows.reshape(expert_count, 1, slot_depth, model_width),
        (expert_count, 2, slot_depth, model_width),
    ).reshape(2 * expert_count, slot_depth, model_width)
    server_gate_up, send_rows = lax.optimization_barrier((server_gate_up, send_rows))
    arrived_rows = lax.all_to_all(send_rows, ("req", "tp"), split_axis=0, concat_axis=0, tiled=True)
    flat_rows = arrived_rows.reshape(-1, model_width)
    both = jnp.dot(flat_rows, server_gate_up[0], preferred_element_type=jnp.float32)
    act = (jax.nn.silu(both[:, :half_units]) * both[:, half_units:]).astype(jnp.bfloat16)
    expert_rows = (
        jnp.dot(act, down_weight[0], preferred_element_type=jnp.float32)
        .astype(jnp.bfloat16)
        .reshape(arrived_rows.shape)
    )
    returned = lax.all_to_all(expert_rows, ("req", "tp"), split_axis=0, concat_axis=0, tiled=True)
    returned = returned.reshape(expert_count, 2, slot_depth, model_width)
    joined_out = (returned[:, 0].astype(jnp.float32) + returned[:, 1].astype(jnp.float32)).reshape(
        expert_count * slot_depth, model_width
    )
    picked_rows = jnp.take(joined_out, entry_slot.reshape(-1), axis=0).reshape(
        shard_rows, top_count, model_width
    )
    moe_out = jnp.sum(picked_rows * entry_gates[:, :, None], axis=1)
    hidden_rows = (residual_own + moe_out).astype(jnp.bfloat16)
    return (server_qkv, server_out, server_gate_up, hidden_rows, new_cache)


def solution(mesh):
    in_specs = (
        P("req", None),
        P(),
        P(),
        P(),
        P(),
        P("req", "tp"),
        P("req", "tp"),
        P("req", "tp"),
        P("tp", "req"),
        P(None, ("req", "tp"), None),
        P(None, ("req", "tp"), None),
        P(("req", "tp"), None, None),
        P(),
        P("req", None, None, "tp"),
        P(),
        P(),
        P(),
        P(),
        P(("req", "tp"), None),
    )
    out_specs = (
        P(None, "tp"),
        P("tp", None),
        P(("req", "tp"), None, None),
        P(("req", "tp"), None),
        P("req", None, "tp"),
    )
    return jax.shard_map(body, mesh=mesh, in_specs=in_specs, out_specs=out_specs, check_vma=False)
```

```python
import functools
import math

import jax
import jax.numpy as jnp
from jax import lax
from jax.experimental import pallas as pl
from jax.experimental.pallas import tpu as pltpu
from jax.sharding import PartitionSpec as P

MESH = pl.DeviceIdType.MESH

norm_eps = 1e-06
rope_base = 50000.0


def rms_scale(values, gain_vec):
    return (
        values * lax.rsqrt(jnp.mean(values * values, axis=-1, keepdims=True) + norm_eps) * gain_vec
    )


def rotate_half(values, cosine, sine_part):
    half_width = values.shape[-1] // 2
    first_half = values[..., :half_width]
    second_half = values[..., half_width:]
    return jnp.concatenate(
        [
            first_half * cosine - second_half * sine_part,
            second_half * cosine + first_half * sine_part,
        ],
        axis=-1,
    )


def split_halves(weights):
    expert_count, rows_here, hidden_units = weights.shape
    return weights.reshape(expert_count, rows_here, 2, hidden_units // 2).transpose(0, 2, 1, 3)


def scatter_sum_kernel(parts, x_ref, out_ref, held, send_sem, recv_sem):
    me = lax.axis_index("tp")
    group = lax.axis_index("req")
    rows = out_ref.shape[0]
    barrier = pltpu.get_barrier_semaphore()
    for step in range(1, parts):
        peer = lax.rem(me + step, parts)
        pl.semaphore_signal(barrier, inc=1, device_id=(group, peer), device_id_type=MESH)
    pl.semaphore_wait(barrier, parts - 1)

    def outgoing(peer):
        return pltpu.make_async_remote_copy(
            src_ref=x_ref.at[pl.ds(pl.multiple_of(peer * rows, rows), rows)],
            dst_ref=held.at[me],
            send_sem=send_sem.at[peer],
            recv_sem=recv_sem.at[me],
            device_id=(group, peer),
            device_id_type=MESH,
        )

    def incoming(peer):
        return pltpu.make_async_remote_copy(
            src_ref=x_ref.at[pl.ds(pl.multiple_of(me * rows, rows), rows)],
            dst_ref=held.at[peer],
            send_sem=send_sem.at[peer],
            recv_sem=recv_sem.at[peer],
            device_id=(group, peer),
            device_id_type=MESH,
        )

    for step in range(1, parts):
        outgoing(lax.rem(me + step, parts)).start()
    total = x_ref[pl.ds(pl.multiple_of(me * rows, rows), rows), :]
    for step in range(1, parts):
        peer = lax.rem(me + parts - step, parts)
        incoming(peer).wait_recv()
        total = total + held[peer]
    for step in range(1, parts):
        outgoing(lax.rem(me + step, parts)).wait_send()
    out_ref[...] = total


def scatter_sum(x, parts):
    rows = x.shape[0] // parts
    return pl.pallas_call(
        functools.partial(scatter_sum_kernel, parts),
        out_shape=jax.ShapeDtypeStruct((rows, x.shape[1]), x.dtype),
        in_specs=[pl.BlockSpec(memory_space=pltpu.VMEM)],
        out_specs=pl.BlockSpec(memory_space=pltpu.VMEM),
        scratch_shapes=[
            pltpu.VMEM((parts, rows, x.shape[1]), x.dtype),
            pltpu.SemaphoreType.DMA((parts,)),
            pltpu.SemaphoreType.DMA((parts,)),
        ],
        compiler_params=pltpu.CompilerParams(collective_id=0, has_side_effects=True),
    )(x)


def copy_kernel(x_ref, o_ref):
    o_ref[...] = x_ref[...]


def copy_rows(x, steps):
    rows = x.shape[0] // steps
    block = (rows,) + x.shape[1:]
    index = lambda i: (i,) + (0,) * (x.ndim - 1)
    return pl.pallas_call(
        copy_kernel,
        out_shape=jax.ShapeDtypeStruct(x.shape, x.dtype),
        grid=(steps,),
        in_specs=[pl.BlockSpec(block, index)],
        out_specs=pl.BlockSpec(block, index),
        cost_estimate=pl.CostEstimate(flops=0, transcendentals=0, bytes_accessed=2 * x.size * x.dtype.itemsize),
    )(x)


def body(
    tokens,
    attn_gain,
    query_gain,
    key_gain,
    moe_gain,
    query_weight,
    key_weight,
    value_weight,
    out_weight,
    gate_weight,
    up_weight,
    down_weight,
    router_weight,
    page_store,
    prompt_lengths,
    continues,
    page_owner,
    page_slot,
    routes,
):
    req_count = lax.axis_size("req")
    req_index = lax.axis_index("req")
    lane_index = lax.axis_index("tp")
    joined_local = jnp.concatenate(
        [
            query_weight.astype(jnp.bfloat16),
            key_weight.astype(jnp.bfloat16),
            value_weight.astype(jnp.bfloat16),
        ],
        axis=1,
    )
    server_qkv, server_out = (
        lax.all_gather(joined_local, "req", axis=0, tiled=True),
        lax.all_gather(out_weight.astype(jnp.bfloat16), "req", axis=1, tiled=True),
    )
    expert_count, rows_here, hidden_units = gate_weight.shape
    half_units = hidden_units // 2
    packed = jnp.concatenate(
        [
            split_halves(gate_weight.astype(jnp.bfloat16)),
            split_halves(up_weight.astype(jnp.bfloat16)),
        ],
        axis=3,
    ).reshape(2 * expert_count, rows_here, hidden_units)
    server_gate_up = lax.all_to_all(packed, ("req", "tp"), split_axis=0, concat_axis=1, tiled=True)
    group_rows, model_width = tokens.shape
    tokens_f32 = tokens.astype(jnp.float32)
    normed = rms_scale(tokens_f32, attn_gain).astype(jnp.bfloat16)
    projected = jnp.dot(normed, server_qkv, preferred_element_type=jnp.float32)
    head_dim = query_gain.shape[0]
    lane_width = server_qkv.shape[1] // 3
    lane_heads = lane_width // head_dim
    query_raw = projected[:, :lane_width].reshape(group_rows, lane_heads, head_dim)
    key_raw = projected[:, lane_width : 2 * lane_width].reshape(group_rows, lane_heads, head_dim)
    value_raw = projected[:, 2 * lane_width :]
    first_length = lax.dynamic_index_in_dim(prompt_lengths, 2 * req_index, 0, keepdims=False)
    carry_flags = lax.dynamic_slice_in_dim(continues, 2 * req_index, 2)
    row_ids = jnp.arange(group_rows, dtype=jnp.int32)
    second = (row_ids >= first_length).astype(jnp.int32)
    within = row_ids - second * first_length
    carried = jnp.where(second == 1, carry_flags[1], carry_flags[0])
    pages_per = page_owner.shape[1]
    page_rows = page_store.shape[1]
    context_len = pages_per * page_rows
    position = (within + context_len * carried).astype(jnp.float32)
    inverse = jnp.power(
        jnp.float32(rope_base), -(jnp.arange(head_dim // 2, dtype=jnp.float32) * 2.0 / head_dim)
    )
    angles = position[:, None, None] * inverse[None, None, :]
    cosine = jnp.cos(angles)
    sine_part = jnp.sin(angles)
    query_rows = rotate_half(rms_scale(query_raw, query_gain), cosine, sine_part).astype(
        jnp.bfloat16
    )
    keys_new = rotate_half(rms_scale(key_raw, key_gain), cosine, sine_part).astype(jnp.bfloat16)
    values_new = value_raw.astype(jnp.bfloat16)
    new_cache = jnp.stack([keys_new.reshape(group_rows, lane_width), values_new], axis=1)
    capacity = max(2, (pages_per + req_count - 2) // (req_count - 1))
    page_ids = jnp.arange(pages_per, dtype=jnp.int32)
    earlier = page_ids[None, :] < page_ids[:, None]
    same_owner = page_owner[:, :, None] == page_owner[:, None, :]
    page_rank = jnp.sum((same_owner & earlier[None]).astype(jnp.int32), axis=2)
    owned_here = page_owner == req_index
    chosen = owned_here[:, None, :] & (
        page_rank[:, None, :] == jnp.arange(capacity, dtype=jnp.int32)[None, :, None]
    )
    send_slot = jnp.sum(jnp.where(chosen, page_slot[:, None, :], 0), axis=2)
    page_shape = page_store.shape[1:]
    outgoing_pages = jnp.take(page_store, send_slot.reshape(-1), axis=0).reshape(
        (req_count, capacity) + page_shape
    )
    arrived_pages = lax.all_to_all(outgoing_pages, "req", split_axis=0, concat_axis=0, tiled=True)
    own_owner = jnp.take(page_owner, req_index, axis=0)
    own_rank = jnp.take(page_rank, req_index, axis=0)
    context = jnp.take(
        arrived_pages.reshape((req_count * capacity,) + page_shape),
        own_owner * capacity + own_rank,
        axis=0,
    )
    context = context.reshape(context_len, 2, lane_heads, head_dim)
    score_scale = 1.0 / math.sqrt(head_dim)
    near_scores = (
        jnp.einsum("ihc,jhc->hij", query_rows, keys_new, preferred_element_type=jnp.float32)
        * score_scale
    )
    far_scores = (
        jnp.einsum("ihc,jhc->hij", query_rows, context[:, 0], preferred_element_type=jnp.float32)
        * score_scale
    )
    same_request = second[:, None] == second[None, :]
    near_weights = jnp.where(same_request[None], jnp.exp(near_scores), jnp.float32(0.0))
    far_weights = jnp.where((carried == 1)[None, :, None], jnp.exp(far_scores), jnp.float32(0.0))
    totals = jnp.sum(near_weights, axis=2, keepdims=True) + jnp.sum(
        far_weights, axis=2, keepdims=True
    )
    near_probs = (near_weights / totals).astype(jnp.bfloat16)
    far_probs = (far_weights / totals).astype(jnp.bfloat16)
    attended = jnp.einsum(
        "hij,jhc->ihc",
        near_probs,
        values_new.reshape(group_rows, lane_heads, head_dim),
        preferred_element_type=jnp.float32,
    )
    attended = attended + jnp.einsum(
        "hij,jhc->ihc", far_probs, context[:, 1], preferred_element_type=jnp.float32
    )
    attended = attended.astype(jnp.bfloat16).reshape(group_rows, lane_width)
    shard_rows = routes.shape[0]
    row_start = lane_index * shard_rows
    qkv_out = copy_rows(server_qkv, 4)
    qkv_out, attended = lax.optimization_barrier((qkv_out, attended))
    head_terms = jnp.dot(attended, server_out, preferred_element_type=jnp.float32)
    server_gate_up, head_terms = lax.optimization_barrier((server_gate_up, head_terms))
    mixed_own = scatter_sum(head_terms, lax.axis_size("tp"))
    residual_own = lax.dynamic_slice_in_dim(tokens_f32, row_start, shard_rows, 0) + mixed_own
    moe_own = rms_scale(residual_own, moe_gain).astype(jnp.bfloat16)
    logits = jnp.dot(moe_own, router_weight, preferred_element_type=jnp.float32)
    exps = jnp.exp(logits)
    routed_exps = jnp.take_along_axis(exps, routes, axis=1)
    entry_gates = routed_exps / jnp.sum(routed_exps, axis=1, keepdims=True)
    top_count = routes.shape[1]
    slot_depth = 3 * shard_rows * top_count // (2 * expert_count)
    flat_routes = routes.reshape(-1)
    onehot = (flat_routes[:, None] == jnp.arange(expert_count, dtype=jnp.int32)[None, :]).astype(
        jnp.int32
    )
    entry_rank = jnp.sum((jnp.cumsum(onehot, axis=0) - onehot) * onehot, axis=1)
    entry_slot = (flat_routes * slot_depth + entry_rank).reshape(shard_rows, top_count)
    select_table = jnp.any(
        entry_slot[None, :, :]
        == jnp.arange(expert_count * slot_depth, dtype=jnp.int32)[:, None, None],
        axis=2,
    ).astype(jnp.bfloat16)
    outgoing_rows = jnp.dot(select_table, moe_own, preferred_element_type=jnp.float32).astype(
        jnp.bfloat16
    )
    send_rows = jnp.broadcast_to(
        outgoing_rows.reshape(expert_count, 1, slot_depth, model_width),
        (expert_count, 2, slot_depth, model_width),
    ).reshape(2 * expert_count, slot_depth, model_width)
    arrived_rows = lax.all_to_all(send_rows, ("req", "tp"), split_axis=0, concat_axis=0, tiled=True)
    flat_rows = arrived_rows.reshape(-1, model_width)
    both = jnp.dot(flat_rows, server_gate_up[0], preferred_element_type=jnp.float32)
    act = (jax.nn.silu(both[:, :half_units]) * both[:, half_units:]).astype(jnp.bfloat16)
    expert_rows = (
        jnp.dot(act, down_weight[0], preferred_element_type=jnp.float32)
        .astype(jnp.bfloat16)
        .reshape(arrived_rows.shape)
    )
    returned = lax.all_to_all(expert_rows, ("req", "tp"), split_axis=0, concat_axis=0, tiled=True)
    returned = returned.reshape(expert_count, 2, slot_depth, model_width)
    joined_out = (returned[:, 0].astype(jnp.float32) + returned[:, 1].astype(jnp.float32)).reshape(
        expert_count * slot_depth, model_width
    )
    picked_rows = jnp.take(joined_out, entry_slot.reshape(-1), axis=0).reshape(
        shard_rows, top_count, model_width
    )
    moe_out = jnp.sum(picked_rows * entry_gates[:, :, None], axis=1)
    hidden_rows = (residual_own + moe_out).astype(jnp.bfloat16)
    gate_up_out = copy_rows(server_gate_up.reshape(server_gate_up.shape[1:]), 4).reshape(server_gate_up.shape)
    return (qkv_out, copy_rows(server_out, 1), gate_up_out, hidden_rows, new_cache)


def solution(mesh):
    in_specs = (
        P("req", None),
        P(),
        P(),
        P(),
        P(),
        P("req", "tp"),
        P("req", "tp"),
        P("req", "tp"),
        P("tp", "req"),
        P(None, ("req", "tp"), None),
        P(None, ("req", "tp"), None),
        P(("req", "tp"), None, None),
        P(),
        P("req", None, None, "tp"),
        P(),
        P(),
        P(),
        P(),
        P(("req", "tp"), None),
    )
    out_specs = (
        P(None, "tp"),
        P("tp", None),
        P(("req", "tp"), None, None),
        P(("req", "tp"), None),
        P("req", None, "tp"),
    )
    return jax.shard_map(body, mesh=mesh, in_specs=in_specs, out_specs=out_specs, check_vma=False)
```

```python
import functools
import math

import jax
import jax.numpy as jnp
from jax import lax
from jax.experimental import pallas as pl
from jax.experimental.pallas import tpu as pltpu
from jax.sharding import PartitionSpec as P

MESH = pl.DeviceIdType.MESH

norm_eps = 1e-06
rope_base = 50000.0


def rms_scale(values, gain_vec):
    return (
        values * lax.rsqrt(jnp.mean(values * values, axis=-1, keepdims=True) + norm_eps) * gain_vec
    )


def rotate_half(values, cosine, sine_part):
    half_width = values.shape[-1] // 2
    first_half = values[..., :half_width]
    second_half = values[..., half_width:]
    return jnp.concatenate(
        [
            first_half * cosine - second_half * sine_part,
            second_half * cosine + first_half * sine_part,
        ],
        axis=-1,
    )


def split_halves(weights):
    expert_count, rows_here, hidden_units = weights.shape
    return weights.reshape(expert_count, rows_here, 2, hidden_units // 2).transpose(0, 2, 1, 3)


def scatter_sum_kernel(parts, x_ref, out_ref, held, send_sem, recv_sem):
    me = lax.axis_index("tp")
    group = lax.axis_index("req")
    rows = out_ref.shape[0]
    barrier = pltpu.get_barrier_semaphore()
    for step in range(1, parts):
        peer = lax.rem(me + step, parts)
        pl.semaphore_signal(barrier, inc=1, device_id=(group, peer), device_id_type=MESH)
    pl.semaphore_wait(barrier, parts - 1)

    def outgoing(peer):
        return pltpu.make_async_remote_copy(
            src_ref=x_ref.at[pl.ds(pl.multiple_of(peer * rows, rows), rows)],
            dst_ref=held.at[me],
            send_sem=send_sem.at[peer],
            recv_sem=recv_sem.at[me],
            device_id=(group, peer),
            device_id_type=MESH,
        )

    def incoming(peer):
        return pltpu.make_async_remote_copy(
            src_ref=x_ref.at[pl.ds(pl.multiple_of(me * rows, rows), rows)],
            dst_ref=held.at[peer],
            send_sem=send_sem.at[peer],
            recv_sem=recv_sem.at[peer],
            device_id=(group, peer),
            device_id_type=MESH,
        )

    for step in range(1, parts):
        outgoing(lax.rem(me + step, parts)).start()
    total = x_ref[pl.ds(pl.multiple_of(me * rows, rows), rows), :]
    for step in range(1, parts):
        peer = lax.rem(me + parts - step, parts)
        incoming(peer).wait_recv()
        total = total + held[peer]
    for step in range(1, parts):
        outgoing(lax.rem(me + step, parts)).wait_send()
    out_ref[...] = total


def scatter_sum(x, parts):
    rows = x.shape[0] // parts
    return pl.pallas_call(
        functools.partial(scatter_sum_kernel, parts),
        out_shape=jax.ShapeDtypeStruct((rows, x.shape[1]), x.dtype),
        in_specs=[pl.BlockSpec(memory_space=pltpu.VMEM)],
        out_specs=pl.BlockSpec(memory_space=pltpu.VMEM),
        scratch_shapes=[
            pltpu.VMEM((parts, rows, x.shape[1]), x.dtype),
            pltpu.SemaphoreType.DMA((parts,)),
            pltpu.SemaphoreType.DMA((parts,)),
        ],
        compiler_params=pltpu.CompilerParams(collective_id=0, has_side_effects=True),
    )(x)


def copy_kernel(x_ref, o_ref):
    o_ref[...] = x_ref[...]


def copy_rows(x, steps):
    rows = x.shape[0] // steps
    block = (rows,) + x.shape[1:]
    index = lambda i: (i,) + (0,) * (x.ndim - 1)
    return pl.pallas_call(
        copy_kernel,
        out_shape=jax.ShapeDtypeStruct(x.shape, x.dtype),
        grid=(steps,),
        in_specs=[pl.BlockSpec(block, index)],
        out_specs=pl.BlockSpec(block, index),
        cost_estimate=pl.CostEstimate(flops=0, transcendentals=0, bytes_accessed=2 * x.size * x.dtype.itemsize),
    )(x)


def body(
    tokens,
    attn_gain,
    query_gain,
    key_gain,
    moe_gain,
    query_weight,
    key_weight,
    value_weight,
    out_weight,
    gate_weight,
    up_weight,
    down_weight,
    router_weight,
    page_store,
    prompt_lengths,
    continues,
    page_owner,
    page_slot,
    routes,
):
    req_count = lax.axis_size("req")
    req_index = lax.axis_index("req")
    lane_index = lax.axis_index("tp")
    joined_local = jnp.concatenate(
        [
            query_weight.astype(jnp.bfloat16),
            key_weight.astype(jnp.bfloat16),
            value_weight.astype(jnp.bfloat16),
        ],
        axis=1,
    )
    server_qkv, server_out = (
        lax.all_gather(joined_local, "req", axis=0, tiled=True),
        lax.all_gather(out_weight.astype(jnp.bfloat16), "req", axis=1, tiled=True),
    )
    expert_count, rows_here, hidden_units = gate_weight.shape
    half_units = hidden_units // 2
    packed = jnp.concatenate(
        [
            split_halves(gate_weight.astype(jnp.bfloat16)),
            split_halves(up_weight.astype(jnp.bfloat16)),
        ],
        axis=3,
    ).reshape(2 * expert_count, rows_here, hidden_units)
    server_gate_up = lax.all_to_all(packed, ("req", "tp"), split_axis=0, concat_axis=1, tiled=True)
    group_rows, model_width = tokens.shape
    tokens_f32 = tokens.astype(jnp.float32)
    normed = rms_scale(tokens_f32, attn_gain).astype(jnp.bfloat16)
    projected = jnp.dot(normed, server_qkv, preferred_element_type=jnp.float32)
    head_dim = query_gain.shape[0]
    lane_width = server_qkv.shape[1] // 3
    lane_heads = lane_width // head_dim
    query_raw = projected[:, :lane_width].reshape(group_rows, lane_heads, head_dim)
    key_raw = projected[:, lane_width : 2 * lane_width].reshape(group_rows, lane_heads, head_dim)
    value_raw = projected[:, 2 * lane_width :]
    first_length = lax.dynamic_index_in_dim(prompt_lengths, 2 * req_index, 0, keepdims=False)
    carry_flags = lax.dynamic_slice_in_dim(continues, 2 * req_index, 2)
    row_ids = jnp.arange(group_rows, dtype=jnp.int32)
    second = (row_ids >= first_length).astype(jnp.int32)
    within = row_ids - second * first_length
    carried = jnp.where(second == 1, carry_flags[1], carry_flags[0])
    pages_per = page_owner.shape[1]
    page_rows = page_store.shape[1]
    context_len = pages_per * page_rows
    position = (within + context_len * carried).astype(jnp.float32)
    inverse = jnp.power(
        jnp.float32(rope_base), -(jnp.arange(head_dim // 2, dtype=jnp.float32) * 2.0 / head_dim)
    )
    angles = position[:, None, None] * inverse[None, None, :]
    cosine = jnp.cos(angles)
    sine_part = jnp.sin(angles)
    query_rows = rotate_half(rms_scale(query_raw, query_gain), cosine, sine_part).astype(
        jnp.bfloat16
    )
    keys_new = rotate_half(rms_scale(key_raw, key_gain), cosine, sine_part).astype(jnp.bfloat16)
    values_new = value_raw.astype(jnp.bfloat16)
    new_cache = jnp.stack([keys_new.reshape(group_rows, lane_width), values_new], axis=1)
    capacity = max(2, (pages_per + req_count - 2) // (req_count - 1))
    page_ids = jnp.arange(pages_per, dtype=jnp.int32)
    earlier = page_ids[None, :] < page_ids[:, None]
    same_owner = page_owner[:, :, None] == page_owner[:, None, :]
    page_rank = jnp.sum((same_owner & earlier[None]).astype(jnp.int32), axis=2)
    owned_here = page_owner == req_index
    chosen = owned_here[:, None, :] & (
        page_rank[:, None, :] == jnp.arange(capacity, dtype=jnp.int32)[None, :, None]
    )
    send_slot = jnp.sum(jnp.where(chosen, page_slot[:, None, :], 0), axis=2)
    page_shape = page_store.shape[1:]
    outgoing_pages = jnp.take(page_store, send_slot.reshape(-1), axis=0).reshape(
        (req_count, capacity) + page_shape
    )
    arrived_pages = lax.all_to_all(outgoing_pages, "req", split_axis=0, concat_axis=0, tiled=True)
    own_owner = jnp.take(page_owner, req_index, axis=0)
    own_rank = jnp.take(page_rank, req_index, axis=0)
    context = jnp.take(
        arrived_pages.reshape((req_count * capacity,) + page_shape),
        own_owner * capacity + own_rank,
        axis=0,
    )
    context = context.reshape(context_len, 2, lane_heads, head_dim)
    score_scale = 1.0 / math.sqrt(head_dim)
    near_scores = (
        jnp.einsum("ihc,jhc->hij", query_rows, keys_new, preferred_element_type=jnp.float32)
        * score_scale
    )
    far_scores = (
        jnp.einsum("ihc,jhc->hij", query_rows, context[:, 0], preferred_element_type=jnp.float32)
        * score_scale
    )
    same_request = second[:, None] == second[None, :]
    near_weights = jnp.where(same_request[None], jnp.exp(near_scores), jnp.float32(0.0))
    far_weights = jnp.where((carried == 1)[None, :, None], jnp.exp(far_scores), jnp.float32(0.0))
    totals = jnp.sum(near_weights, axis=2, keepdims=True) + jnp.sum(
        far_weights, axis=2, keepdims=True
    )
    near_probs = (near_weights / totals).astype(jnp.bfloat16)
    far_probs = (far_weights / totals).astype(jnp.bfloat16)
    attended = jnp.einsum(
        "hij,jhc->ihc",
        near_probs,
        values_new.reshape(group_rows, lane_heads, head_dim),
        preferred_element_type=jnp.float32,
    )
    attended = attended + jnp.einsum(
        "hij,jhc->ihc", far_probs, context[:, 1], preferred_element_type=jnp.float32
    )
    attended = attended.astype(jnp.bfloat16).reshape(group_rows, lane_width)
    shard_rows = routes.shape[0]
    row_start = lane_index * shard_rows
    qkv_out = copy_rows(server_qkv, 4)
    qkv_out, attended = lax.optimization_barrier((qkv_out, attended))
    head_terms = jnp.dot(attended, server_out, preferred_element_type=jnp.float32)
    server_gate_up, head_terms = lax.optimization_barrier((server_gate_up, head_terms))
    mixed_own = scatter_sum(head_terms, lax.axis_size("tp"))
    residual_own = lax.dynamic_slice_in_dim(tokens_f32, row_start, shard_rows, 0) + mixed_own
    moe_own = rms_scale(residual_own, moe_gain).astype(jnp.bfloat16)
    logits = jnp.dot(moe_own, router_weight, preferred_element_type=jnp.float32)
    exps = jnp.exp(logits)
    routed_exps = jnp.take_along_axis(exps, routes, axis=1)
    entry_gates = routed_exps / jnp.sum(routed_exps, axis=1, keepdims=True)
    top_count = routes.shape[1]
    slot_depth = 3 * shard_rows * top_count // (2 * expert_count)
    flat_routes = routes.reshape(-1)
    onehot = (flat_routes[:, None] == jnp.arange(expert_count, dtype=jnp.int32)[None, :]).astype(
        jnp.int32
    )
    entry_rank = jnp.sum((jnp.cumsum(onehot, axis=0) - onehot) * onehot, axis=1)
    entry_slot = (flat_routes * slot_depth + entry_rank).reshape(shard_rows, top_count)
    select_table = jnp.any(
        entry_slot[None, :, :]
        == jnp.arange(expert_count * slot_depth, dtype=jnp.int32)[:, None, None],
        axis=2,
    ).astype(jnp.bfloat16)
    outgoing_rows = jnp.dot(select_table, moe_own, preferred_element_type=jnp.float32).astype(
        jnp.bfloat16
    )
    send_rows = jnp.broadcast_to(
        outgoing_rows.reshape(expert_count, 1, slot_depth, model_width),
        (expert_count, 2, slot_depth, model_width),
    ).reshape(2 * expert_count, slot_depth, model_width)
    arrived_rows = lax.all_to_all(send_rows, ("req", "tp"), split_axis=0, concat_axis=0, tiled=True)
    flat_rows = arrived_rows.reshape(-1, model_width)
    both = jnp.dot(flat_rows, server_gate_up[0], preferred_element_type=jnp.float32)
    act = (jax.nn.silu(both[:, :half_units]) * both[:, half_units:]).astype(jnp.bfloat16)
    expert_rows = (
        jnp.dot(act, down_weight[0], preferred_element_type=jnp.float32)
        .astype(jnp.bfloat16)
        .reshape(arrived_rows.shape)
    )
    returned = lax.all_to_all(expert_rows, ("req", "tp"), split_axis=0, concat_axis=0, tiled=True)
    slot_weights = jnp.sum(
        jnp.where(
            entry_slot[:, :, None] == jnp.arange(expert_count * slot_depth, dtype=jnp.int32)[None, None, :],
            entry_gates[:, :, None],
            jnp.float32(0.0),
        ),
        axis=1,
    ).reshape(shard_rows, expert_count, 1, slot_depth)
    slot_weights = jnp.broadcast_to(
        slot_weights, (shard_rows, expert_count, 2, slot_depth)
    ).reshape(shard_rows, 2 * expert_count, slot_depth)
    moe_out = jnp.einsum(
        "ixk,xkd->id",
        slot_weights,
        returned.astype(jnp.float32),
        precision=lax.Precision.HIGHEST,
        preferred_element_type=jnp.float32,
    )
    hidden_rows = (residual_own + moe_out).astype(jnp.bfloat16)
    gate_up_out = copy_rows(server_gate_up.reshape(server_gate_up.shape[1:]), 4).reshape(server_gate_up.shape)
    return (qkv_out, copy_rows(server_out, 1), gate_up_out, hidden_rows, new_cache)


def solution(mesh):
    in_specs = (
        P("req", None),
        P(),
        P(),
        P(),
        P(),
        P("req", "tp"),
        P("req", "tp"),
        P("req", "tp"),
        P("tp", "req"),
        P(None, ("req", "tp"), None),
        P(None, ("req", "tp"), None),
        P(("req", "tp"), None, None),
        P(),
        P("req", None, None, "tp"),
        P(),
        P(),
        P(),
        P(),
        P(("req", "tp"), None),
    )
    out_specs = (
        P(None, "tp"),
        P("tp", None),
        P(("req", "tp"), None, None),
        P(("req", "tp"), None),
        P("req", None, "tp"),
    )
    return jax.shard_map(body, mesh=mesh, in_specs=in_specs, out_specs=out_specs, check_vma=False)
```

```python
import functools
import math

import jax
import jax.numpy as jnp
from jax import lax
from jax.experimental import pallas as pl
from jax.experimental.pallas import tpu as pltpu
from jax.sharding import PartitionSpec as P

MESH = pl.DeviceIdType.MESH

norm_eps = 1e-06
rope_base = 50000.0


def rms_scale(values, gain_vec):
    return (
        values * lax.rsqrt(jnp.mean(values * values, axis=-1, keepdims=True) + norm_eps) * gain_vec
    )


def rotate_half(values, cosine, sine_part):
    half_width = values.shape[-1] // 2
    first_half = values[..., :half_width]
    second_half = values[..., half_width:]
    return jnp.concatenate(
        [
            first_half * cosine - second_half * sine_part,
            second_half * cosine + first_half * sine_part,
        ],
        axis=-1,
    )


def split_halves(weights):
    expert_count, rows_here, hidden_units = weights.shape
    return weights.reshape(expert_count, rows_here, 2, hidden_units // 2).transpose(0, 2, 1, 3)


def scatter_sum_kernel(parts, x_ref, out_ref, held, send_sem, recv_sem):
    me = lax.axis_index("tp")
    group = lax.axis_index("req")
    rows = out_ref.shape[0]
    barrier = pltpu.get_barrier_semaphore()
    for step in range(1, parts):
        peer = lax.rem(me + step, parts)
        pl.semaphore_signal(barrier, inc=1, device_id=(group, peer), device_id_type=MESH)
    pl.semaphore_wait(barrier, parts - 1)

    def outgoing(peer):
        return pltpu.make_async_remote_copy(
            src_ref=x_ref.at[pl.ds(pl.multiple_of(peer * rows, rows), rows)],
            dst_ref=held.at[me],
            send_sem=send_sem.at[peer],
            recv_sem=recv_sem.at[me],
            device_id=(group, peer),
            device_id_type=MESH,
        )

    def incoming(peer):
        return pltpu.make_async_remote_copy(
            src_ref=x_ref.at[pl.ds(pl.multiple_of(me * rows, rows), rows)],
            dst_ref=held.at[peer],
            send_sem=send_sem.at[peer],
            recv_sem=recv_sem.at[peer],
            device_id=(group, peer),
            device_id_type=MESH,
        )

    for step in range(1, parts):
        outgoing(lax.rem(me + step, parts)).start()
    total = x_ref[pl.ds(pl.multiple_of(me * rows, rows), rows), :]
    for step in range(1, parts):
        peer = lax.rem(me + parts - step, parts)
        incoming(peer).wait_recv()
        total = total + held[peer]
    for step in range(1, parts):
        outgoing(lax.rem(me + step, parts)).wait_send()
    out_ref[...] = total


def scatter_sum(x, parts):
    rows = x.shape[0] // parts
    return pl.pallas_call(
        functools.partial(scatter_sum_kernel, parts),
        out_shape=jax.ShapeDtypeStruct((rows, x.shape[1]), x.dtype),
        in_specs=[pl.BlockSpec(memory_space=pltpu.VMEM)],
        out_specs=pl.BlockSpec(memory_space=pltpu.VMEM),
        scratch_shapes=[
            pltpu.VMEM((parts, rows, x.shape[1]), x.dtype),
            pltpu.SemaphoreType.DMA((parts,)),
            pltpu.SemaphoreType.DMA((parts,)),
        ],
        compiler_params=pltpu.CompilerParams(collective_id=0, has_side_effects=True),
    )(x)


def copy_kernel(x_ref, o_ref):
    o_ref[...] = x_ref[...]


def copy_rows(x, steps):
    rows = x.shape[0] // steps
    block = (rows,) + x.shape[1:]
    index = lambda i: (i,) + (0,) * (x.ndim - 1)
    return pl.pallas_call(
        copy_kernel,
        out_shape=jax.ShapeDtypeStruct(x.shape, x.dtype),
        grid=(steps,),
        in_specs=[pl.BlockSpec(block, index)],
        out_specs=pl.BlockSpec(block, index),
        cost_estimate=pl.CostEstimate(flops=0, transcendentals=0, bytes_accessed=2 * x.size * x.dtype.itemsize),
    )(x)


def body(
    tokens,
    attn_gain,
    query_gain,
    key_gain,
    moe_gain,
    query_weight,
    key_weight,
    value_weight,
    out_weight,
    gate_weight,
    up_weight,
    down_weight,
    router_weight,
    page_store,
    prompt_lengths,
    continues,
    page_owner,
    page_slot,
    routes,
):
    req_count = lax.axis_size("req")
    req_index = lax.axis_index("req")
    lane_index = lax.axis_index("tp")
    joined_local = jnp.concatenate(
        [
            query_weight.astype(jnp.bfloat16),
            key_weight.astype(jnp.bfloat16),
            value_weight.astype(jnp.bfloat16),
        ],
        axis=1,
    )
    server_qkv, server_out = (
        lax.all_gather(joined_local, "req", axis=0, tiled=True),
        lax.all_gather(out_weight.astype(jnp.bfloat16), "req", axis=1, tiled=True),
    )
    expert_count, rows_here, hidden_units = gate_weight.shape
    half_units = hidden_units // 2
    packed = jnp.concatenate(
        [
            split_halves(gate_weight.astype(jnp.bfloat16)),
            split_halves(up_weight.astype(jnp.bfloat16)),
        ],
        axis=3,
    ).reshape(2 * expert_count, rows_here, hidden_units)
    server_gate_up = lax.all_to_all(packed, ("req", "tp"), split_axis=0, concat_axis=1, tiled=True)
    group_rows, model_width = tokens.shape
    tokens_f32 = tokens.astype(jnp.float32)
    normed = rms_scale(tokens_f32, attn_gain).astype(jnp.bfloat16)
    projected = jnp.dot(normed, server_qkv, preferred_element_type=jnp.float32)
    head_dim = query_gain.shape[0]
    lane_width = server_qkv.shape[1] // 3
    lane_heads = lane_width // head_dim
    query_raw = projected[:, :lane_width].reshape(group_rows, lane_heads, head_dim)
    key_raw = projected[:, lane_width : 2 * lane_width].reshape(group_rows, lane_heads, head_dim)
    value_raw = projected[:, 2 * lane_width :]
    first_length = lax.dynamic_index_in_dim(prompt_lengths, 2 * req_index, 0, keepdims=False)
    carry_flags = lax.dynamic_slice_in_dim(continues, 2 * req_index, 2)
    row_ids = jnp.arange(group_rows, dtype=jnp.int32)
    second = (row_ids >= first_length).astype(jnp.int32)
    within = row_ids - second * first_length
    carried = jnp.where(second == 1, carry_flags[1], carry_flags[0])
    pages_per = page_owner.shape[1]
    page_rows = page_store.shape[1]
    context_len = pages_per * page_rows
    position = (within + context_len * carried).astype(jnp.float32)
    inverse = jnp.power(
        jnp.float32(rope_base), -(jnp.arange(head_dim // 2, dtype=jnp.float32) * 2.0 / head_dim)
    )
    angles = position[:, None, None] * inverse[None, None, :]
    cosine = jnp.cos(angles)
    sine_part = jnp.sin(angles)
    query_rows = rotate_half(rms_scale(query_raw, query_gain), cosine, sine_part).astype(
        jnp.bfloat16
    )
    keys_new = rotate_half(rms_scale(key_raw, key_gain), cosine, sine_part).astype(jnp.bfloat16)
    values_new = value_raw.astype(jnp.bfloat16)
    new_cache = jnp.stack([keys_new.reshape(group_rows, lane_width), values_new], axis=1)
    capacity = max(2, (pages_per + req_count - 2) // (req_count - 1))
    page_ids = jnp.arange(pages_per, dtype=jnp.int32)
    earlier = page_ids[None, :] < page_ids[:, None]
    same_owner = page_owner[:, :, None] == page_owner[:, None, :]
    page_rank = jnp.sum((same_owner & earlier[None]).astype(jnp.int32), axis=2)
    owned_here = page_owner == req_index
    chosen = owned_here[:, None, :] & (
        page_rank[:, None, :] == jnp.arange(capacity, dtype=jnp.int32)[None, :, None]
    )
    send_slot = jnp.sum(jnp.where(chosen, page_slot[:, None, :], 0), axis=2)
    page_shape = page_store.shape[1:]
    outgoing_pages = jnp.take(page_store, send_slot.reshape(-1), axis=0).reshape(
        (req_count, capacity) + page_shape
    )
    arrived_pages = lax.all_to_all(outgoing_pages, "req", split_axis=0, concat_axis=0, tiled=True)
    own_owner = jnp.take(page_owner, req_index, axis=0)
    own_rank = jnp.take(page_rank, req_index, axis=0)
    context = jnp.take(
        arrived_pages.reshape((req_count * capacity,) + page_shape),
        own_owner * capacity + own_rank,
        axis=0,
    )
    context = context.reshape(context_len, 2, lane_heads, head_dim)
    score_scale = 1.0 / math.sqrt(head_dim)
    near_scores = (
        jnp.einsum("ihc,jhc->hij", query_rows, keys_new, preferred_element_type=jnp.float32)
        * score_scale
    )
    far_scores = (
        jnp.einsum("ihc,jhc->hij", query_rows, context[:, 0], preferred_element_type=jnp.float32)
        * score_scale
    )
    same_request = second[:, None] == second[None, :]
    near_weights = jnp.where(same_request[None], jnp.exp(near_scores), jnp.float32(0.0))
    far_weights = jnp.where((carried == 1)[None, :, None], jnp.exp(far_scores), jnp.float32(0.0))
    totals = jnp.sum(near_weights, axis=2, keepdims=True) + jnp.sum(
        far_weights, axis=2, keepdims=True
    )
    near_probs = (near_weights / totals).astype(jnp.bfloat16)
    far_probs = (far_weights / totals).astype(jnp.bfloat16)
    attended = jnp.einsum(
        "hij,jhc->ihc",
        near_probs,
        values_new.reshape(group_rows, lane_heads, head_dim),
        preferred_element_type=jnp.float32,
    )
    attended = attended + jnp.einsum(
        "hij,jhc->ihc", far_probs, context[:, 1], preferred_element_type=jnp.float32
    )
    attended = attended.astype(jnp.bfloat16).reshape(group_rows, lane_width)
    shard_rows = routes.shape[0]
    row_start = lane_index * shard_rows
    qkv_out = copy_rows(server_qkv, 4)
    qkv_out, attended = lax.optimization_barrier((qkv_out, attended))
    head_terms = jnp.dot(attended, server_out, preferred_element_type=jnp.float32)
    server_gate_up, head_terms = lax.optimization_barrier((server_gate_up, head_terms))
    mixed_own = scatter_sum(head_terms, lax.axis_size("tp"))
    residual_own = lax.dynamic_slice_in_dim(tokens_f32, row_start, shard_rows, 0) + mixed_own
    moe_own = rms_scale(residual_own, moe_gain).astype(jnp.bfloat16)
    logits = jnp.dot(moe_own, router_weight, preferred_element_type=jnp.float32)
    exps = jnp.exp(logits)
    routed_exps = jnp.take_along_axis(exps, routes, axis=1)
    entry_gates = routed_exps / jnp.sum(routed_exps, axis=1, keepdims=True)
    top_count = routes.shape[1]
    slot_depth = 3 * shard_rows * top_count // (2 * expert_count)
    flat_routes = routes.reshape(-1)
    onehot = (flat_routes[:, None] == jnp.arange(expert_count, dtype=jnp.int32)[None, :]).astype(
        jnp.int32
    )
    entry_rank = jnp.sum((jnp.cumsum(onehot, axis=0) - onehot) * onehot, axis=1)
    entry_slot = (flat_routes * slot_depth + entry_rank).reshape(shard_rows, top_count)
    select_table = jnp.any(
        entry_slot[None, :, :]
        == jnp.arange(expert_count * slot_depth, dtype=jnp.int32)[:, None, None],
        axis=2,
    ).astype(jnp.bfloat16)
    outgoing_rows = jnp.dot(select_table, moe_own, preferred_element_type=jnp.float32).astype(
        jnp.bfloat16
    )
    send_rows = jnp.broadcast_to(
        outgoing_rows.reshape(expert_count, 1, slot_depth, model_width),
        (expert_count, 2, slot_depth, model_width),
    ).reshape(2 * expert_count, slot_depth, model_width)
    arrived_rows = lax.all_to_all(send_rows, ("req", "tp"), split_axis=0, concat_axis=0, tiled=True)
    both = jnp.einsum("xkd,df->xkf", arrived_rows, server_gate_up[0], preferred_element_type=jnp.float32)
    act = (jax.nn.silu(both[..., :half_units]) * both[..., half_units:]).astype(jnp.bfloat16)
    expert_rows = jnp.einsum(
        "xkf,fd->xkd", act, down_weight[0], preferred_element_type=jnp.float32
    ).astype(jnp.bfloat16)
    returned = lax.all_to_all(expert_rows, ("req", "tp"), split_axis=0, concat_axis=0, tiled=True)
    slot_weights = jnp.sum(
        jnp.where(
            entry_slot[:, :, None] == jnp.arange(expert_count * slot_depth, dtype=jnp.int32)[None, None, :],
            entry_gates[:, :, None],
            jnp.float32(0.0),
        ),
        axis=1,
    ).reshape(shard_rows, expert_count, 1, slot_depth)
    slot_weights = jnp.broadcast_to(
        slot_weights, (shard_rows, expert_count, 2, slot_depth)
    ).reshape(shard_rows, 2 * expert_count, slot_depth)
    moe_out = jnp.einsum(
        "ixk,xkd->id",
        slot_weights,
        returned.astype(jnp.float32),
        precision=lax.Precision.HIGHEST,
        preferred_element_type=jnp.float32,
    )
    hidden_rows = (residual_own + moe_out).astype(jnp.bfloat16)
    gate_up_out = copy_rows(server_gate_up.reshape(server_gate_up.shape[1:]), 4).reshape(server_gate_up.shape)
    return (qkv_out, copy_rows(server_out, 1), gate_up_out, hidden_rows, new_cache)


def solution(mesh):
    in_specs = (
        P("req", None),
        P(),
        P(),
        P(),
        P(),
        P("req", "tp"),
        P("req", "tp"),
        P("req", "tp"),
        P("tp", "req"),
        P(None, ("req", "tp"), None),
        P(None, ("req", "tp"), None),
        P(("req", "tp"), None, None),
        P(),
        P("req", None, None, "tp"),
        P(),
        P(),
        P(),
        P(),
        P(("req", "tp"), None),
    )
    out_specs = (
        P(None, "tp"),
        P("tp", None),
        P(("req", "tp"), None, None),
        P(("req", "tp"), None),
        P("req", None, "tp"),
    )
    return jax.shard_map(body, mesh=mesh, in_specs=in_specs, out_specs=out_specs, check_vma=False)
```

```python
import functools
import math

import jax
import jax.numpy as jnp
from jax import lax
from jax.experimental import pallas as pl
from jax.experimental.pallas import tpu as pltpu
from jax.sharding import PartitionSpec as P

MESH = pl.DeviceIdType.MESH

norm_eps = 1e-06
rope_base = 50000.0


def rms_scale(values, gain_vec):
    return (
        values * lax.rsqrt(jnp.mean(values * values, axis=-1, keepdims=True) + norm_eps) * gain_vec
    )


def rotate_half(values, cosine, sine_part):
    half_width = values.shape[-1] // 2
    first_half = values[..., :half_width]
    second_half = values[..., half_width:]
    return jnp.concatenate(
        [
            first_half * cosine - second_half * sine_part,
            second_half * cosine + first_half * sine_part,
        ],
        axis=-1,
    )


def split_halves(weights):
    expert_count, rows_here, hidden_units = weights.shape
    return weights.reshape(expert_count, rows_here, 2, hidden_units // 2).transpose(0, 2, 1, 3)


def scatter_sum_kernel(parts, x_ref, out_ref, held, send_sem, recv_sem):
    me = lax.axis_index("tp")
    group = lax.axis_index("req")
    rows = out_ref.shape[0]
    barrier = pltpu.get_barrier_semaphore()
    for step in range(1, parts):
        peer = lax.rem(me + step, parts)
        pl.semaphore_signal(barrier, inc=1, device_id=(group, peer), device_id_type=MESH)
    pl.semaphore_wait(barrier, parts - 1)

    def outgoing(peer):
        return pltpu.make_async_remote_copy(
            src_ref=x_ref.at[pl.ds(pl.multiple_of(peer * rows, rows), rows)],
            dst_ref=held.at[me],
            send_sem=send_sem.at[peer],
            recv_sem=recv_sem.at[me],
            device_id=(group, peer),
            device_id_type=MESH,
        )

    def incoming(peer):
        return pltpu.make_async_remote_copy(
            src_ref=x_ref.at[pl.ds(pl.multiple_of(me * rows, rows), rows)],
            dst_ref=held.at[peer],
            send_sem=send_sem.at[peer],
            recv_sem=recv_sem.at[peer],
            device_id=(group, peer),
            device_id_type=MESH,
        )

    for step in range(1, parts):
        outgoing(lax.rem(me + step, parts)).start()
    total = x_ref[pl.ds(pl.multiple_of(me * rows, rows), rows), :]
    for step in range(1, parts):
        peer = lax.rem(me + parts - step, parts)
        incoming(peer).wait_recv()
        total = total + held[peer]
    for step in range(1, parts):
        outgoing(lax.rem(me + step, parts)).wait_send()
    out_ref[...] = total


def scatter_sum(x, parts):
    rows = x.shape[0] // parts
    return pl.pallas_call(
        functools.partial(scatter_sum_kernel, parts),
        out_shape=jax.ShapeDtypeStruct((rows, x.shape[1]), x.dtype),
        in_specs=[pl.BlockSpec(memory_space=pltpu.VMEM)],
        out_specs=pl.BlockSpec(memory_space=pltpu.VMEM),
        scratch_shapes=[
            pltpu.VMEM((parts, rows, x.shape[1]), x.dtype),
            pltpu.SemaphoreType.DMA((parts,)),
            pltpu.SemaphoreType.DMA((parts,)),
        ],
        compiler_params=pltpu.CompilerParams(collective_id=0, has_side_effects=True),
    )(x)


def copy_kernel(x_ref, o_ref):
    o_ref[...] = x_ref[...]


def copy_rows(x, steps):
    rows = x.shape[0] // steps
    block = (rows,) + x.shape[1:]
    index = lambda i: (i,) + (0,) * (x.ndim - 1)
    return pl.pallas_call(
        copy_kernel,
        out_shape=jax.ShapeDtypeStruct(x.shape, x.dtype),
        grid=(steps,),
        in_specs=[pl.BlockSpec(block, index)],
        out_specs=pl.BlockSpec(block, index),
        cost_estimate=pl.CostEstimate(flops=0, transcendentals=0, bytes_accessed=2 * x.size * x.dtype.itemsize),
    )(x)


def copy_columns(x, width, steps):
    rows = x.shape[0] // steps
    return pl.pallas_call(
        copy_kernel,
        out_shape=jax.ShapeDtypeStruct((x.shape[0], width), x.dtype),
        grid=(steps,),
        in_specs=[pl.BlockSpec((rows, width), lambda i: (i, 0))],
        out_specs=pl.BlockSpec((rows, width), lambda i: (i, 0)),
        cost_estimate=pl.CostEstimate(flops=0, transcendentals=0, bytes_accessed=2 * x.shape[0] * width * x.dtype.itemsize),
    )(x)


def body(
    tokens,
    attn_gain,
    query_gain,
    key_gain,
    moe_gain,
    query_weight,
    key_weight,
    value_weight,
    out_weight,
    gate_weight,
    up_weight,
    down_weight,
    router_weight,
    page_store,
    prompt_lengths,
    continues,
    page_owner,
    page_slot,
    routes,
):
    req_count = lax.axis_size("req")
    req_index = lax.axis_index("req")
    lane_index = lax.axis_index("tp")
    joined_local = jnp.concatenate(
        [
            query_weight.astype(jnp.bfloat16),
            key_weight.astype(jnp.bfloat16),
            value_weight.astype(jnp.bfloat16),
        ],
        axis=1,
    )
    out_block = out_weight.astype(jnp.bfloat16)
    qkv_width = joined_local.shape[1]
    out_rows, out_cols = out_block.shape
    group_rows_w = joined_local.shape[0]
    gathered = lax.all_gather(
        jnp.concatenate([joined_local, out_block.reshape(group_rows_w, -1)], axis=1), "req", axis=0, tiled=True
    )
    server_qkv = gathered[:, :qkv_width]
    server_out = (
        gathered[:, qkv_width:]
        .reshape(req_count, out_rows, out_cols)
        .transpose(1, 0, 2)
        .reshape(out_rows, req_count * out_cols)
    )
    expert_count, rows_here, hidden_units = gate_weight.shape
    half_units = hidden_units // 2
    packed = jnp.concatenate(
        [
            split_halves(gate_weight.astype(jnp.bfloat16)),
            split_halves(up_weight.astype(jnp.bfloat16)),
        ],
        axis=3,
    ).reshape(2 * expert_count, rows_here, hidden_units)
    server_gate_up = lax.all_to_all(packed, ("req", "tp"), split_axis=0, concat_axis=1, tiled=True)
    group_rows, model_width = tokens.shape
    tokens_f32 = tokens.astype(jnp.float32)
    normed = rms_scale(tokens_f32, attn_gain).astype(jnp.bfloat16)
    projected = jnp.dot(normed, server_qkv, preferred_element_type=jnp.float32)
    head_dim = query_gain.shape[0]
    lane_width = server_qkv.shape[1] // 3
    lane_heads = lane_width // head_dim
    query_raw = projected[:, :lane_width].reshape(group_rows, lane_heads, head_dim)
    key_raw = projected[:, lane_width : 2 * lane_width].reshape(group_rows, lane_heads, head_dim)
    value_raw = projected[:, 2 * lane_width :]
    first_length = lax.dynamic_index_in_dim(prompt_lengths, 2 * req_index, 0, keepdims=False)
    carry_flags = lax.dynamic_slice_in_dim(continues, 2 * req_index, 2)
    row_ids = jnp.arange(group_rows, dtype=jnp.int32)
    second = (row_ids >= first_length).astype(jnp.int32)
    within = row_ids - second * first_length
    carried = jnp.where(second == 1, carry_flags[1], carry_flags[0])
    pages_per = page_owner.shape[1]
    page_rows = page_store.shape[1]
    context_len = pages_per * page_rows
    position = (within + context_len * carried).astype(jnp.float32)
    inverse = jnp.power(
        jnp.float32(rope_base), -(jnp.arange(head_dim // 2, dtype=jnp.float32) * 2.0 / head_dim)
    )
    angles = position[:, None, None] * inverse[None, None, :]
    cosine = jnp.cos(angles)
    sine_part = jnp.sin(angles)
    query_rows = rotate_half(rms_scale(query_raw, query_gain), cosine, sine_part).astype(
        jnp.bfloat16
    )
    keys_new = rotate_half(rms_scale(key_raw, key_gain), cosine, sine_part).astype(jnp.bfloat16)
    values_new = value_raw.astype(jnp.bfloat16)
    new_cache = jnp.stack([keys_new.reshape(group_rows, lane_width), values_new], axis=1)
    capacity = max(2, (pages_per + req_count - 2) // (req_count - 1))
    page_ids = jnp.arange(pages_per, dtype=jnp.int32)
    earlier = page_ids[None, :] < page_ids[:, None]
    same_owner = page_owner[:, :, None] == page_owner[:, None, :]
    page_rank = jnp.sum((same_owner & earlier[None]).astype(jnp.int32), axis=2)
    owned_here = page_owner == req_index
    chosen = owned_here[:, None, :] & (
        page_rank[:, None, :] == jnp.arange(capacity, dtype=jnp.int32)[None, :, None]
    )
    send_slot = jnp.sum(jnp.where(chosen, page_slot[:, None, :], 0), axis=2)
    page_shape = page_store.shape[1:]
    outgoing_pages = jnp.take(page_store, send_slot.reshape(-1), axis=0).reshape(
        (req_count, capacity) + page_shape
    )
    arrived_pages = lax.all_to_all(outgoing_pages, "req", split_axis=0, concat_axis=0, tiled=True)
    own_owner = jnp.take(page_owner, req_index, axis=0)
    own_rank = jnp.take(page_rank, req_index, axis=0)
    context = jnp.take(
        arrived_pages.reshape((req_count * capacity,) + page_shape),
        own_owner * capacity + own_rank,
        axis=0,
    )
    context = context.reshape(context_len, 2, lane_heads, head_dim)
    score_scale = 1.0 / math.sqrt(head_dim)
    near_scores = (
        jnp.einsum("ihc,jhc->hij", query_rows, keys_new, preferred_element_type=jnp.float32)
        * score_scale
    )
    far_scores = (
        jnp.einsum("ihc,jhc->hij", query_rows, context[:, 0], preferred_element_type=jnp.float32)
        * score_scale
    )
    same_request = second[:, None] == second[None, :]
    near_weights = jnp.where(same_request[None], jnp.exp(near_scores), jnp.float32(0.0))
    far_weights = jnp.where((carried == 1)[None, :, None], jnp.exp(far_scores), jnp.float32(0.0))
    totals = jnp.sum(near_weights, axis=2, keepdims=True) + jnp.sum(
        far_weights, axis=2, keepdims=True
    )
    near_probs = (near_weights / totals).astype(jnp.bfloat16)
    far_probs = (far_weights / totals).astype(jnp.bfloat16)
    attended = jnp.einsum(
        "hij,jhc->ihc",
        near_probs,
        values_new.reshape(group_rows, lane_heads, head_dim),
        preferred_element_type=jnp.float32,
    )
    attended = attended + jnp.einsum(
        "hij,jhc->ihc", far_probs, context[:, 1], preferred_element_type=jnp.float32
    )
    attended = attended.astype(jnp.bfloat16).reshape(group_rows, lane_width)
    shard_rows = routes.shape[0]
    row_start = lane_index * shard_rows
    qkv_out = copy_columns(gathered, qkv_width, 4)
    qkv_out, attended = lax.optimization_barrier((qkv_out, attended))
    head_terms = jnp.dot(attended, server_out, preferred_element_type=jnp.float32)
    server_gate_up, head_terms = lax.optimization_barrier((server_gate_up, head_terms))
    mixed_own = scatter_sum(head_terms, lax.axis_size("tp"))
    residual_own = lax.dynamic_slice_in_dim(tokens_f32, row_start, shard_rows, 0) + mixed_own
    moe_own = rms_scale(residual_own, moe_gain).astype(jnp.bfloat16)
    logits = jnp.dot(moe_own, router_weight, preferred_element_type=jnp.float32)
    exps = jnp.exp(logits)
    routed_exps = jnp.take_along_axis(exps, routes, axis=1)
    entry_gates = routed_exps / jnp.sum(routed_exps, axis=1, keepdims=True)
    top_count = routes.shape[1]
    slot_depth = 3 * shard_rows * top_count // (2 * expert_count)
    flat_routes = routes.reshape(-1)
    onehot = (flat_routes[:, None] == jnp.arange(expert_count, dtype=jnp.int32)[None, :]).astype(
        jnp.int32
    )
    entry_rank = jnp.sum((jnp.cumsum(onehot, axis=0) - onehot) * onehot, axis=1)
    entry_slot = (flat_routes * slot_depth + entry_rank).reshape(shard_rows, top_count)
    select_table = jnp.any(
        entry_slot[None, :, :]
        == jnp.arange(expert_count * slot_depth, dtype=jnp.int32)[:, None, None],
        axis=2,
    ).astype(jnp.bfloat16)
    outgoing_rows = jnp.dot(select_table, moe_own, preferred_element_type=jnp.float32).astype(
        jnp.bfloat16
    )
    send_rows = jnp.broadcast_to(
        outgoing_rows.reshape(expert_count, 1, slot_depth, model_width),
        (expert_count, 2, slot_depth, model_width),
    ).reshape(2 * expert_count, slot_depth, model_width)
    arrived_rows = lax.all_to_all(send_rows, ("req", "tp"), split_axis=0, concat_axis=0, tiled=True)
    both = jnp.einsum("xkd,df->xkf", arrived_rows, server_gate_up[0], preferred_element_type=jnp.float32)
    act = (jax.nn.silu(both[..., :half_units]) * both[..., half_units:]).astype(jnp.bfloat16)
    expert_rows = jnp.einsum(
        "xkf,fd->xkd", act, down_weight[0], preferred_element_type=jnp.float32
    ).astype(jnp.bfloat16)
    returned = lax.all_to_all(expert_rows, ("req", "tp"), split_axis=0, concat_axis=0, tiled=True)
    slot_weights = jnp.sum(
        jnp.where(
            entry_slot[:, :, None] == jnp.arange(expert_count * slot_depth, dtype=jnp.int32)[None, None, :],
            entry_gates[:, :, None],
            jnp.float32(0.0),
        ),
        axis=1,
    ).reshape(shard_rows, expert_count, 1, slot_depth)
    slot_weights = jnp.broadcast_to(
        slot_weights, (shard_rows, expert_count, 2, slot_depth)
    ).reshape(shard_rows, 2 * expert_count, slot_depth)
    moe_out = jnp.einsum(
        "ixk,xkd->id",
        slot_weights,
        returned.astype(jnp.float32),
        precision=lax.Precision.HIGHEST,
        preferred_element_type=jnp.float32,
    )
    hidden_rows = (residual_own + moe_out).astype(jnp.bfloat16)
    gate_up_out = copy_rows(server_gate_up.reshape(server_gate_up.shape[1:]), 4).reshape(server_gate_up.shape)
    return (qkv_out, copy_rows(server_out, 1), gate_up_out, hidden_rows, new_cache)


def solution(mesh):
    in_specs = (
        P("req", None),
        P(),
        P(),
        P(),
        P(),
        P("req", "tp"),
        P("req", "tp"),
        P("req", "tp"),
        P("tp", "req"),
        P(None, ("req", "tp"), None),
        P(None, ("req", "tp"), None),
        P(("req", "tp"), None, None),
        P(),
        P("req", None, None, "tp"),
        P(),
        P(),
        P(),
        P(),
        P(("req", "tp"), None),
    )
    out_specs = (
        P(None, "tp"),
        P("tp", None),
        P(("req", "tp"), None, None),
        P(("req", "tp"), None),
        P("req", None, "tp"),
    )
    return jax.shard_map(body, mesh=mesh, in_specs=in_specs, out_specs=out_specs, check_vma=False)
```

```python
import functools
import math

import jax
import jax.numpy as jnp
from jax import lax
from jax.experimental import pallas as pl
from jax.experimental.pallas import tpu as pltpu
from jax.sharding import PartitionSpec as P

MESH = pl.DeviceIdType.MESH

norm_eps = 1e-06
rope_base = 50000.0


def rms_scale(values, gain_vec):
    return (
        values * lax.rsqrt(jnp.mean(values * values, axis=-1, keepdims=True) + norm_eps) * gain_vec
    )


def rotate_half(values, cosine, sine_part):
    half_width = values.shape[-1] // 2
    first_half = values[..., :half_width]
    second_half = values[..., half_width:]
    return jnp.concatenate(
        [
            first_half * cosine - second_half * sine_part,
            second_half * cosine + first_half * sine_part,
        ],
        axis=-1,
    )


def split_halves(weights):
    expert_count, rows_here, hidden_units = weights.shape
    return weights.reshape(expert_count, rows_here, 2, hidden_units // 2).transpose(0, 2, 1, 3)


def scatter_sum_kernel(parts, x_ref, out_ref, held, send_sem, recv_sem):
    me = lax.axis_index("tp")
    group = lax.axis_index("req")
    rows = out_ref.shape[0]
    barrier = pltpu.get_barrier_semaphore()
    for step in range(1, parts):
        peer = lax.rem(me + step, parts)
        pl.semaphore_signal(barrier, inc=1, device_id=(group, peer), device_id_type=MESH)
    pl.semaphore_wait(barrier, parts - 1)

    def outgoing(peer):
        return pltpu.make_async_remote_copy(
            src_ref=x_ref.at[pl.ds(pl.multiple_of(peer * rows, rows), rows)],
            dst_ref=held.at[me],
            send_sem=send_sem.at[peer],
            recv_sem=recv_sem.at[me],
            device_id=(group, peer),
            device_id_type=MESH,
        )

    def incoming(peer):
        return pltpu.make_async_remote_copy(
            src_ref=x_ref.at[pl.ds(pl.multiple_of(me * rows, rows), rows)],
            dst_ref=held.at[peer],
            send_sem=send_sem.at[peer],
            recv_sem=recv_sem.at[peer],
            device_id=(group, peer),
            device_id_type=MESH,
        )

    for step in range(1, parts):
        outgoing(lax.rem(me + step, parts)).start()
    total = x_ref[pl.ds(pl.multiple_of(me * rows, rows), rows), :]
    for step in range(1, parts):
        peer = lax.rem(me + parts - step, parts)
        incoming(peer).wait_recv()
        total = total + held[peer]
    for step in range(1, parts):
        outgoing(lax.rem(me + step, parts)).wait_send()
    out_ref[...] = total


def scatter_sum(x, parts):
    rows = x.shape[0] // parts
    return pl.pallas_call(
        functools.partial(scatter_sum_kernel, parts),
        out_shape=jax.ShapeDtypeStruct((rows, x.shape[1]), x.dtype),
        in_specs=[pl.BlockSpec(memory_space=pltpu.VMEM)],
        out_specs=pl.BlockSpec(memory_space=pltpu.VMEM),
        scratch_shapes=[
            pltpu.VMEM((parts, rows, x.shape[1]), x.dtype),
            pltpu.SemaphoreType.DMA((parts,)),
            pltpu.SemaphoreType.DMA((parts,)),
        ],
        compiler_params=pltpu.CompilerParams(collective_id=0, has_side_effects=True),
    )(x)


def copy_kernel(x_ref, o_ref):
    o_ref[...] = x_ref[...]


def copy_rows(x, steps):
    rows = x.shape[0] // steps
    block = (rows,) + x.shape[1:]
    index = lambda i: (i,) + (0,) * (x.ndim - 1)
    return pl.pallas_call(
        copy_kernel,
        out_shape=jax.ShapeDtypeStruct(x.shape, x.dtype),
        grid=(steps,),
        in_specs=[pl.BlockSpec(block, index)],
        out_specs=pl.BlockSpec(block, index),
        cost_estimate=pl.CostEstimate(flops=0, transcendentals=0, bytes_accessed=2 * x.size * x.dtype.itemsize),
    )(x)


def copy_columns(x, width, steps):
    rows = x.shape[0] // steps
    return pl.pallas_call(
        copy_kernel,
        out_shape=jax.ShapeDtypeStruct((x.shape[0], width), x.dtype),
        grid=(steps,),
        in_specs=[pl.BlockSpec((rows, width), lambda i: (i, 0))],
        out_specs=pl.BlockSpec((rows, width), lambda i: (i, 0)),
        cost_estimate=pl.CostEstimate(flops=0, transcendentals=0, bytes_accessed=2 * x.shape[0] * width * x.dtype.itemsize),
    )(x)


def body(
    tokens,
    attn_gain,
    query_gain,
    key_gain,
    moe_gain,
    query_weight,
    key_weight,
    value_weight,
    out_weight,
    gate_weight,
    up_weight,
    down_weight,
    router_weight,
    page_store,
    prompt_lengths,
    continues,
    page_owner,
    page_slot,
    routes,
):
    req_count = lax.axis_size("req")
    req_index = lax.axis_index("req")
    lane_index = lax.axis_index("tp")
    joined_local = jnp.concatenate(
        [
            query_weight.astype(jnp.bfloat16),
            key_weight.astype(jnp.bfloat16),
            value_weight.astype(jnp.bfloat16),
        ],
        axis=1,
    )
    out_block = out_weight.astype(jnp.bfloat16)
    qkv_width = joined_local.shape[1]
    out_rows, out_cols = out_block.shape
    group_rows_w = joined_local.shape[0]
    gathered = lax.all_gather(
        jnp.concatenate([joined_local, out_block.reshape(group_rows_w, -1)], axis=1), "req", axis=0, tiled=True
    )
    server_qkv = gathered[:, :qkv_width]
    server_out = (
        gathered[:, qkv_width:]
        .reshape(req_count, out_rows, out_cols)
        .transpose(1, 0, 2)
        .reshape(out_rows, req_count * out_cols)
    )
    expert_count, rows_here, hidden_units = gate_weight.shape
    half_units = hidden_units // 2
    packed = jnp.concatenate(
        [
            split_halves(gate_weight.astype(jnp.bfloat16)),
            split_halves(up_weight.astype(jnp.bfloat16)),
        ],
        axis=3,
    ).reshape(2 * expert_count, rows_here, hidden_units)
    server_gate_up = lax.all_to_all(packed, ("req", "tp"), split_axis=0, concat_axis=1, tiled=True)
    group_rows, model_width = tokens.shape
    tokens_f32 = tokens.astype(jnp.float32)
    normed = rms_scale(tokens_f32, attn_gain).astype(jnp.bfloat16)
    projected = jnp.dot(normed, server_qkv, preferred_element_type=jnp.float32)
    head_dim = query_gain.shape[0]
    lane_width = server_qkv.shape[1] // 3
    lane_heads = lane_width // head_dim
    query_raw = projected[:, :lane_width].reshape(group_rows, lane_heads, head_dim)
    key_raw = projected[:, lane_width : 2 * lane_width].reshape(group_rows, lane_heads, head_dim)
    value_raw = projected[:, 2 * lane_width :]
    first_length = lax.dynamic_index_in_dim(prompt_lengths, 2 * req_index, 0, keepdims=False)
    carry_flags = lax.dynamic_slice_in_dim(continues, 2 * req_index, 2)
    row_ids = jnp.arange(group_rows, dtype=jnp.int32)
    second = (row_ids >= first_length).astype(jnp.int32)
    within = row_ids - second * first_length
    carried = jnp.where(second == 1, carry_flags[1], carry_flags[0])
    pages_per = page_owner.shape[1]
    page_rows = page_store.shape[1]
    context_len = pages_per * page_rows
    position = (within + context_len * carried).astype(jnp.float32)
    inverse = jnp.power(
        jnp.float32(rope_base), -(jnp.arange(head_dim // 2, dtype=jnp.float32) * 2.0 / head_dim)
    )
    angles = position[:, None, None] * inverse[None, None, :]
    cosine = jnp.cos(angles)
    sine_part = jnp.sin(angles)
    query_rows = rotate_half(rms_scale(query_raw, query_gain), cosine, sine_part).astype(
        jnp.bfloat16
    )
    keys_new = rotate_half(rms_scale(key_raw, key_gain), cosine, sine_part).astype(jnp.bfloat16)
    values_new = value_raw.astype(jnp.bfloat16)
    new_cache = jnp.stack([keys_new.reshape(group_rows, lane_width), values_new], axis=1)
    capacity = max(2, (pages_per + req_count - 2) // (req_count - 1))
    page_ids = jnp.arange(pages_per, dtype=jnp.int32)
    earlier = page_ids[None, :] < page_ids[:, None]
    same_owner = page_owner[:, :, None] == page_owner[:, None, :]
    page_rank = jnp.sum((same_owner & earlier[None]).astype(jnp.int32), axis=2)
    owned_here = page_owner == req_index
    chosen = owned_here[:, None, :] & (
        page_rank[:, None, :] == jnp.arange(capacity, dtype=jnp.int32)[None, :, None]
    )
    send_slot = jnp.sum(jnp.where(chosen, page_slot[:, None, :], 0), axis=2)
    page_shape = page_store.shape[1:]
    outgoing_pages = jnp.take(page_store, send_slot.reshape(-1), axis=0).reshape(
        (req_count, capacity) + page_shape
    )
    arrived_pages = lax.all_to_all(outgoing_pages, "req", split_axis=0, concat_axis=0, tiled=True)
    own_owner = jnp.take(page_owner, req_index, axis=0)
    own_rank = jnp.take(page_rank, req_index, axis=0)
    context = jnp.take(
        arrived_pages.reshape((req_count * capacity,) + page_shape),
        own_owner * capacity + own_rank,
        axis=0,
    )
    context = context.reshape(context_len, 2, lane_heads, head_dim)
    score_scale = 1.0 / math.sqrt(head_dim)
    near_scores = (
        jnp.einsum("ihc,jhc->hij", query_rows, keys_new, preferred_element_type=jnp.float32)
        * score_scale
    )
    far_scores = (
        jnp.einsum("ihc,jhc->hij", query_rows, context[:, 0], preferred_element_type=jnp.float32)
        * score_scale
    )
    same_request = second[:, None] == second[None, :]
    near_weights = jnp.where(same_request[None], jnp.exp(near_scores), jnp.float32(0.0))
    far_weights = jnp.where((carried == 1)[None, :, None], jnp.exp(far_scores), jnp.float32(0.0))
    totals = jnp.sum(near_weights, axis=2, keepdims=True) + jnp.sum(
        far_weights, axis=2, keepdims=True
    )
    near_probs = (near_weights / totals).astype(jnp.bfloat16)
    far_probs = (far_weights / totals).astype(jnp.bfloat16)
    attended = jnp.einsum(
        "hij,jhc->ihc",
        near_probs,
        values_new.reshape(group_rows, lane_heads, head_dim),
        preferred_element_type=jnp.float32,
    )
    attended = attended + jnp.einsum(
        "hij,jhc->ihc", far_probs, context[:, 1], preferred_element_type=jnp.float32
    )
    attended = attended.astype(jnp.bfloat16).reshape(group_rows, lane_width)
    shard_rows = routes.shape[0]
    row_start = lane_index * shard_rows
    qkv_out = copy_columns(gathered, qkv_width, 4)
    qkv_out, attended = lax.optimization_barrier((qkv_out, attended))
    head_terms = jnp.dot(attended, server_out, preferred_element_type=jnp.float32)
    mixed_own = scatter_sum(head_terms, lax.axis_size("tp"))
    residual_own = lax.dynamic_slice_in_dim(tokens_f32, row_start, shard_rows, 0) + mixed_own
    moe_own = rms_scale(residual_own, moe_gain).astype(jnp.bfloat16)
    logits = jnp.dot(moe_own, router_weight, preferred_element_type=jnp.float32)
    exps = jnp.exp(logits)
    routed_exps = jnp.take_along_axis(exps, routes, axis=1)
    entry_gates = routed_exps / jnp.sum(routed_exps, axis=1, keepdims=True)
    top_count = routes.shape[1]
    slot_depth = 3 * shard_rows * top_count // (2 * expert_count)
    flat_routes = routes.reshape(-1)
    onehot = (flat_routes[:, None] == jnp.arange(expert_count, dtype=jnp.int32)[None, :]).astype(
        jnp.int32
    )
    entry_rank = jnp.sum((jnp.cumsum(onehot, axis=0) - onehot) * onehot, axis=1)
    entry_slot = (flat_routes * slot_depth + entry_rank).reshape(shard_rows, top_count)
    select_table = jnp.any(
        entry_slot[None, :, :]
        == jnp.arange(expert_count * slot_depth, dtype=jnp.int32)[:, None, None],
        axis=2,
    ).astype(jnp.bfloat16)
    outgoing_rows = jnp.dot(select_table, moe_own, preferred_element_type=jnp.float32).astype(
        jnp.bfloat16
    )
    send_rows = jnp.broadcast_to(
        outgoing_rows.reshape(expert_count, 1, slot_depth, model_width),
        (expert_count, 2, slot_depth, model_width),
    ).reshape(2 * expert_count, slot_depth, model_width)
    server_gate_up, send_rows = lax.optimization_barrier((server_gate_up, send_rows))
    arrived_rows = lax.all_to_all(send_rows, ("req", "tp"), split_axis=0, concat_axis=0, tiled=True)
    both = jnp.einsum("xkd,df->xkf", arrived_rows, server_gate_up[0], preferred_element_type=jnp.float32)
    act = (jax.nn.silu(both[..., :half_units]) * both[..., half_units:]).astype(jnp.bfloat16)
    expert_rows = jnp.einsum(
        "xkf,fd->xkd", act, down_weight[0], preferred_element_type=jnp.float32
    ).astype(jnp.bfloat16)
    returned = lax.all_to_all(expert_rows, ("req", "tp"), split_axis=0, concat_axis=0, tiled=True)
    slot_weights = jnp.sum(
        jnp.where(
            entry_slot[:, :, None] == jnp.arange(expert_count * slot_depth, dtype=jnp.int32)[None, None, :],
            entry_gates[:, :, None],
            jnp.float32(0.0),
        ),
        axis=1,
    ).reshape(shard_rows, expert_count, 1, slot_depth)
    slot_weights = jnp.broadcast_to(
        slot_weights, (shard_rows, expert_count, 2, slot_depth)
    ).reshape(shard_rows, 2 * expert_count, slot_depth)
    moe_out = jnp.einsum(
        "ixk,xkd->id",
        slot_weights,
        returned.astype(jnp.float32),
        precision=lax.Precision.HIGHEST,
        preferred_element_type=jnp.float32,
    )
    hidden_rows = (residual_own + moe_out).astype(jnp.bfloat16)
    gate_up_out = copy_rows(server_gate_up.reshape(server_gate_up.shape[1:]), 4).reshape(server_gate_up.shape)
    return (qkv_out, copy_rows(server_out, 1), gate_up_out, hidden_rows, new_cache)


def solution(mesh):
    in_specs = (
        P("req", None),
        P(),
        P(),
        P(),
        P(),
        P("req", "tp"),
        P("req", "tp"),
        P("req", "tp"),
        P("tp", "req"),
        P(None, ("req", "tp"), None),
        P(None, ("req", "tp"), None),
        P(("req", "tp"), None, None),
        P(),
        P("req", None, None, "tp"),
        P(),
        P(),
        P(),
        P(),
        P(("req", "tp"), None),
    )
    out_specs = (
        P(None, "tp"),
        P("tp", None),
        P(("req", "tp"), None, None),
        P(("req", "tp"), None),
        P("req", None, "tp"),
    )
    return jax.shard_map(body, mesh=mesh, in_specs=in_specs, out_specs=out_specs, check_vma=False)
```

```python
import functools
import math

import jax
import jax.numpy as jnp
from jax import lax
from jax.experimental import pallas as pl
from jax.experimental.pallas import tpu as pltpu
from jax.sharding import PartitionSpec as P

MESH = pl.DeviceIdType.MESH

norm_eps = 1e-06
rope_base = 50000.0


def rms_scale(values, gain_vec):
    return (
        values * lax.rsqrt(jnp.mean(values * values, axis=-1, keepdims=True) + norm_eps) * gain_vec
    )


def rotate_half(values, cosine, sine_part):
    half_width = values.shape[-1] // 2
    first_half = values[..., :half_width]
    second_half = values[..., half_width:]
    return jnp.concatenate(
        [
            first_half * cosine - second_half * sine_part,
            second_half * cosine + first_half * sine_part,
        ],
        axis=-1,
    )


def split_halves(weights):
    expert_count, rows_here, hidden_units = weights.shape
    return weights.reshape(expert_count, rows_here, 2, hidden_units // 2).transpose(0, 2, 1, 3)


def scatter_sum_kernel(parts, x_ref, out_ref, held, send_sem, recv_sem):
    me = lax.axis_index("tp")
    group = lax.axis_index("req")
    rows = out_ref.shape[0]
    barrier = pltpu.get_barrier_semaphore()
    for step in range(1, parts):
        peer = lax.rem(me + step, parts)
        pl.semaphore_signal(barrier, inc=1, device_id=(group, peer), device_id_type=MESH)
    pl.semaphore_wait(barrier, parts - 1)

    def outgoing(peer):
        return pltpu.make_async_remote_copy(
            src_ref=x_ref.at[pl.ds(pl.multiple_of(peer * rows, rows), rows)],
            dst_ref=held.at[me],
            send_sem=send_sem.at[peer],
            recv_sem=recv_sem.at[me],
            device_id=(group, peer),
            device_id_type=MESH,
        )

    def incoming(peer):
        return pltpu.make_async_remote_copy(
            src_ref=x_ref.at[pl.ds(pl.multiple_of(me * rows, rows), rows)],
            dst_ref=held.at[peer],
            send_sem=send_sem.at[peer],
            recv_sem=recv_sem.at[peer],
            device_id=(group, peer),
            device_id_type=MESH,
        )

    for step in range(1, parts):
        outgoing(lax.rem(me + step, parts)).start()
    total = x_ref[pl.ds(pl.multiple_of(me * rows, rows), rows), :]
    for step in range(1, parts):
        peer = lax.rem(me + parts - step, parts)
        incoming(peer).wait_recv()
        total = total + held[peer]
    for step in range(1, parts):
        outgoing(lax.rem(me + step, parts)).wait_send()
    out_ref[...] = total


def scatter_sum(x, parts):
    rows = x.shape[0] // parts
    return pl.pallas_call(
        functools.partial(scatter_sum_kernel, parts),
        out_shape=jax.ShapeDtypeStruct((rows, x.shape[1]), x.dtype),
        in_specs=[pl.BlockSpec(memory_space=pltpu.VMEM)],
        out_specs=pl.BlockSpec(memory_space=pltpu.VMEM),
        scratch_shapes=[
            pltpu.VMEM((parts, rows, x.shape[1]), x.dtype),
            pltpu.SemaphoreType.DMA((parts,)),
            pltpu.SemaphoreType.DMA((parts,)),
        ],
        compiler_params=pltpu.CompilerParams(collective_id=0, has_side_effects=True),
    )(x)


def copy_kernel(x_ref, o_ref):
    o_ref[...] = x_ref[...]


def copy_rows(x, steps):
    rows = x.shape[0] // steps
    block = (rows,) + x.shape[1:]
    index = lambda i: (i,) + (0,) * (x.ndim - 1)
    return pl.pallas_call(
        copy_kernel,
        out_shape=jax.ShapeDtypeStruct(x.shape, x.dtype),
        grid=(steps,),
        in_specs=[pl.BlockSpec(block, index)],
        out_specs=pl.BlockSpec(block, index),
        cost_estimate=pl.CostEstimate(flops=0, transcendentals=0, bytes_accessed=2 * x.size * x.dtype.itemsize),
    )(x)


def copy_columns(x, width, steps):
    rows = x.shape[0] // steps
    return pl.pallas_call(
        copy_kernel,
        out_shape=jax.ShapeDtypeStruct((x.shape[0], width), x.dtype),
        grid=(steps,),
        in_specs=[pl.BlockSpec((rows, width), lambda i: (i, 0))],
        out_specs=pl.BlockSpec((rows, width), lambda i: (i, 0)),
        cost_estimate=pl.CostEstimate(flops=0, transcendentals=0, bytes_accessed=2 * x.shape[0] * width * x.dtype.itemsize),
    )(x)


def body(
    tokens,
    attn_gain,
    query_gain,
    key_gain,
    moe_gain,
    query_weight,
    key_weight,
    value_weight,
    out_weight,
    gate_weight,
    up_weight,
    down_weight,
    router_weight,
    page_store,
    prompt_lengths,
    continues,
    page_owner,
    page_slot,
    routes,
):
    req_count = lax.axis_size("req")
    req_index = lax.axis_index("req")
    lane_index = lax.axis_index("tp")
    joined_local = jnp.concatenate(
        [
            query_weight.astype(jnp.bfloat16),
            key_weight.astype(jnp.bfloat16),
            value_weight.astype(jnp.bfloat16),
        ],
        axis=1,
    )
    out_block = out_weight.astype(jnp.bfloat16)
    qkv_width = joined_local.shape[1]
    out_rows, out_cols = out_block.shape
    group_rows_w = joined_local.shape[0]
    gathered = lax.all_gather(
        jnp.concatenate([joined_local, out_block.reshape(group_rows_w, -1)], axis=1), "req", axis=0, tiled=True
    )
    server_qkv = gathered[:, :qkv_width]
    server_out = (
        gathered[:, qkv_width:]
        .reshape(req_count, out_rows, out_cols)
        .transpose(1, 0, 2)
        .reshape(out_rows, req_count * out_cols)
    )
    expert_count, rows_here, hidden_units = gate_weight.shape
    half_units = hidden_units // 2
    packed = jnp.concatenate(
        [
            split_halves(gate_weight.astype(jnp.bfloat16)),
            split_halves(up_weight.astype(jnp.bfloat16)),
        ],
        axis=3,
    ).reshape(2 * expert_count, rows_here, hidden_units)
    server_gate_up = lax.all_to_all(packed, ("req", "tp"), split_axis=0, concat_axis=1, tiled=True)
    group_rows, model_width = tokens.shape
    tokens_f32 = tokens.astype(jnp.float32)
    normed = rms_scale(tokens_f32, attn_gain).astype(jnp.bfloat16)
    projected = jnp.dot(normed, server_qkv, preferred_element_type=jnp.float32)
    head_dim = query_gain.shape[0]
    lane_width = server_qkv.shape[1] // 3
    lane_heads = lane_width // head_dim
    query_raw = projected[:, :lane_width].reshape(group_rows, lane_heads, head_dim)
    key_raw = projected[:, lane_width : 2 * lane_width].reshape(group_rows, lane_heads, head_dim)
    value_raw = projected[:, 2 * lane_width :]
    first_length = lax.dynamic_index_in_dim(prompt_lengths, 2 * req_index, 0, keepdims=False)
    carry_flags = lax.dynamic_slice_in_dim(continues, 2 * req_index, 2)
    row_ids = jnp.arange(group_rows, dtype=jnp.int32)
    second = (row_ids >= first_length).astype(jnp.int32)
    within = row_ids - second * first_length
    carried = jnp.where(second == 1, carry_flags[1], carry_flags[0])
    pages_per = page_owner.shape[1]
    page_rows = page_store.shape[1]
    context_len = pages_per * page_rows
    position = (within + context_len * carried).astype(jnp.float32)
    inverse = jnp.power(
        jnp.float32(rope_base), -(jnp.arange(head_dim // 2, dtype=jnp.float32) * 2.0 / head_dim)
    )
    angles = position[:, None, None] * inverse[None, None, :]
    cosine = jnp.cos(angles)
    sine_part = jnp.sin(angles)
    query_rows = rotate_half(rms_scale(query_raw, query_gain), cosine, sine_part).astype(
        jnp.bfloat16
    )
    keys_new = rotate_half(rms_scale(key_raw, key_gain), cosine, sine_part).astype(jnp.bfloat16)
    values_new = value_raw.astype(jnp.bfloat16)
    new_cache = jnp.stack([keys_new.reshape(group_rows, lane_width), values_new], axis=1)
    capacity = max(2, (pages_per + req_count - 2) // (req_count - 1))
    page_ids = jnp.arange(pages_per, dtype=jnp.int32)
    earlier = page_ids[None, :] < page_ids[:, None]
    same_owner = page_owner[:, :, None] == page_owner[:, None, :]
    page_rank = jnp.sum((same_owner & earlier[None]).astype(jnp.int32), axis=2)
    owned_here = page_owner == req_index
    chosen = owned_here[:, None, :] & (
        page_rank[:, None, :] == jnp.arange(capacity, dtype=jnp.int32)[None, :, None]
    )
    send_slot = jnp.sum(jnp.where(chosen, page_slot[:, None, :], 0), axis=2)
    page_shape = page_store.shape[1:]
    outgoing_pages = jnp.take(page_store, send_slot.reshape(-1), axis=0, mode="clip").reshape(
        (req_count, capacity) + page_shape
    )
    arrived_pages = lax.all_to_all(outgoing_pages, "req", split_axis=0, concat_axis=0, tiled=True)
    own_owner = jnp.take(page_owner, req_index, axis=0)
    own_rank = jnp.take(page_rank, req_index, axis=0)
    context = jnp.take(
        arrived_pages.reshape((req_count * capacity,) + page_shape),
        own_owner * capacity + own_rank,
        axis=0,
        mode="clip",
    )
    context = context.reshape(context_len, 2, lane_heads, head_dim)
    score_scale = 1.0 / math.sqrt(head_dim)
    near_scores = (
        jnp.einsum("ihc,jhc->hij", query_rows, keys_new, preferred_element_type=jnp.float32)
        * score_scale
    )
    far_scores = (
        jnp.einsum("ihc,jhc->hij", query_rows, context[:, 0], preferred_element_type=jnp.float32)
        * score_scale
    )
    same_request = second[:, None] == second[None, :]
    near_weights = jnp.where(same_request[None], jnp.exp(near_scores), jnp.float32(0.0))
    far_weights = jnp.where((carried == 1)[None, :, None], jnp.exp(far_scores), jnp.float32(0.0))
    totals = jnp.sum(near_weights, axis=2, keepdims=True) + jnp.sum(
        far_weights, axis=2, keepdims=True
    )
    near_probs = (near_weights / totals).astype(jnp.bfloat16)
    far_probs = (far_weights / totals).astype(jnp.bfloat16)
    attended = jnp.einsum(
        "hij,jhc->ihc",
        near_probs,
        values_new.reshape(group_rows, lane_heads, head_dim),
        preferred_element_type=jnp.float32,
    )
    attended = attended + jnp.einsum(
        "hij,jhc->ihc", far_probs, context[:, 1], preferred_element_type=jnp.float32
    )
    attended = attended.astype(jnp.bfloat16).reshape(group_rows, lane_width)
    shard_rows = routes.shape[0]
    row_start = lane_index * shard_rows
    qkv_out = copy_columns(gathered, qkv_width, 4)
    qkv_out, attended = lax.optimization_barrier((qkv_out, attended))
    head_terms = jnp.dot(attended, server_out, preferred_element_type=jnp.float32)
    mixed_own = scatter_sum(head_terms, lax.axis_size("tp"))
    residual_own = lax.dynamic_slice_in_dim(tokens_f32, row_start, shard_rows, 0) + mixed_own
    moe_own = rms_scale(residual_own, moe_gain).astype(jnp.bfloat16)
    logits = jnp.dot(moe_own, router_weight, preferred_element_type=jnp.float32)
    exps = jnp.exp(logits)
    routed_exps = jnp.take_along_axis(exps, routes, axis=1)
    entry_gates = routed_exps / jnp.sum(routed_exps, axis=1, keepdims=True)
    top_count = routes.shape[1]
    slot_depth = 3 * shard_rows * top_count // (2 * expert_count)
    flat_routes = routes.reshape(-1)
    onehot = (flat_routes[:, None] == jnp.arange(expert_count, dtype=jnp.int32)[None, :]).astype(
        jnp.int32
    )
    entry_rank = jnp.sum((jnp.cumsum(onehot, axis=0) - onehot) * onehot, axis=1)
    entry_slot = (flat_routes * slot_depth + entry_rank).reshape(shard_rows, top_count)
    select_table = jnp.any(
        entry_slot[None, :, :]
        == jnp.arange(expert_count * slot_depth, dtype=jnp.int32)[:, None, None],
        axis=2,
    ).astype(jnp.bfloat16)
    outgoing_rows = jnp.dot(select_table, moe_own, preferred_element_type=jnp.float32).astype(
        jnp.bfloat16
    )
    send_rows = jnp.broadcast_to(
        outgoing_rows.reshape(expert_count, 1, slot_depth, model_width),
        (expert_count, 2, slot_depth, model_width),
    ).reshape(2 * expert_count, slot_depth, model_width)
    server_gate_up, send_rows = lax.optimization_barrier((server_gate_up, send_rows))
    arrived_rows = lax.all_to_all(send_rows, ("req", "tp"), split_axis=0, concat_axis=0, tiled=True)
    both = jnp.einsum("xkd,df->xkf", arrived_rows, server_gate_up[0], preferred_element_type=jnp.float32)
    act = (jax.nn.silu(both[..., :half_units]) * both[..., half_units:]).astype(jnp.bfloat16)
    expert_rows = jnp.einsum(
        "xkf,fd->xkd", act, down_weight[0], preferred_element_type=jnp.float32
    ).astype(jnp.bfloat16)
    returned = lax.all_to_all(expert_rows, ("req", "tp"), split_axis=0, concat_axis=0, tiled=True)
    slot_weights = jnp.sum(
        jnp.where(
            entry_slot[:, :, None] == jnp.arange(expert_count * slot_depth, dtype=jnp.int32)[None, None, :],
            entry_gates[:, :, None],
            jnp.float32(0.0),
        ),
        axis=1,
    ).reshape(shard_rows, expert_count, 1, slot_depth)
    slot_weights = jnp.broadcast_to(
        slot_weights, (shard_rows, expert_count, 2, slot_depth)
    ).reshape(shard_rows, 2 * expert_count, slot_depth)
    moe_out = jnp.einsum(
        "ixk,xkd->id",
        slot_weights,
        returned.astype(jnp.float32),
        precision=lax.Precision.HIGHEST,
        preferred_element_type=jnp.float32,
    )
    hidden_rows = (residual_own + moe_out).astype(jnp.bfloat16)
    gate_up_out = copy_rows(server_gate_up.reshape(server_gate_up.shape[1:]), 4).reshape(server_gate_up.shape)
    return (qkv_out, copy_rows(server_out, 1), gate_up_out, hidden_rows, new_cache)


def solution(mesh):
    in_specs = (
        P("req", None),
        P(),
        P(),
        P(),
        P(),
        P("req", "tp"),
        P("req", "tp"),
        P("req", "tp"),
        P("tp", "req"),
        P(None, ("req", "tp"), None),
        P(None, ("req", "tp"), None),
        P(("req", "tp"), None, None),
        P(),
        P("req", None, None, "tp"),
        P(),
        P(),
        P(),
        P(),
        P(("req", "tp"), None),
    )
    out_specs = (
        P(None, "tp"),
        P("tp", None),
        P(("req", "tp"), None, None),
        P(("req", "tp"), None),
        P("req", None, "tp"),
    )
    return jax.shard_map(body, mesh=mesh, in_specs=in_specs, out_specs=out_specs, check_vma=False)
```
